128 devices in a mesh: head: 8 (over y_lo, z), ctx: 16 (over x, y_hi, core).
Axes of the slice: x: 4, y: 4 (y_hi: 2, y_lo: 2; y = y_hi * 2 + y_lo), z: 4, core: 2. Of those that a mesh axis runs over, the one named last changes fastest.
Arguments:
- keys: bfloat16 [8192, 5120], P('ctx', 'head'), may hold values from -6 to 6
- queries: bfloat16 [8192, 5120], P('ctx', 'head'), may hold values from -6 to 6
- values: bfloat16 [8192, 5120], P('ctx', 'head'), may hold values from -6 to 6
- rates: float32 [8192, 16], P('ctx', 'head'), may hold values from 0.02 to 1
- gate_fast: float32 [16, 320, 640], P('head'), may hold values from -0.3125 to 0.3125
- up_fast: float32 [16, 320, 640], P('head'), may hold values from -0.3125 to 0.3125
- down_fast: float32 [16, 320, 640], P('head'), may hold values from -0.25 to 0.25
- out_weight: bfloat16 [5120, 5120], P('head'), may hold values from -0.078125 to 0.078125
Outputs:
- layer_out: bfloat16 [8192, 5120], P(('ctx', 'head'))
The draws below stay inside these ranges and needn't reach their ends.
All inputs are finite; a program needn't handle non-finite values.
Results may differ from the reference program's by a relative error of at most 0.011.
Values sent between devices are 32-bit elements; how exact they have to be, the bound alone decides.
No kernel may reach another device: no remote copies, remote signals or barrier semaphores. Data moves between devices by JAX's collectives and lax.ppermute only.
A program may use at most 128 MiB of HBM per device.

```python
import math
import jax
import jax.numpy as jnp
from jax import lax

D = 5120
DH = 320
DFF = 640
NS_STEPS = 5
HEADS = 16
TOKENS = 8192


def steps_of(rng, extent, split, low, largest):
    def one(dim, blocks):
        draws = jax.random.uniform(jax.random.fold_in(jax.random.fold_in(rng, 6), dim), (blocks,), jnp.float32, low / len(split), largest / len(split))
        return jnp.repeat(jnp.exp(draws), extent[dim] // blocks).reshape((-1,) + (1,) * (len(extent) - dim - 1))

    factor_of = one(*split[0])
    for cut in split[1:]:
        factor_of = factor_of * one(*cut)
    return factor_of


def centred(rng, dims, scale, limit, split=(), kind=jnp.bfloat16):
    gain = steps_of(rng, dims, split, -0.22, 0.18) if split else 1.0
    values = jax.random.normal(rng, dims, jnp.float32) * scale * gain
    return jnp.minimum(jnp.maximum(values, -limit), limit).astype(kind)


def setup_inputs(seed: int = 0) -> dict:
    splits = jax.random.split(jax.random.key(seed), 9)
    return {
        "keys": centred(splits[0], (TOKENS, D), 1.0, 6.0, ((0, 16), (1, 8))),
        "queries": centred(splits[1], (TOKENS, D), 1.0, 6.0, ((0, 16), (1, 8))),
        "values": centred(splits[2], (TOKENS, D), 1.0, 6.0, ((0, 16), (1, 8))),
        "rates": jnp.clip(jnp.exp(math.log(1.0) - 3.912023 * jax.random.uniform(splits[3], (TOKENS, HEADS), jnp.float32) ** steps_of(splits[3], (TOKENS, HEADS), ((0, 16), (1, 8)), -0.2, 0.2)), 0.02, 1.0),
        "gate_fast": centred(splits[4], (HEADS, DH, DFF), DH ** -0.5, 0.3125, ((0, 8),), jnp.float32),
        "up_fast": centred(splits[5], (HEADS, DH, DFF), DH ** -0.5, 0.3125, ((0, 8),), jnp.float32),
        "down_fast": centred(splits[6], (HEADS, DH, DFF), DFF ** -0.5, 0.25, ((0, 8),), jnp.float32),
        "out_weight": centred(splits[7], (D, D), D ** -0.5, 0.078125, ((0, 8),)),
    }


ns_a = 3.4445
ns_b = -4.775
ns_c = 2.0315
eps_value = 1e-06

def head_grads(args):
    key_head, value_head, rate_head, gate_b, up_b, down_b = args
    gate = jnp.dot(key_head, gate_b, preferred_element_type=jnp.float32)
    upper = jnp.dot(key_head, up_b, preferred_element_type=jnp.float32)
    sig = jax.nn.sigmoid(gate)
    act = gate * sig
    hidden = (act * upper).astype(jnp.bfloat16)
    dout = (-rate_head[:, None] * value_head.astype(jnp.float32)).astype(jnp.bfloat16)
    dhid = jnp.dot(dout, down_b, preferred_element_type=jnp.float32)
    dgate = (dhid * upper * sig * (1.0 + gate * (1.0 - sig))).astype(jnp.bfloat16)
    dup = (dhid * act).astype(jnp.bfloat16)
    grad_gate = jnp.dot(key_head.T, dgate, preferred_element_type=jnp.float32)
    grad_up = jnp.dot(key_head.T, dup, preferred_element_type=jnp.float32)
    grad_down = jnp.dot(dout.T, hidden, preferred_element_type=jnp.float32)
    return jnp.stack([grad_gate, grad_up, grad_down])

def head_query(args):
    query_head, new_gate, new_up, new_down = args
    gate = jnp.dot(query_head, new_gate, preferred_element_type=jnp.float32)
    upper = jnp.dot(query_head, new_up, preferred_element_type=jnp.float32)
    hidden = (gate * jax.nn.sigmoid(gate) * upper).astype(jnp.bfloat16)
    return jnp.dot(hidden, new_down.T, preferred_element_type=jnp.float32).astype(jnp.bfloat16)

def newton(grads):
    scale = lax.rsqrt(lax.optimization_barrier(jnp.sum(grads * grads, axis=(-2, -1), keepdims=True)) + eps_value)
    iterate = grads * scale
    for sweep_index in range(NS_STEPS):
        gram = jnp.einsum('...df,...ef->...de', iterate, iterate, precision=lax.Precision.HIGHEST)
        square = jnp.einsum('...de,...ef->...df', gram, gram, precision=lax.Precision.HIGHEST)
        mixer = ns_b * gram + ns_c * square
        iterate = ns_a * iterate + jnp.einsum('...de,...ef->...df', mixer, iterate, precision=lax.Precision.HIGHEST)
    return iterate

def reference(keys, queries, values, rates, gate_fast, up_fast, down_fast, out_weight):
    key_heads = keys.reshape(TOKENS, HEADS, DH).transpose(1, 0, 2)
    value_heads = values.reshape(TOKENS, HEADS, DH).transpose(1, 0, 2)
    query_heads = queries.reshape(TOKENS, HEADS, DH).transpose(1, 0, 2)
    fast = jnp.stack([gate_fast, up_fast, down_fast])
    fast_b = fast.astype(jnp.bfloat16)
    grads = lax.map(head_grads, (key_heads, value_heads, rates.T, fast_b[0], fast_b[1], fast_b[2]))
    grads = grads.transpose(1, 0, 2, 3)
    updated = (fast - newton(grads)).astype(jnp.bfloat16)
    outputs = lax.map(head_query, (query_heads, updated[0], updated[1], updated[2]))
    joined = outputs.transpose(1, 0, 2).reshape(TOKENS, D)
    return jnp.dot(joined, out_weight, preferred_element_type=jnp.float32).astype(jnp.bfloat16)
```

```python
import jax
import jax.numpy as jnp
from jax import lax
from jax.experimental import pallas as pl
from jax.experimental.pallas import tpu as pltpu
from jax.sharding import Mesh, PartitionSpec as P

NS_STEPS = 5
ns_a = 3.4445
ns_b = -4.775
ns_c = 2.0315
eps_value = 1e-06

AXES = ("yl", "z", "x", "yh", "core")
PLANE = ("x", "yh")
SHARDS = 8
F32 = jnp.float32
BF16 = jnp.bfloat16


def mm(a, b):
    return jnp.dot(a, b, preferred_element_type=F32)


def mm_nt(a, b):
    return lax.dot_general(a, b, (((1,), (1,)), ((), ())), preferred_element_type=F32)


def grads_kernel(head_ref, k_ref, v_ref, r_ref, g_ref, u_ref, d_ref, o_ref, k_s, v_s, hk_s, dg_s, du_s):
    head = head_ref[0]
    rows, width = k_s.shape
    for h in range(2):

        @pl.when(head == h)
        def _():
            k_s[...] = k_ref[:, h * width : (h + 1) * width]
            rate = r_ref[:, h : h + 1]
            v = v_ref[:, h * width : (h + 1) * width].astype(F32)
            v_s[...] = (-rate * v).astype(BF16)

    wg = g_ref[0].astype(BF16)
    wu = u_ref[0].astype(BF16)
    wd = d_ref[0].astype(BF16)
    step = 128
    for t in range(0, rows, step):
        at = slice(t, t + step)
        k = k_s[at, :]
        gate = mm(k, wg)
        upper = mm(k, wu)
        dhid = mm(v_s[at, :], wd)
        sig = jax.nn.sigmoid(gate)
        act = gate * sig
        hk_s[at, :] = (act * upper).astype(BF16)
        dg_s[at, :] = (dhid * upper * sig * (1.0 + gate * (1.0 - sig))).astype(BF16)
        du_s[at, :] = (dhid * act).astype(BF16)
    kt = k_s[...].T
    vt = v_s[...].T
    part = width // SHARDS
    for m, (left, right) in enumerate(((kt, dg_s), (kt, du_s), (vt, hk_s))):
        grad = mm(left, right[...])
        for j in range(SHARDS):
            o_ref[j, m] = grad[j * part : (j + 1) * part, :]


def head_grads(head, keys, values, rates, gate, up, down):
    rows = keys.shape[0]
    heads, width, hidden = gate.shape
    whole = lambda a: pl.BlockSpec(a.shape, lambda i, h: (0,) * a.ndim)
    one = pl.BlockSpec((1, width, hidden), lambda i, h: (h[0], 0, 0))
    shape = (SHARDS, 3, width // SHARDS, hidden)
    return pl.pallas_call(
        grads_kernel,
        out_shape=jax.ShapeDtypeStruct(shape, F32),
        grid_spec=pltpu.PrefetchScalarGridSpec(
            num_scalar_prefetch=1,
            grid=(1,),
            in_specs=[whole(keys), whole(values), whole(rates), one, one, one],
            out_specs=pl.BlockSpec(shape, lambda i, h: (0, 0, 0, 0)),
            scratch_shapes=[
                pltpu.VMEM((rows, width), BF16),
                pltpu.VMEM((rows, width), BF16),
                pltpu.VMEM((rows, hidden), BF16),
                pltpu.VMEM((rows, hidden), BF16),
                pltpu.VMEM((rows, hidden), BF16),
            ],
        ),
        compiler_params=pltpu.CompilerParams(vmem_limit_bytes=56 << 20),
        name="head_grads",
    )(head, keys, values, rates, gate, up, down)


def split(x):
    high = x.astype(BF16)
    return high, (x - high.astype(F32)).astype(BF16)


def newton_kernel(g_ref, o_ref):
    width = g_ref.shape[0] * g_ref.shape[2]
    hidden = g_ref.shape[3]
    for m in range(g_ref.shape[1]):
        grad = g_ref[:, m].reshape(width, hidden)
        total = jnp.sum(jnp.sum(grad * grad, axis=1, keepdims=True), axis=0, keepdims=True)
        x = grad * lax.rsqrt(total + eps_value)
        for _ in range(NS_STEPS):
            xh, xl = split(x)
            gram = mm_nt(jnp.concatenate([xh, xh, xl], axis=1), jnp.concatenate([xh, xl, xh], axis=1))
            ah, al = split(gram)
            square = mm(jnp.concatenate([ah, ah, al], axis=1), jnp.concatenate([ah, al, ah], axis=0))
            mh, ml = split(ns_b * gram + ns_c * square)
            x = ns_a * x + mm(jnp.concatenate([mh, mh, ml], axis=1), jnp.concatenate([xh, xl, xh], axis=0))
        o_ref[m] = x


def newton(grads):
    shape = (grads.shape[1], grads.shape[0] * grads.shape[2], grads.shape[3])
    return pl.pallas_call(
        newton_kernel,
        out_shape=jax.ShapeDtypeStruct(shape, F32),
        compiler_params=pltpu.CompilerParams(vmem_limit_bytes=56 << 20),
        name="newton",
    )(grads)


def query_kernel(head_ref, q_ref, x_ref, g_ref, u_ref, d_ref, o_ref, q_s):
    head = head_ref[0]
    rows, width = q_s.shape
    for h in range(2):

        @pl.when(head == h)
        def _():
            q_s[...] = q_ref[:, h * width : (h + 1) * width]

    vg = (g_ref[0] - x_ref[0]).astype(BF16)
    vu = (u_ref[0] - x_ref[1]).astype(BF16)
    vd = (d_ref[0] - x_ref[2]).astype(BF16)
    step = 128
    for t in range(0, rows, step):
        q = q_s[t : t + step, :]
        gate = mm(q, vg)
        hidden = (gate * jax.nn.sigmoid(gate) * mm(q, vu)).astype(BF16)
        o_ref[t : t + step, :] = mm_nt(hidden, vd).astype(BF16)


def head_query(head, queries, x, gate, up, down):
    rows = queries.shape[0]
    heads, width, hidden = gate.shape
    whole = lambda a: pl.BlockSpec(a.shape, lambda i, h: (0,) * a.ndim)
    one = pl.BlockSpec((1, width, hidden), lambda i, h: (h[0], 0, 0))
    return pl.pallas_call(
        query_kernel,
        out_shape=jax.ShapeDtypeStruct((rows, width), BF16),
        grid_spec=pltpu.PrefetchScalarGridSpec(
            num_scalar_prefetch=1,
            grid=(1,),
            in_specs=[whole(queries), whole(x), one, one, one],
            out_specs=pl.BlockSpec((rows, width), lambda i, h: (0, 0)),
            scratch_shapes=[pltpu.VMEM((rows, width), BF16)],
        ),
        compiler_params=pltpu.CompilerParams(vmem_limit_bytes=56 << 20),
        name="head_query",
    )(head, queries, x, gate, up, down)


def swap(a, axis):
    return lax.ppermute(a, axis, [(0, 1), (1, 0)])


def ring(a, shift):
    return lax.ppermute(a, "z", [(i, (i + shift) % 4) for i in range(4)])


def relative(a):
    yl, z = lax.axis_index("yl"), lax.axis_index("z")
    a = a.reshape((2, 4, a.shape[0] // 8) + a.shape[1:])
    a = lax.dynamic_slice_in_dim(jnp.concatenate([a, a], axis=1), z, 4, axis=1)
    return lax.dynamic_slice_in_dim(jnp.concatenate([a, a], axis=0), yl, 2, axis=0)


def plane_scatter(a):
    return jnp.sum(lax.all_to_all(a, PLANE, 0, 0, tiled=True), axis=0)


def plane_gather(a):
    same = jnp.broadcast_to(a[None], (SHARDS,) + a.shape)
    return lax.all_to_all(same, PLANE, 0, 0, tiled=True)


def project_scatter(rel, weight, cut):
    rows, depth = rel.shape[2:]
    left, right = weight[:, :cut], weight[:, cut:]
    part = lambda o, w: mm(o.reshape(-1, depth), w).reshape(o.shape[:-1] + (w.shape[1],))
    half = rows // 2

    b_far = part(rel[1], right)
    b_from_y = swap(b_far, "yl")
    a_two = part(rel[:, 2], left)
    a_up = ring(a_two[0], 1)
    a_down = ring(a_two[1], -1)
    a_one = part(rel[:, 1], left)
    a_three = part(rel[:, 3], left)
    b_near = part(rel[0], right)
    a_zero = part(rel[:, 0], left)

    a_one = jnp.stack([a_one[0] + a_up, a_one[1]])
    a_three = jnp.stack([a_three[0], a_three[1] + a_down])
    a_one = ring(a_one, 1)
    a_three = ring(a_three, -1)
    b = b_near + b_from_y
    b_up = ring(b[2, :half], 1)
    b_down = ring(b[2, half:], -1)
    a = a_zero + a_one + a_three
    a_from_y = swap(a[1], "yl")
    b_one = ring(jnp.concatenate([b[1, :half] + b_up, b[1, half:]]), 1)
    b_three = ring(jnp.concatenate([b[3, :half], b[3, half:] + b_down]), -1)
    return jnp.concatenate([a[0] + a_from_y, b[0] + b_one + b_three], axis=1)


def body(keys, queries, values, rates, gate, up, down, out_weight):
    core = lax.axis_index("core").astype(jnp.int32)
    mine, other = core[None], (1 - core)[None]
    weights = (gate, up, down)
    theirs = head_grads(other, keys, values, rates, *weights)
    received = swap(theirs, "core")
    ours = head_grads(mine, keys, values, rates, *weights)
    whole = plane_gather(plane_scatter(ours + received))
    x_mine = newton(whole)
    x_other = swap(x_mine, "core")
    q = relative(queries)
    q = q.reshape(-1, q.shape[-1])
    o_mine = head_query(mine, q, x_mine, *weights)
    o_other = head_query(other, q, x_other, *weights)
    joined = jnp.where(
        core == 0, jnp.concatenate([o_mine, o_other], axis=1), jnp.concatenate([o_other, o_mine], axis=1)
    )
    rel = joined.reshape(2, 4, -1, joined.shape[1])
    return project_scatter(rel, out_weight, 2816).astype(BF16)


def solution(mesh):
    fine = Mesh(mesh.devices.reshape(2, 4, 4, 2, 2), AXES)
    ctx, head = ("x", "yh", "core"), ("yl", "z")
    in_specs = (
        P(ctx, head),
        P(ctx, head),
        P(ctx, head),
        P(ctx, head),
        P(head, None, None),
        P(head, None, None),
        P(head, None, None),
        P(head, None),
    )
    out_specs = P(ctx + head, None)
    return jax.shard_map(body, mesh=fine, in_specs=in_specs, out_specs=out_specs, check_vma=False)
```

```python
import jax
import jax.numpy as jnp
from jax import lax
from jax.experimental import pallas as pl
from jax.experimental.pallas import tpu as pltpu
from jax.sharding import Mesh, PartitionSpec as P

NS_STEPS = 5
ns_a = 3.4445
ns_b = -4.775
ns_c = 2.0315
eps_value = 1e-06

AXES = ("yl", "z", "x", "yh", "core")
PLANE = ("x", "yh")
SHARDS = 8
TILE = 256
F32 = jnp.float32
BF16 = jnp.bfloat16


def mm(a, b):
    return jnp.dot(a, b, preferred_element_type=F32)


def mm_nt(a, b):
    return lax.dot_general(a, b, (((1,), (1,)), ((), ())), preferred_element_type=F32)


def grads_kernel(head_ref, k_ref, v_ref, r_ref, g_ref, u_ref, d_ref, o_ref, k_s, v_s, hk_s, dg_s, du_s):
    head = head_ref[0]
    rows, width = k_s.shape
    for h in range(2):

        @pl.when(head == h)
        def _():
            k_s[...] = k_ref[:, h * width : (h + 1) * width]
            rate = r_ref[h : h + 1, :].T
            v = v_ref[:, h * width : (h + 1) * width].astype(F32)
            v_s[...] = (-rate * v).astype(BF16)

    wg = g_ref[0].astype(BF16)
    wu = u_ref[0].astype(BF16)
    wd = d_ref[0].astype(BF16)
    step = 128
    for t in range(0, rows, step):
        at = slice(t, t + step)
        k = k_s[at, :]
        gate = mm(k, wg)
        upper = mm(k, wu)
        dhid = mm(v_s[at, :], wd)
        sig = jax.nn.sigmoid(gate)
        act = gate * sig
        hk_s[at, :] = (act * upper).astype(BF16)
        dg_s[at, :] = (dhid * upper * sig * (1.0 + gate * (1.0 - sig))).astype(BF16)
        du_s[at, :] = (dhid * act).astype(BF16)
    kt = k_s[...].T
    vt = v_s[...].T
    part = width // SHARDS
    for m, (left, right) in enumerate(((kt, dg_s), (kt, du_s), (vt, hk_s))):
        grad = mm(left, right[...])
        for j in range(SHARDS):
            o_ref[j, m] = grad[j * part : (j + 1) * part, :]


def head_grads(head, keys, values, rates, gate, up, down):
    rows = keys.shape[0]
    heads, width, hidden = gate.shape
    whole = lambda a: pl.BlockSpec(a.shape, lambda i, h: (0,) * a.ndim)
    one = pl.BlockSpec((1, width, hidden), lambda i, h: (h[0], 0, 0))
    shape = (SHARDS, 3, width // SHARDS, hidden)
    return pl.pallas_call(
        grads_kernel,
        out_shape=jax.ShapeDtypeStruct(shape, F32),
        grid_spec=pltpu.PrefetchScalarGridSpec(
            num_scalar_prefetch=1,
            grid=(1,),
            in_specs=[whole(keys), whole(values), whole(rates), one, one, one],
            out_specs=pl.BlockSpec(shape, lambda i, h: (0, 0, 0, 0)),
            scratch_shapes=[
                pltpu.VMEM((rows, width), BF16),
                pltpu.VMEM((rows, width), BF16),
                pltpu.VMEM((rows, hidden), BF16),
                pltpu.VMEM((rows, hidden), BF16),
                pltpu.VMEM((rows, hidden), BF16),
            ],
        ),
        compiler_params=pltpu.CompilerParams(vmem_limit_bytes=56 << 20),
        name="head_grads",
    )(head, keys, values, rates, gate, up, down)


def split(x):
    high = x.astype(BF16)
    return high, (x - high.astype(F32)).astype(BF16)


def packed(high, low):
    return jnp.concatenate([high, high, low], axis=1)


def mirrored(left, corner):
    at = left.shape[1]
    return jnp.concatenate([left, jnp.concatenate([left[at:].T, corner], axis=0)], axis=1)


def gram_of(xh, xl):
    a, b = packed(xh, xl), jnp.concatenate([xh, xl, xh], axis=1)
    return mirrored(mm_nt(a, b[:TILE]), mm_nt(a[TILE:], b[TILE:]))


def square_of(ah, al):
    a, b = packed(ah, al), jnp.concatenate([ah, al, ah], axis=0)
    return mirrored(mm(a, b[:, :TILE]), mm(a[TILE:], b[:, TILE:]))


def newton_kernel(g_ref, o_ref):
    matrices, width, hidden = o_ref.shape
    every = range(matrices)
    for m in every:
        grad = g_ref[:, m].reshape(width, hidden)
        total = jnp.sum(jnp.sum(grad * grad, axis=1, keepdims=True), axis=0, keepdims=True)
        o_ref[m] = grad * lax.rsqrt(total + eps_value)

    def sweep(_, carry):
        xs = [o_ref[m] for m in every]
        parts = [split(x) for x in xs]
        grams = [gram_of(*p) for p in parts]
        squares = [square_of(*split(g)) for g in grams]
        mixers = [split(ns_b * g + ns_c * q) for g, q in zip(grams, squares)]
        for m, x, (xh, xl), mixer in zip(every, xs, parts, mixers):
            o_ref[m] = ns_a * x + mm(packed(*mixer), jnp.concatenate([xh, xl, xh], axis=0))
        return carry

    lax.fori_loop(0, NS_STEPS, sweep, 0)


def newton(grads):
    shape = (grads.shape[1], grads.shape[0] * grads.shape[2], grads.shape[3])
    return pl.pallas_call(
        newton_kernel,
        out_shape=jax.ShapeDtypeStruct(shape, F32),
        compiler_params=pltpu.CompilerParams(vmem_limit_bytes=56 << 20),
        name="newton",
    )(grads)


def query_rows(at_ref, q_ref, q_s):
    rows, width = q_s.shape
    block = rows // 8
    for h in range(2):

        @pl.when(at_ref[0] == h)
        def _():
            for r in range(8):
                row = ((at_ref[1] + r // 4) % 2) * 4 + (at_ref[2] + r % 4) % 4
                source = pl.ds(pl.multiple_of(row * block, block), block)
                q_s[r * block : (r + 1) * block, :] = q_ref[source, h * width : (h + 1) * width]


def query_chunks(q_s, x_ref, g_ref, u_ref, d_ref):
    vg = (g_ref[0] - x_ref[0]).astype(BF16)
    vu = (u_ref[0] - x_ref[1]).astype(BF16)
    vd = (d_ref[0] - x_ref[2]).astype(BF16)
    step = 128
    for t in range(0, q_s.shape[0], step):
        q = q_s[t : t + step, :]
        gate = mm(q, vg)
        hidden = (gate * jax.nn.sigmoid(gate) * mm(q, vu)).astype(BF16)
        yield slice(t, t + step), mm_nt(hidden, vd).astype(BF16)


def first_kernel(at_ref, q_ref, x_ref, g_ref, u_ref, d_ref, o_ref, q_s):
    query_rows(at_ref, q_ref, q_s)
    for rows, o in query_chunks(q_s, x_ref, g_ref, u_ref, d_ref):
        o_ref[rows, :] = o


def second_kernel(at_ref, q_ref, x_ref, g_ref, u_ref, d_ref, p_ref, o_ref, q_s, o_s):
    width = q_s.shape[1]
    query_rows(at_ref, q_ref, q_s)
    for rows, o in query_chunks(q_s, x_ref, g_ref, u_ref, d_ref):
        o_s[rows, :] = o
    for h in range(2):

        @pl.when(at_ref[0] == h)
        def _():
            o_ref[:, h * width : (h + 1) * width] = o_s[...]
            o_ref[:, (1 - h) * width : (2 - h) * width] = p_ref[...]


def head_query(kernel, at, queries, x, gate, up, down, *first):
    rows = queries.shape[0]
    heads, width, hidden = gate.shape
    whole = lambda a: pl.BlockSpec(a.shape, lambda i, at: (0,) * a.ndim)
    one = pl.BlockSpec((1, width, hidden), lambda i, at: (at[0], 0, 0))
    scratch = [pltpu.VMEM((rows, width), BF16)] * (1 + len(first))
    columns = width * (1 + len(first))
    return pl.pallas_call(
        kernel,
        out_shape=jax.ShapeDtypeStruct((rows, columns), BF16),
        grid_spec=pltpu.PrefetchScalarGridSpec(
            num_scalar_prefetch=1,
            grid=(1,),
            in_specs=[whole(queries), whole(x), one, one, one] + [whole(a) for a in first],
            out_specs=pl.BlockSpec((rows, columns), lambda i, at: (0, 0)),
            scratch_shapes=scratch,
        ),
        compiler_params=pltpu.CompilerParams(vmem_limit_bytes=56 << 20),
        name="head_query",
    )(at, queries, x, gate, up, down, *first)


def swap(a, axis):
    return lax.ppermute(a, axis, [(0, 1), (1, 0)])


def ring(a, shift):
    return lax.ppermute(a, "z", [(i, (i + shift) % 4) for i in range(4)])


def plane_scatter(a):
    return jnp.sum(lax.all_to_all(a, PLANE, 0, 0, tiled=True), axis=0)


def plane_gather(a):
    same = jnp.broadcast_to(a[None], (SHARDS,) + a.shape)
    return lax.all_to_all(same, PLANE, 0, 0, tiled=True)


def project_scatter(rel, weight, cut):
    rows, depth = rel.shape[2:]
    left, right = weight[:, :cut], weight[:, cut:]
    part = lambda o, w: mm(o.reshape(-1, depth), w).reshape(o.shape[:-1] + (w.shape[1],))
    half = rows // 2

    b_far = part(rel[1], right)
    b_from_y = swap(b_far, "yl")
    a_two = part(rel[:, 2], left)
    a_up = ring(a_two[0], 1)
    a_down = ring(a_two[1], -1)
    a_one = part(rel[:, 1], left)
    a_three = part(rel[:, 3], left)
    b_near = part(rel[0], right)
    a_zero = part(rel[:, 0], left)

    a_one = jnp.stack([a_one[0] + a_up, a_one[1]])
    a_three = jnp.stack([a_three[0], a_three[1] + a_down])
    a_one = ring(a_one, 1)
    a_three = ring(a_three, -1)
    b = b_near + b_from_y
    b_up = ring(b[2, :half], 1)
    b_down = ring(b[2, half:], -1)
    a = a_zero + a_one + a_three
    a_from_y = swap(a[1], "yl")
    b_one = ring(jnp.concatenate([b[1, :half] + b_up, b[1, half:]]), 1)
    b_three = ring(jnp.concatenate([b[3, :half], b[3, half:] + b_down]), -1)
    return jnp.concatenate([a[0] + a_from_y, b[0] + b_one + b_three], axis=1)


def body(keys, queries, values, rates, gate, up, down, out_weight):
    core, yl, z = (lax.axis_index(name).astype(jnp.int32) for name in ("core", "yl", "z"))
    mine, other = jnp.stack([core, yl, z]), jnp.stack([1 - core, yl, z])
    weights = (gate, up, down)
    theirs = head_grads(other, keys, values, rates.T, *weights)
    received = swap(theirs, "core")
    ours = head_grads(mine, keys, values, rates.T, *weights)
    whole = plane_gather(plane_scatter(ours + received))
    x_mine = newton(whole)
    x_other = swap(x_mine, "core")
    o_mine = head_query(first_kernel, mine, queries, x_mine, *weights)
    joined = head_query(second_kernel, other, queries, x_other, *weights, o_mine)
    rel = joined.reshape(2, 4, -1, joined.shape[1])
    return project_scatter(rel, out_weight, 2816).astype(BF16)


def solution(mesh):
    fine = Mesh(mesh.devices.reshape(2, 4, 4, 2, 2), AXES)
    ctx, head = ("x", "yh", "core"), ("yl", "z")
    in_specs = (
        P(ctx, head),
        P(ctx, head),
        P(ctx, head),
        P(ctx, head),
        P(head, None, None),
        P(head, None, None),
        P(head, None, None),
        P(head, None),
    )
    out_specs = P(ctx + head, None)
    return jax.shard_map(body, mesh=fine, in_specs=in_specs, out_specs=out_specs, check_vma=False)
```

```python
import jax
import jax.numpy as jnp
from jax import lax
from jax.experimental import pallas as pl
from jax.experimental.pallas import tpu as pltpu
from jax.sharding import Mesh, PartitionSpec as P

NS_STEPS = 5
ns_a = 3.4445
ns_b = -4.775
ns_c = 2.0315
eps_value = 1e-06

AXES = ("yl", "z", "x", "yh", "core")
PLANE = ("x", "yh")
SHARDS = 8
TILE = 256
VMEM_LIMIT = 24 << 20
SHARES = (14, 10, 9, 7)
F32 = jnp.float32
BF16 = jnp.bfloat16


def mm(a, b):
    return jnp.dot(a, b, preferred_element_type=F32)


def mm_nt(a, b):
    return lax.dot_general(a, b, (((1,), (1,)), ((), ())), preferred_element_type=F32)


def grads_kernel(head_ref, k_ref, v_ref, r_ref, g_ref, u_ref, d_ref, o_ref, k_s, v_s, hk_s, dg_s, du_s):
    head = head_ref[0]
    rows, width = k_s.shape
    for h in range(2):

        @pl.when(head == h)
        def _():
            k_s[...] = k_ref[:, h * width : (h + 1) * width]
            rate = r_ref[h : h + 1, :].T
            v = v_ref[:, h * width : (h + 1) * width].astype(F32)
            v_s[...] = (-rate * v).astype(BF16)

    wg = g_ref[head].astype(BF16)
    wu = u_ref[head].astype(BF16)
    wd = d_ref[head].astype(BF16)
    step = 256
    for t in range(0, rows, step):
        at = slice(t, t + step)
        k = k_s[at, :]
        gate = mm(k, wg)
        upper = mm(k, wu)
        dhid = mm(v_s[at, :], wd)
        sig = jax.nn.sigmoid(gate)
        act = gate * sig
        hk_s[at, :] = (act * upper).astype(BF16)
        dg_s[at, :] = (dhid * upper * sig * (1.0 + gate * (1.0 - sig))).astype(BF16)
        du_s[at, :] = (dhid * act).astype(BF16)
    kt = k_s[...].T
    vt = v_s[...].T
    part = width // SHARDS
    for m, (left, right) in enumerate(((kt, dg_s), (kt, du_s), (vt, hk_s))):
        grad = mm(left, right[...])
        for j in range(SHARDS):
            o_ref[j, m] = grad[j * part : (j + 1) * part, :]


def call(kernel, name, outs, scratch, scalars, *operands):
    specs = [pl.BlockSpec(memory_space=pltpu.SMEM)] + [pl.BlockSpec(memory_space=pltpu.VMEM)] * len(operands)
    return pl.pallas_call(
        kernel,
        out_shape=outs,
        in_specs=specs,
        out_specs=jax.tree.map(lambda _: pl.BlockSpec(memory_space=pltpu.VMEM), outs),
        scratch_shapes=scratch,
        compiler_params=pltpu.CompilerParams(vmem_limit_bytes=VMEM_LIMIT),
        name=name,
    )(scalars, *operands)


def head_grads(at, keys, values, rates, gate, up, down):
    rows = keys.shape[0]
    heads, width, hidden = gate.shape
    scratch = [pltpu.VMEM((rows, width), BF16)] * 2 + [pltpu.VMEM((rows, hidden), BF16)] * 3
    shape = jax.ShapeDtypeStruct((SHARDS, 3, width // SHARDS, hidden), F32)
    return call(grads_kernel, "head_grads", shape, scratch, at, keys, values, rates, gate, up, down)


def split(x):
    high = x.astype(BF16)
    return high, (x - high.astype(F32)).astype(BF16)


def packed(high, low):
    return jnp.concatenate([high, high, low], axis=1)


def mirrored(left, corner):
    at = left.shape[1]
    return jnp.concatenate([left, jnp.concatenate([left[at:].T, corner], axis=0)], axis=1)


def gram_of(xh, xl):
    a, b = packed(xh, xl), jnp.concatenate([xh, xl, xh], axis=1)
    return mirrored(mm_nt(a, b[:TILE]), mm_nt(a[TILE:], b[TILE:]))


def square_of(ah, al):
    a, b = packed(ah, al), jnp.concatenate([ah, al, ah], axis=0)
    return mirrored(mm(a, b[:, :TILE]), mm(a[TILE:], b[:, TILE:]))


def newton_kernel(g_ref, o_ref):
    matrices, width, hidden = o_ref.shape
    every = range(matrices)
    for m in every:
        grad = g_ref[:, m].reshape(width, hidden)
        total = jnp.sum(jnp.sum(grad * grad, axis=1, keepdims=True), axis=0, keepdims=True)
        o_ref[m] = grad * lax.rsqrt(total + eps_value)

    def sweep(_, carry):
        xs = [o_ref[m] for m in every]
        parts = [split(x) for x in xs]
        grams = [gram_of(*p) for p in parts]
        squares = [square_of(*split(g)) for g in grams]
        mixers = [split(ns_b * g + ns_c * q) for g, q in zip(grams, squares)]
        for m, x, (xh, xl), mixer in zip(every, xs, parts, mixers):
            o_ref[m] = ns_a * x + mm(packed(*mixer), jnp.concatenate([xh, xl, xh], axis=0))
        return carry

    lax.fori_loop(0, NS_STEPS, sweep, 0)


def newton(grads):
    shape = (grads.shape[1], grads.shape[0] * grads.shape[2], grads.shape[3])
    return pl.pallas_call(
        newton_kernel,
        out_shape=jax.ShapeDtypeStruct(shape, F32),
        compiler_params=pltpu.CompilerParams(vmem_limit_bytes=VMEM_LIMIT),
        name="newton",
    )(grads)


def query_rows(at_ref, q_ref, q_s):
    rows, width = q_s.shape
    block = rows // 8
    for h in range(2):

        @pl.when(at_ref[0] == h)
        def _():
            for r in range(8):
                row = ((at_ref[1] + r // 4) % 2) * 4 + (at_ref[2] + r % 4) % 4
                source = pl.ds(pl.multiple_of(row * block, block), block)
                q_s[r * block : (r + 1) * block, :] = q_ref[source, h * width : (h + 1) * width]


def query_chunks(at_ref, q_s, x_ref, g_ref, u_ref, d_ref):
    head = at_ref[0]
    vg = (g_ref[head] - x_ref[0]).astype(BF16)
    vu = (u_ref[head] - x_ref[1]).astype(BF16)
    vd = (d_ref[head] - x_ref[2]).astype(BF16)
    step = 256
    for t in range(0, q_s.shape[0], step):
        q = q_s[t : t + step, :]
        gate = mm(q, vg)
        hidden = (gate * jax.nn.sigmoid(gate) * mm(q, vu)).astype(BF16)
        yield slice(t, t + step), mm_nt(hidden, vd).astype(BF16)


def first_kernel(at_ref, q_ref, x_ref, g_ref, u_ref, d_ref, o_ref, q_s):
    query_rows(at_ref, q_ref, q_s)
    for rows, o in query_chunks(at_ref, q_s, x_ref, g_ref, u_ref, d_ref):
        o_ref[rows, :] = o


def second_kernel(at_ref, q_ref, x_ref, g_ref, u_ref, d_ref, p_ref, y_ref, z_ref, q_s, o_s):
    width = q_s.shape[1]
    query_rows(at_ref, q_ref, q_s)
    for rows, o in query_chunks(at_ref, q_s, x_ref, g_ref, u_ref, d_ref):
        o_s[rows, :] = o
    block = q_s.shape[0] // 8
    for h in range(2):

        @pl.when(at_ref[0] == h)
        def _():
            for dy in range(2):
                for dz in range(4):
                    rows = pl.ds((dy * 4 + dz) * block, block)
                    to_y, to_z = pl.ds(dz * block, block), pl.ds(dy * block, block)
                    for at, ref in ((h, o_s), (1 - h, p_ref)):
                        columns = pl.ds(at * width, width)
                        y_ref[dy, to_y, columns] = ref[rows, :]
                        z_ref[dz, to_z, columns] = ref[rows, :]


def first_query(at, queries, x, *weights):
    rows, width = queries.shape[0], x.shape[1]
    scratch = [pltpu.VMEM((rows, width), BF16)]
    shape = jax.ShapeDtypeStruct((rows, width), BF16)
    return call(first_kernel, "first_query", shape, scratch, at, queries, x, *weights)


def second_query(at, queries, x, gate, up, down, first):
    rows, width = first.shape
    scratch = [pltpu.VMEM((rows, width), BF16)] * 2
    shapes = [jax.ShapeDtypeStruct((n, rows // n, 2 * width), BF16) for n in (2, 4)]
    return call(second_kernel, "second_query", shapes, scratch, at, queries, x, gate, up, down, first)


def swap(a, axis):
    return lax.ppermute(a, axis, [(0, 1), (1, 0)])


def ring(a, shift):
    return lax.ppermute(a, "z", [(i, (i + shift) % 4) for i in range(4)])


def plane_scatter(a):
    return jnp.sum(lax.all_to_all(a, PLANE, 0, 0, tiled=True), axis=0)


def plane_gather(a):
    same = jnp.broadcast_to(a[None], (SHARDS,) + a.shape)
    return lax.all_to_all(same, PLANE, 0, 0, tiled=True)


def along_z(parts, split_parts):
    two_up, two_down, join = split_parts(parts[2])
    up, down = ring(two_up, 1), ring(two_down, -1)
    one_up, one_down, _ = split_parts(parts[1])
    three_up, three_down, _ = split_parts(parts[3])
    one = ring(join(one_up + up, one_down), 1)
    three = ring(join(three_up, three_down + down), -1)
    return parts[0] + one + three


def z_first(by_z, weight):
    parts = [mm(o, weight) for o in by_z]
    half = by_z.shape[1] // 2
    split_parts = lambda a: (a[:half], a[half:], lambda u, d: jnp.concatenate([u, d], axis=0))
    a = along_z(parts, split_parts)
    return a[:half] + swap(a[half:], "yl")


def y_first(by_y, weight):
    far = swap(mm(by_y[1], weight), "yl")
    b = mm(by_y[0], weight) + far
    b = b.reshape(4, -1, b.shape[1])
    half = b.shape[1] // 2
    split_parts = lambda a: (a[:half], a[half:], lambda u, d: jnp.concatenate([u, d], axis=0))
    return along_z([b[d] for d in range(4)], split_parts)


def project_scatter(by_y, by_z, weight):
    cuts = [0]
    for share in SHARES:
        cuts.append(cuts[-1] + share * weight.shape[1] // sum(SHARES))
    pieces = [weight[:, i:j] for i, j in zip(cuts, cuts[1:])]
    right = [y_first(by_y, w) for w in pieces[2:]]
    left = [z_first(by_z, w) for w in pieces[:2]]
    return jnp.concatenate(left + right, axis=1)


def body(keys, queries, values, rates, gate, up, down, out_weight):
    core, yl, z = (lax.axis_index(name).astype(jnp.int32) for name in ("core", "yl", "z"))
    mine, other = jnp.stack([core, yl, z]), jnp.stack([1 - core, yl, z])
    weights = (gate, up, down)
    theirs = head_grads(other, keys, values, rates.T, *weights)
    received = swap(theirs, "core")
    ours = head_grads(mine, keys, values, rates.T, *weights)
    whole = plane_gather(plane_scatter(ours + received))
    x_mine = newton(whole)
    x_other = swap(x_mine, "core")
    o_mine = first_query(mine, queries, x_mine, *weights)
    by_y, by_z = second_query(other, queries, x_other, *weights, o_mine)
    return project_scatter(by_y, by_z, out_weight).astype(BF16)


def solution(mesh):
    fine = Mesh(mesh.devices.reshape(2, 4, 4, 2, 2), AXES)
    ctx, head = ("x", "yh", "core"), ("yl", "z")
    in_specs = (
        P(ctx, head),
        P(ctx, head),
        P(ctx, head),
        P(ctx, head),
        P(head, None, None),
        P(head, None, None),
        P(head, None, None),
        P(head, None),
    )
    out_specs = P(ctx + head, None)
    return jax.shard_map(body, mesh=fine, in_specs=in_specs, out_specs=out_specs, check_vma=False)
```

```python
import jax
import jax.numpy as jnp
from jax import lax
from jax.experimental import pallas as pl
from jax.experimental.pallas import tpu as pltpu
from jax.sharding import Mesh, PartitionSpec as P

NS_STEPS = 5
ns_a = 3.4445
ns_b = -4.775
ns_c = 2.0315
eps_value = 1e-06

AXES = ("yl", "z", "x", "yh", "core")
PLANE = ("x", "yh")
SHARDS = 8
TILE = 256
VMEM_LIMIT = 24 << 20
CUT = 3072
F32 = jnp.float32
BF16 = jnp.bfloat16


def mm(a, b):
    return jnp.dot(a, b, preferred_element_type=F32)


def mm_nt(a, b):
    return lax.dot_general(a, b, (((1,), (1,)), ((), ())), preferred_element_type=F32)


def call(kernel, name, outs, scratch, *operands):
    specs = [pl.BlockSpec(memory_space=pltpu.SMEM if a.dtype == jnp.int32 else pltpu.VMEM) for a in operands]
    return pl.pallas_call(
        kernel,
        out_shape=outs,
        in_specs=specs,
        out_specs=jax.tree.map(lambda _: pl.BlockSpec(memory_space=pltpu.VMEM), outs),
        scratch_shapes=scratch,
        compiler_params=pltpu.CompilerParams(vmem_limit_bytes=VMEM_LIMIT),
        name=name,
    )(*operands)


def out(shape, dtype):
    return jax.ShapeDtypeStruct(shape, dtype)


def sort_tokens_kernel(at_ref, k_ref, v_ref, r_ref, k_o, d_o, sent):
    width = k_o.shape[1]
    for h in range(2):

        @pl.when(at_ref[0] == h)
        def _():
            near, far = slice(h * width, (h + 1) * width), slice((1 - h) * width, (2 - h) * width)
            k_o[...] = k_ref[:, near]
            sent[:, :width] = k_ref[:, far].astype(F32)
            for head, columns in ((h, near), (1 - h, far)):
                rate = r_ref[head : head + 1, :].T
                d = (-rate * v_ref[:, columns].astype(F32)).astype(BF16)
                if head == h:
                    d_o[...] = d
                else:
                    sent[:, width:] = d.astype(F32)


def sort_tokens(at, keys, values, rates):
    shape = (keys.shape[0], keys.shape[1] // 2)
    shapes = [out(shape, BF16), out(shape, BF16), out(keys.shape, F32)]
    return call(sort_tokens_kernel, "sort_tokens", shapes, [], at, keys, values, rates)


def side_by_side(rows, r, block, width):
    top = (r * block) % (rows // 2)
    left = width * ((r * block) // (rows // 2))
    return slice(top, top + block), slice(left, left + width)


def sort_queries_kernel(at_ref, q_ref, q_o, sent):
    rows, width = q_o.shape
    block = rows // 8
    for h in range(2):

        @pl.when(at_ref[0] == h)
        def _():
            near, far = slice(h * width, (h + 1) * width), slice((1 - h) * width, (2 - h) * width)
            for r in range(8):
                row = ((at_ref[1] + r // 4) % 2) * 4 + (at_ref[2] + r % 4) % 4
                source = pl.ds(pl.multiple_of(row * block, block), block)
                q_o[r * block : (r + 1) * block, :] = q_ref[source, near]
                to_rows, to_columns = side_by_side(rows, r, block, width)
                sent[to_rows, to_columns] = q_ref[source, far].astype(F32)


def sort_queries(at, queries):
    rows, columns = queries.shape
    shapes = [out((rows, columns // 2), BF16), out((rows // 2, columns), F32)]
    return call(sort_queries_kernel, "sort_queries", shapes, [], at, queries)


def grads_of(k_ref, d_ref, w_ref, hk_s, dg_s, du_s):
    rows = k_ref.shape[0]
    wg, wu, wd = w_ref[0], w_ref[1], w_ref[2]
    step = 256
    for t in range(0, rows, step):
        at = slice(t, t + step)
        k = k_ref[at, :]
        gate = mm(k, wg)
        upper = mm(k, wu)
        dhid = mm(d_ref[at, :], wd)
        sig = jax.nn.sigmoid(gate)
        act = gate * sig
        hk_s[at, :] = (act * upper).astype(BF16)
        dg_s[at, :] = (dhid * upper * sig * (1.0 + gate * (1.0 - sig))).astype(BF16)
        du_s[at, :] = (dhid * act).astype(BF16)
    kt = k_ref[...].T
    dt = d_ref[...].T
    for m, (left, right) in enumerate(((kt, dg_s), (kt, du_s), (dt, hk_s))):
        yield m, mm(left, right[...])


def near_grads_kernel(at_ref, k_ref, d_ref, g_ref, u_ref, w_ref, o_ref, b_ref, f_s, hk_s, dg_s, du_s, sems):
    copies = [
        pltpu.make_async_copy(ref.at[at_ref[0]], f_s.at[m], sems.at[m]) for m, ref in enumerate((g_ref, u_ref, w_ref))
    ]
    for copy in copies:
        copy.start()
    for m, copy in enumerate(copies):
        copy.wait()
        b_ref[m] = f_s[m].astype(BF16)
    for m, grad in grads_of(k_ref, d_ref, b_ref, hk_s, dg_s, du_s):
        o_ref[m] = grad


def far_grads_kernel(came, b_ref, p_ref, o_ref, k_s, d_s, hk_s, dg_s, du_s):
    part = o_ref.shape[2]
    width = k_s.shape[1]
    k_s[...] = came[:, :width].astype(BF16)
    d_s[...] = came[:, width:].astype(BF16)
    for m, grad in grads_of(k_s, d_s, b_ref, hk_s, dg_s, du_s):
        for j in range(SHARDS):
            rows = slice(j * part, (j + 1) * part)
            o_ref[j, m] = grad[rows, :] + p_ref[m, rows, :]


def near_grads(at, k, d, gate, up, down):
    heads, width, hidden = gate.shape
    vmem, hbm = pl.BlockSpec(memory_space=pltpu.VMEM), pl.BlockSpec(memory_space=pltpu.HBM)
    shape = (3, width, hidden)
    return pl.pallas_call(
        near_grads_kernel,
        out_shape=[out(shape, F32), out(shape, BF16)],
        in_specs=[pl.BlockSpec(memory_space=pltpu.SMEM), vmem, vmem, hbm, hbm, hbm],
        out_specs=[vmem, vmem],
        scratch_shapes=[pltpu.VMEM(shape, F32)]
        + [pltpu.VMEM((k.shape[0], hidden), BF16)] * 3
        + [pltpu.SemaphoreType.DMA((3,))],
        compiler_params=pltpu.CompilerParams(vmem_limit_bytes=VMEM_LIMIT),
        name="near_grads",
    )(at, k, d, gate, up, down)


def far_grads(came, w, partial):
    heads, width, hidden = partial.shape
    rows = came.shape[0]
    scratch = [pltpu.VMEM((rows, width), BF16)] * 2 + [pltpu.VMEM((rows, hidden), BF16)] * 3
    shape = out((SHARDS, 3, width // SHARDS, hidden), F32)
    return call(far_grads_kernel, "far_grads", shape, scratch, came, w, partial)


def split(x):
    high = x.astype(BF16)
    return high, (x - high.astype(F32)).astype(BF16)


def packed(high, low):
    return jnp.concatenate([high, high, low], axis=1)


def mirrored(left, corner):
    at = left.shape[1]
    return jnp.concatenate([left, jnp.concatenate([left[at:].T, corner], axis=0)], axis=1)


def gram_of(xh, xl):
    a, b = packed(xh, xl), jnp.concatenate([xh, xl, xh], axis=1)
    return mirrored(mm_nt(a, b[:TILE]), mm_nt(a[TILE:], b[TILE:]))


def square_of(ah, al):
    a, b = packed(ah, al), jnp.concatenate([ah, al, ah], axis=0)
    return mirrored(mm(a, b[:, :TILE]), mm(a[TILE:], b[:, TILE:]))


def newton_kernel(at_ref, g_ref, wg_ref, wu_ref, wd_ref, v_ref, x_s, f_s, sems):
    copies = [
        pltpu.make_async_copy(ref.at[at_ref[0]], f_s.at[m], sems.at[m])
        for m, ref in enumerate((wg_ref, wu_ref, wd_ref))
    ]
    for copy in copies:
        copy.start()
    matrices, width, hidden = x_s.shape
    every = range(matrices)
    for m in every:
        grad = g_ref[:, m].reshape(width, hidden)
        total = jnp.sum(jnp.sum(grad * grad, axis=1, keepdims=True), axis=0, keepdims=True)
        x_s[m] = grad * lax.rsqrt(total + eps_value)

    def sweep(_, carry):
        xs = [x_s[m] for m in every]
        parts = [split(x) for x in xs]
        grams = [gram_of(*p) for p in parts]
        squares = [square_of(*split(g)) for g in grams]
        mixers = [split(ns_b * g + ns_c * q) for g, q in zip(grams, squares)]
        for m, x, (xh, xl), mixer in zip(every, xs, parts, mixers):
            x_s[m] = ns_a * x + mm(packed(*mixer), jnp.concatenate([xh, xl, xh], axis=0))
        return carry

    lax.fori_loop(0, NS_STEPS, sweep, 0)
    for m, copy in enumerate(copies):
        copy.wait()
        v_ref[m] = (f_s[m] - x_s[m]).astype(BF16)


def newton(at, grads, gate, up, down):
    shape = (grads.shape[1], grads.shape[0] * grads.shape[2], grads.shape[3])
    vmem, hbm = pl.BlockSpec(memory_space=pltpu.VMEM), pl.BlockSpec(memory_space=pltpu.HBM)
    return pl.pallas_call(
        newton_kernel,
        out_shape=out(shape, BF16),
        in_specs=[pl.BlockSpec(memory_space=pltpu.SMEM), vmem, hbm, hbm, hbm],
        out_specs=vmem,
        scratch_shapes=[pltpu.VMEM(shape, F32)] * 2 + [pltpu.SemaphoreType.DMA((3,))],
        compiler_params=pltpu.CompilerParams(vmem_limit_bytes=VMEM_LIMIT),
        name="newton",
    )(at, grads, gate, up, down)


def query_rows(q, v_ref):
    gate = mm(q, v_ref[0])
    hidden = (gate * jax.nn.sigmoid(gate) * mm(q, v_ref[1])).astype(BF16)
    return mm_nt(hidden, v_ref[2]).astype(BF16)


def far_query_kernel(came, v_ref, o_ref):
    width = came.shape[1] // 2
    for left in (0, width):
        columns = slice(left, left + width)
        o_ref[:, columns] = query_rows(came[:, columns].astype(BF16), v_ref).astype(F32)


def near_query_kernel(q_ref, v_ref, o_ref):
    half = q_ref.shape[0] // 2
    for top in (0, half):
        rows = slice(top, top + half)
        o_ref[rows, :] = query_rows(q_ref[rows, :], v_ref)


def join_kernel(at_ref, o_ref, came, y_ref, z_ref):
    rows, width = o_ref.shape
    block = rows // 8
    for h in range(2):

        @pl.when(at_ref[0] == h)
        def _():
            near, far = slice(h * width, (h + 1) * width), slice((1 - h) * width, (2 - h) * width)
            for dy in range(2):
                for dz in range(4):
                    r = dy * 4 + dz
                    to_y, to_z = pl.ds(dz * block, block), pl.ds(dy * block, block)
                    mine = o_ref[r * block : (r + 1) * block, :]
                    other = came[side_by_side(rows, r, block, width)].astype(BF16)
                    for columns, piece in ((near, mine), (far, other)):
                        y_ref[dy, to_y, columns] = piece
                        z_ref[dz, to_z, columns] = piece


def join(at, mine, came):
    rows, width = mine.shape
    shapes = [out((n, rows // n, 2 * width), BF16) for n in (2, 4)]
    return call(join_kernel, "join", shapes, [], at, mine, came)


def swap(a, axis):
    return lax.ppermute(a, axis, [(0, 1), (1, 0)])


def ring(a, shift):
    return lax.ppermute(a, "z", [(i, (i + shift) % 4) for i in range(4)])


def plane_scatter(a):
    return jnp.sum(lax.all_to_all(a, PLANE, 0, 0, tiled=True), axis=0)


def plane_gather(a):
    same = jnp.broadcast_to(a[None], (SHARDS,) + a.shape)
    return lax.all_to_all(same, PLANE, 0, 0, tiled=True)


def after(a, *others):
    return lax.optimization_barrier((a, others))[0]


def halves(a):
    half = a.shape[0] // 2
    return a[:half], a[half:]


def pass_two(a):
    up, down = halves(a)
    return ring(up, 1), ring(down, -1)


def pass_one(one, three, came):
    up, down = came
    one = jnp.concatenate([one[: up.shape[0]] + up, one[up.shape[0] :]], axis=0)
    three = jnp.concatenate([three[: up.shape[0]], three[up.shape[0] :] + down], axis=0)
    return (ring(one, 1), ring(three, -1)), (one, three)


def project_scatter(by_y, by_z, weight):
    wa, wb = weight[:, :CUT], weight[:, CUT:]
    b_far = mm(by_y[1], wb)
    b_came = swap(b_far, "yl")
    by_z = after(by_z, b_far)
    up, down = halves(by_z[2])
    a_came = ring(mm(up, wa), 1), ring(mm(down, wa), -1)
    a_came, a_sent = pass_one(mm(by_z[1], wa), mm(by_z[3], wa), a_came)
    b = mm(by_y[0], wb) + after(b_came, a_sent)
    b = b.reshape(4, -1, b.shape[1])
    b_came = pass_two(b[2])
    a = mm(by_z[0], wa) + sum(a_came)
    a, a_far = halves(a)
    a_came = swap(a_far, "yl")
    b_came, _ = pass_one(b[1], b[3], b_came)
    return jnp.concatenate([a + a_came, b[0] + sum(b_came)], axis=1)


def body(keys, queries, values, rates, gate, up, down, out_weight):
    at = jnp.stack([lax.axis_index(name).astype(jnp.int32) for name in ("core", "yl", "z")])
    weights = tuple(pltpu.with_memory_space_constraint(w, pltpu.HBM) for w in (gate, up, down))
    k, d, sent = sort_tokens(at, keys, values, rates.T)
    came = swap(sent, "core")
    partial, rounded = near_grads(at, k, d, *weights)
    q, q_sent = sort_queries(at, after(queries, partial))
    whole = plane_gather(plane_scatter(far_grads(came, rounded, partial)))
    q_came = swap(q_sent, "core")
    v = newton(at, whole, *weights)
    o_came = swap(call(far_query_kernel, "far_query", out(q_sent.shape, F32), [], q_came, v), "core")
    o = call(near_query_kernel, "near_query", out(q.shape, BF16), [], q, v)
    by_y, by_z = join(at, o, o_came)
    return project_scatter(by_y, by_z, out_weight).astype(BF16)


def solution(mesh):
    fine = Mesh(mesh.devices.reshape(2, 4, 4, 2, 2), AXES)
    ctx, head = ("x", "yh", "core"), ("yl", "z")
    in_specs = (
        P(ctx, head),
        P(ctx, head),
        P(ctx, head),
        P(ctx, head),
        P(head, None, None),
        P(head, None, None),
        P(head, None, None),
        P(head, None),
    )
    out_specs = P(ctx + head, None)
    return jax.shard_map(body, mesh=fine, in_specs=in_specs, out_specs=out_specs, check_vma=False)
```

```python
import functools

import jax
import jax.numpy as jnp
from jax import lax
from jax.experimental import pallas as pl
from jax.experimental.pallas import tpu as pltpu
from jax.sharding import Mesh, PartitionSpec as P

NS_STEPS = 5
ns_a = 3.4445
ns_b = -4.775
ns_c = 2.0315
eps_value = 1e-06

AXES = ("yl", "z", "x", "yh", "core")
PLANE = ("x", "yh")
SHARDS = 8
TILE = 256
VMEM_LIMIT = 16 << 20
CUTS = (2048, 3968)
F32 = jnp.float32
BF16 = jnp.bfloat16


def mm(a, b):
    return jnp.dot(a, b, preferred_element_type=F32)


def mm_nt(a, b):
    return lax.dot_general(a, b, (((1,), (1,)), ((), ())), preferred_element_type=F32)


def call(kernel, name, outs, scratch, *operands):
    specs = [pl.BlockSpec(memory_space=pltpu.SMEM if a.dtype == jnp.int32 else pltpu.VMEM) for a in operands]
    return pl.pallas_call(
        kernel,
        out_shape=outs,
        in_specs=specs,
        out_specs=jax.tree.map(lambda _: pl.BlockSpec(memory_space=pltpu.VMEM), outs),
        scratch_shapes=scratch,
        compiler_params=pltpu.CompilerParams(vmem_limit_bytes=VMEM_LIMIT),
        name=name,
    )(*operands)


def out(shape, dtype):
    return jax.ShapeDtypeStruct(shape, dtype)


def sort_tokens_kernel(at_ref, k_ref, v_ref, r_ref, k_o, d_o, sent):
    width = k_o.shape[1]
    for h in range(2):

        @pl.when(at_ref[0] == h)
        def _():
            near, far = slice(h * width, (h + 1) * width), slice((1 - h) * width, (2 - h) * width)
            k_o[...] = k_ref[:, near]
            sent[:, :width] = k_ref[:, far].astype(F32)
            for head, columns in ((h, near), (1 - h, far)):
                rate = r_ref[head : head + 1, :].T
                d = (-rate * v_ref[:, columns].astype(F32)).astype(BF16)
                if head == h:
                    d_o[...] = d
                else:
                    sent[:, width:] = d.astype(F32)


def sort_tokens(at, keys, values, rates):
    shape = (keys.shape[0], keys.shape[1] // 2)
    shapes = [out(shape, BF16), out(shape, BF16), out(keys.shape, F32)]
    return call(sort_tokens_kernel, "sort_tokens", shapes, [], at, keys, values, rates)


def side_by_side(rows, r, block, width):
    top = (r * block) % (rows // 2)
    left = width * ((r * block) // (rows // 2))
    return slice(top, top + block), slice(left, left + width)


def sort_queries_kernel(at_ref, q_ref, q_o, sent):
    rows, width = q_o.shape
    block = rows // 8
    for h in range(2):

        @pl.when(at_ref[0] == h)
        def _():
            near, far = slice(h * width, (h + 1) * width), slice((1 - h) * width, (2 - h) * width)
            for r in range(8):
                row = ((at_ref[1] + r // 4) % 2) * 4 + (at_ref[2] + r % 4) % 4
                source = pl.ds(pl.multiple_of(row * block, block), block)
                q_o[r * block : (r + 1) * block, :] = q_ref[source, near]
                to_rows, to_columns = side_by_side(rows, r, block, width)
                sent[to_rows, to_columns] = q_ref[source, far].astype(F32)


def sort_queries(at, queries):
    rows, columns = queries.shape
    shapes = [out((rows, columns // 2), BF16), out((rows // 2, columns), F32)]
    return call(sort_queries_kernel, "sort_queries", shapes, [], at, queries)


def grads_of(k_ref, d_ref, w_ref, hk_s, dg_s, du_s):
    rows = k_ref.shape[0]
    wg, wu, wd = w_ref[0], w_ref[1], w_ref[2]
    step = 256
    for t in range(0, rows, step):
        at = slice(t, t + step)
        k = k_ref[at, :]
        gate = mm(k, wg)
        upper = mm(k, wu)
        dhid = mm(d_ref[at, :], wd)
        sig = jax.nn.sigmoid(gate)
        act = gate * sig
        hk_s[at, :] = (act * upper).astype(BF16)
        dg_s[at, :] = (dhid * upper * sig * (1.0 + gate * (1.0 - sig))).astype(BF16)
        du_s[at, :] = (dhid * act).astype(BF16)
    kt = k_ref[...].T
    dt = d_ref[...].T
    for m, (left, right) in enumerate(((kt, dg_s), (kt, du_s), (dt, hk_s))):
        yield m, mm(left, right[...])


def near_grads_kernel(at_ref, k_ref, d_ref, g_ref, u_ref, w_ref, o_ref, b_ref, f_s, hk_s, dg_s, du_s, sems):
    copies = [
        pltpu.make_async_copy(ref.at[at_ref[0]], f_s.at[m], sems.at[m]) for m, ref in enumerate((g_ref, u_ref, w_ref))
    ]
    for copy in copies:
        copy.start()
    for m, copy in enumerate(copies):
        copy.wait()
        b_ref[m] = f_s[m].astype(BF16)
    for m, grad in grads_of(k_ref, d_ref, b_ref, hk_s, dg_s, du_s):
        o_ref[m] = grad


def far_grads_kernel(came, b_ref, p_ref, o_ref, k_s, d_s, hk_s, dg_s, du_s):
    part = o_ref.shape[2]
    width = k_s.shape[1]
    k_s[...] = came[:, :width].astype(BF16)
    d_s[...] = came[:, width:].astype(BF16)
    for m, grad in grads_of(k_s, d_s, b_ref, hk_s, dg_s, du_s):
        for j in range(SHARDS):
            rows = slice(j * part, (j + 1) * part)
            o_ref[j, m] = grad[rows, :] + p_ref[m, rows, :]


def near_grads(at, k, d, gate, up, down):
    heads, width, hidden = gate.shape
    vmem, hbm = pl.BlockSpec(memory_space=pltpu.VMEM), pl.BlockSpec(memory_space=pltpu.HBM)
    shape = (3, width, hidden)
    return pl.pallas_call(
        near_grads_kernel,
        out_shape=[out(shape, F32), out(shape, BF16)],
        in_specs=[pl.BlockSpec(memory_space=pltpu.SMEM), vmem, vmem, hbm, hbm, hbm],
        out_specs=[vmem, vmem],
        scratch_shapes=[pltpu.VMEM(shape, F32)]
        + [pltpu.VMEM((k.shape[0], hidden), BF16)] * 3
        + [pltpu.SemaphoreType.DMA((3,))],
        compiler_params=pltpu.CompilerParams(vmem_limit_bytes=VMEM_LIMIT),
        name="near_grads",
    )(at, k, d, gate, up, down)


def far_grads(came, w, partial):
    heads, width, hidden = partial.shape
    rows = came.shape[0]
    scratch = [pltpu.VMEM((rows, width), BF16)] * 2 + [pltpu.VMEM((rows, hidden), BF16)] * 3
    shape = out((SHARDS, 3, width // SHARDS, hidden), F32)
    return call(far_grads_kernel, "far_grads", shape, scratch, came, w, partial)


def split(x):
    high = x.astype(BF16)
    return high, (x - high.astype(F32)).astype(BF16)


def packed(high, low):
    return jnp.concatenate([high, high, low], axis=1)


def mirrored(left, corner):
    at = left.shape[1]
    return jnp.concatenate([left, jnp.concatenate([left[at:].T, corner], axis=0)], axis=1)


def gram_of(xh, xl):
    a, b = packed(xh, xl), jnp.concatenate([xh, xl, xh], axis=1)
    return mirrored(mm_nt(a, b[:TILE]), mm_nt(a[TILE:], b[TILE:]))


def square_of(ah, al):
    a, b = packed(ah, al), jnp.concatenate([ah, al, ah], axis=0)
    return mirrored(mm(a, b[:, :TILE]), mm(a[TILE:], b[:, TILE:]))


def newton_kernel(at_ref, g_ref, wg_ref, wu_ref, wd_ref, v_ref, x_s, f_s, sems):
    copies = [
        pltpu.make_async_copy(ref.at[at_ref[0]], f_s.at[m], sems.at[m])
        for m, ref in enumerate((wg_ref, wu_ref, wd_ref))
    ]
    for copy in copies:
        copy.start()
    matrices, width, hidden = x_s.shape
    every = range(matrices)
    for m in every:
        grad = g_ref[:, m].reshape(width, hidden)
        total = jnp.sum(jnp.sum(grad * grad, axis=1, keepdims=True), axis=0, keepdims=True)
        x_s[m] = grad * lax.rsqrt(total + eps_value)

    def sweep(_, carry):
        xs = [x_s[m] for m in every]
        parts = [split(x) for x in xs]
        grams = [gram_of(*p) for p in parts]
        squares = [square_of(*split(g)) for g in grams]
        mixers = [split(ns_b * g + ns_c * q) for g, q in zip(grams, squares)]
        for m, x, (xh, xl), mixer in zip(every, xs, parts, mixers):
            x_s[m] = ns_a * x + mm(packed(*mixer), jnp.concatenate([xh, xl, xh], axis=0))
        return carry

    lax.fori_loop(0, NS_STEPS, sweep, 0)
    for m, copy in enumerate(copies):
        copy.wait()
        v_ref[m] = (f_s[m] - x_s[m]).astype(BF16)


def newton(at, grads, gate, up, down):
    shape = (grads.shape[1], grads.shape[0] * grads.shape[2], grads.shape[3])
    vmem, hbm = pl.BlockSpec(memory_space=pltpu.VMEM), pl.BlockSpec(memory_space=pltpu.HBM)
    return pl.pallas_call(
        newton_kernel,
        out_shape=out(shape, BF16),
        in_specs=[pl.BlockSpec(memory_space=pltpu.SMEM), vmem, hbm, hbm, hbm],
        out_specs=vmem,
        scratch_shapes=[pltpu.VMEM(shape, F32)] * 2 + [pltpu.SemaphoreType.DMA((3,))],
        compiler_params=pltpu.CompilerParams(vmem_limit_bytes=VMEM_LIMIT),
        name="newton",
    )(at, grads, gate, up, down)


def query_rows(q, v_ref):
    gate = mm(q, v_ref[0])
    hidden = (gate * jax.nn.sigmoid(gate) * mm(q, v_ref[1])).astype(BF16)
    return mm_nt(hidden, v_ref[2]).astype(BF16)


def far_query_kernel(came, v_ref, o_ref):
    width = came.shape[1] // 2
    for left in (0, width):
        columns = slice(left, left + width)
        o_ref[:, columns] = query_rows(came[:, columns].astype(BF16), v_ref).astype(F32)


def near_query_kernel(q_ref, v_ref, o_ref):
    half = q_ref.shape[0] // 2
    for top in (0, half):
        rows = slice(top, top + half)
        o_ref[rows, :] = query_rows(q_ref[rows, :], v_ref)


def join_kernel(at_ref, o_ref, came, y_ref, z_ref, *sent):
    rows, width = o_ref.shape
    block = rows // 8
    for dy in range(2):
        for dz in range(4):
            r = dy * 4 + dz
            to_y, to_z = pl.ds(dz * block, block), pl.ds(dy * block, block)
            mine = o_ref[r * block : (r + 1) * block, :]
            other = came[side_by_side(rows, r, block, width)]
            if dz > 0:
                sent[dz - 1][to_z, :width] = mine.astype(F32)
                sent[dz - 1][to_z, width:] = other
            for h in range(2):

                @pl.when(at_ref[0] == h)
                def _():
                    near, far = slice(h * width, (h + 1) * width), slice((1 - h) * width, (2 - h) * width)
                    for columns, piece in ((near, mine), (far, other.astype(BF16))):
                        y_ref[dy, to_y, columns] = piece
                        z_ref[dz, to_z, columns] = piece


def join(at, mine, came):
    rows, width = mine.shape
    shapes = [out((n, rows // n, 2 * width), BF16) for n in (2, 4)] + [out((rows // 4, 2 * width), F32)] * 3
    return call(join_kernel, "join", shapes, [], at, mine, came)


def gathered_kernel(counts, o_ref, w_ref, *refs):
    lefts, pieces, (near_ref, far_ref) = refs[:3], list(refs[3:-2]), refs[-2:]
    total = mm(o_ref[0], w_ref[...])
    for left, count in zip(lefts, counts):
        right = jnp.concatenate([pieces.pop(0)[...].astype(BF16) for _ in range(count)], axis=0)
        total = total + mm(left[...].astype(BF16), right)
    half = near_ref.shape[0]
    near_ref[...] = total[:half]
    far_ref[...] = total[half:]


def gathered_product(by_z, weight, lefts, sources):
    rows, depth = by_z.shape[1:]
    pieces = [piece for source in sources for piece in source]
    columns, step = pieces[0].shape[1], 512
    whole = pl.BlockSpec((rows, depth), lambda n: (0, 0))
    specs = [pl.BlockSpec((1, rows, depth), lambda n: (0, 0, 0)), pl.BlockSpec((depth, step), lambda n: (0, n))]
    specs += [whole] * len(lefts) + [pl.BlockSpec((a.shape[0], step), lambda n: (0, n)) for a in pieces]
    return pl.pallas_call(
        functools.partial(gathered_kernel, [len(source) for source in sources]),
        out_shape=[out((rows // 2, columns), F32)] * 2,
        grid=(columns // step,),
        in_specs=specs,
        out_specs=[pl.BlockSpec((rows // 2, step), lambda n: (0, n))] * 2,
        compiler_params=pltpu.CompilerParams(vmem_limit_bytes=VMEM_LIMIT),
        name="gathered_product",
    )(by_z, weight, *lefts, *pieces)


def swap(a, axis):
    return lax.ppermute(a, axis, [(0, 1), (1, 0)])


def ring(a, shift):
    return lax.ppermute(a, "z", [(i, (i + shift) % 4) for i in range(4)])


def plane_scatter(a):
    return jnp.sum(lax.all_to_all(a, PLANE, 0, 0, tiled=True), axis=0)


def plane_gather(a):
    same = jnp.broadcast_to(a[None], (SHARDS,) + a.shape)
    return lax.all_to_all(same, PLANE, 0, 0, tiled=True)


def after(a, *others):
    return lax.optimization_barrier((a, others))[0]


def halves(a):
    half = a.shape[0] // 2
    return a[:half], a[half:]


def pass_two(a):
    up, down = halves(a)
    return ring(up, 1), ring(down, -1)


def pass_one(one, three, came):
    up, down = came
    one = jnp.concatenate([one[: up.shape[0]] + up, one[up.shape[0] :]], axis=0)
    three = jnp.concatenate([three[: up.shape[0]], three[up.shape[0] :] + down], axis=0)
    return (ring(one, 1), ring(three, -1)), (one, three)


def own_part(weight):
    depth = weight.shape[0]
    half = lax.dynamic_slice_in_dim(weight[:, : CUTS[0]], lax.axis_index("core") * (depth // 2), depth // 2)
    return half.astype(F32)


def swapped(parts):
    return [swap(part, "core") for part in parts]


def project_scatter(by_y, by_z, sent, weight, sources):
    wa, wb = weight[:, CUTS[0] : CUTS[1]], weight[:, CUTS[1] :]
    b_far = mm(by_y[1], wb)
    b_came = swap(b_far, "yl")
    sent = after(sent, b_far)
    lefts = [ring(o, d) for o, d in zip(sent, (1, 2, -1))]
    by_z = after(by_z, b_far)
    a_came = pass_two(mm(by_z[2], wa))
    a_came, a_sent = pass_one(mm(by_z[1], wa), mm(by_z[3], wa), a_came)
    b = mm(by_y[0], wb) + after(b_came, a_sent)
    b = b.reshape(4, -1, b.shape[1])
    b_came = pass_two(b[2])
    c, c_far = gathered_product(by_z, weight, after(lefts, b), sources)
    c_came = swap(c_far, "yl")
    b_came, b_sent = pass_one(b[1], b[3], after(b_came, c_far))
    a = mm(by_z[0], wa) + sum(after(a_came, b_sent))
    a, a_far = halves(a)
    a_came = swap(a_far, "yl")
    return jnp.concatenate([c + c_came, a + a_came, b[0] + sum(b_came)], axis=1)


def body(keys, queries, values, rates, gate, up, down, out_weight):
    at = jnp.stack([lax.axis_index(name).astype(jnp.int32) for name in ("core", "yl", "z")])
    weights = tuple(pltpu.with_memory_space_constraint(w, pltpu.HBM) for w in (gate, up, down))
    k, d, sent = sort_tokens(at, keys, values, rates.T)
    came = swap(sent, "core")
    part = own_part(after(out_weight, sent))
    rows = part.shape[0] // 4
    cut = lambda i, j: part[i * rows : j * rows]
    first = [ring(cut(0, 2), 1), ring(cut(2, 4), -1), ring(cut(2, 3), 1), ring(cut(1, 2), -1)]
    partial, rounded = near_grads(at, k, d, *weights)
    total = plane_scatter(far_grads(came, rounded, partial))
    total, first = lax.optimization_barrier((total, first))
    ends = after((cut(3, 4), cut(0, 1)), total)
    second = [ring(first[0], 1), ring(first[1], -1), ring(ends[0], 1), ring(ends[1], -1)]
    first_core = swapped(first)
    q, q_sent = sort_queries(at, after(queries, total))
    whole = plane_gather(total)
    whole, second, first_core = lax.optimization_barrier((whole, second, first_core))
    second_core = swapped(second)
    pieces = []
    for came_first, came_second in ((first, second), (first_core, second_core)):
        below = [came_first[0], came_first[2], came_second[2]]
        above = [came_second[3], came_first[3], came_first[1]]
        pieces.append((below, came_second[:2], above))
    sources = [mine + others for mine, others in zip(*pieces)]
    q_came = swap(after(q_sent, whole), "core")
    v = newton(at, whole, *weights)
    o_came = swap(call(far_query_kernel, "far_query", out(q_sent.shape, F32), [], q_came, v), "core")
    o = call(near_query_kernel, "near_query", out(q.shape, BF16), [], q, v)
    by_y, by_z, *sent = join(at, o, o_came)
    return project_scatter(by_y, by_z, sent, out_weight, sources).astype(BF16)


def solution(mesh):
    fine = Mesh(mesh.devices.reshape(2, 4, 4, 2, 2), AXES)
    ctx, head = ("x", "yh", "core"), ("yl", "z")
    in_specs = (
        P(ctx, head),
        P(ctx, head),
        P(ctx, head),
        P(ctx, head),
        P(head, None, None),
        P(head, None, None),
        P(head, None, None),
        P(head, None),
    )
    out_specs = P(ctx + head, None)
    return jax.shard_map(body, mesh=fine, in_specs=in_specs, out_specs=out_specs, check_vma=False)
```

```python
import jax
import jax.numpy as jnp
from jax import lax
from jax.experimental import pallas as pl
from jax.experimental.pallas import tpu as pltpu
from jax.sharding import Mesh, PartitionSpec as P

NS_STEPS = 5
ns_a = 3.4445
ns_b = -4.775
ns_c = 2.0315
eps_value = 1e-06

AXES = ("yl", "z", "x", "yh", "core")
PLANE = ("x", "yh")
SHARDS = 8
TILE = 256
VMEM_LIMIT = 24 << 20
CUT = 2816
F32 = jnp.float32
BF16 = jnp.bfloat16


def mm(a, b):
    return jnp.dot(a, b, preferred_element_type=F32)


def mm_nt(a, b):
    return lax.dot_general(a, b, (((1,), (1,)), ((), ())), preferred_element_type=F32)


def call(kernel, name, outs, scratch, *operands):
    specs = [pl.BlockSpec(memory_space=pltpu.SMEM if a.dtype == jnp.int32 else pltpu.VMEM) for a in operands]
    return pl.pallas_call(
        kernel,
        out_shape=outs,
        in_specs=specs,
        out_specs=jax.tree.map(lambda _: pl.BlockSpec(memory_space=pltpu.VMEM), outs),
        scratch_shapes=scratch,
        compiler_params=pltpu.CompilerParams(vmem_limit_bytes=VMEM_LIMIT),
        name=name,
    )(*operands)


def out(shape, dtype):
    return jax.ShapeDtypeStruct(shape, dtype)


def sort_tokens_kernel(at_ref, k_ref, v_ref, r_ref, k_o, d_o, sent):
    width = k_o.shape[1]
    for h in range(2):

        @pl.when(at_ref[0] == h)
        def _():
            near, far = slice(h * width, (h + 1) * width), slice((1 - h) * width, (2 - h) * width)
            k_o[...] = k_ref[:, near]
            sent[:, :width] = k_ref[:, far].astype(F32)
            for head, columns in ((h, near), (1 - h, far)):
                rate = r_ref[head : head + 1, :].T
                d = (-rate * v_ref[:, columns].astype(F32)).astype(BF16)
                if head == h:
                    d_o[...] = d
                else:
                    sent[:, width:] = d.astype(F32)


def sort_tokens(at, keys, values, rates):
    shape = (keys.shape[0], keys.shape[1] // 2)
    shapes = [out(shape, BF16), out(shape, BF16), out(keys.shape, F32)]
    return call(sort_tokens_kernel, "sort_tokens", shapes, [], at, keys, values, rates)


def side_by_side(rows, r, block, width):
    top = (r * block) % (rows // 2)
    left = width * ((r * block) // (rows // 2))
    return slice(top, top + block), slice(left, left + width)


def sort_queries_kernel(at_ref, q_ref, q_o, sent):
    rows, width = q_o.shape
    block = rows // 8
    for h in range(2):

        @pl.when(at_ref[0] == h)
        def _():
            near, far = slice(h * width, (h + 1) * width), slice((1 - h) * width, (2 - h) * width)
            for r in range(8):
                row = ((at_ref[1] + r // 4) % 2) * 4 + (at_ref[2] + r % 4) % 4
                source = pl.ds(pl.multiple_of(row * block, block), block)
                q_o[r * block : (r + 1) * block, :] = q_ref[source, near]
                to_rows, to_columns = side_by_side(rows, r, block, width)
                sent[to_rows, to_columns] = q_ref[source, far].astype(F32)


def sort_queries(at, queries):
    rows, columns = queries.shape
    shapes = [out((rows, columns // 2), BF16), out((rows // 2, columns), F32)]
    return call(sort_queries_kernel, "sort_queries", shapes, [], at, queries)


def grads_of(k_ref, d_ref, w_ref, hk_s, dg_s, du_s):
    rows = k_ref.shape[0]
    wg, wu, wd = w_ref[0], w_ref[1], w_ref[2]
    step = 256
    for t in range(0, rows, step):
        at = slice(t, t + step)
        k = k_ref[at, :]
        gate = mm(k, wg)
        upper = mm(k, wu)
        dhid = mm(d_ref[at, :], wd)
        sig = jax.nn.sigmoid(gate)
        act = gate * sig
        hk_s[at, :] = (act * upper).astype(BF16)
        dg_s[at, :] = (dhid * upper * sig * (1.0 + gate * (1.0 - sig))).astype(BF16)
        du_s[at, :] = (dhid * act).astype(BF16)
    kt = k_ref[...].T
    dt = d_ref[...].T
    for m, (left, right) in enumerate(((kt, dg_s), (kt, du_s), (dt, hk_s))):
        yield m, mm(left, right[...])


def near_grads_kernel(at_ref, k_ref, d_ref, g_ref, u_ref, w_ref, o_ref, b_ref, f_s, hk_s, dg_s, du_s, sems):
    copies = [
        pltpu.make_async_copy(ref.at[at_ref[0]], f_s.at[m], sems.at[m]) for m, ref in enumerate((g_ref, u_ref, w_ref))
    ]
    for copy in copies:
        copy.start()
    for m, copy in enumerate(copies):
        copy.wait()
        b_ref[m] = f_s[m].astype(BF16)
    for m, grad in grads_of(k_ref, d_ref, b_ref, hk_s, dg_s, du_s):
        o_ref[m] = grad


def far_grads_kernel(came, b_ref, p_ref, o_ref, k_s, d_s, hk_s, dg_s, du_s):
    part = o_ref.shape[2]
    width = k_s.shape[1]
    k_s[...] = came[:, :width].astype(BF16)
    d_s[...] = came[:, width:].astype(BF16)
    for m, grad in grads_of(k_s, d_s, b_ref, hk_s, dg_s, du_s):
        for j in range(SHARDS):
            rows = slice(j * part, (j + 1) * part)
            o_ref[j, m] = grad[rows, :] + p_ref[m, rows, :]


def near_grads(at, k, d, gate, up, down):
    heads, width, hidden = gate.shape
    vmem, hbm = pl.BlockSpec(memory_space=pltpu.VMEM), pl.BlockSpec(memory_space=pltpu.HBM)
    shape = (3, width, hidden)
    return pl.pallas_call(
        near_grads_kernel,
        out_shape=[out(shape, F32), out(shape, BF16)],
        in_specs=[pl.BlockSpec(memory_space=pltpu.SMEM), vmem, vmem, hbm, hbm, hbm],
        out_specs=[vmem, vmem],
        scratch_shapes=[pltpu.VMEM(shape, F32)]
        + [pltpu.VMEM((k.shape[0], hidden), BF16)] * 3
        + [pltpu.SemaphoreType.DMA((3,))],
        compiler_params=pltpu.CompilerParams(vmem_limit_bytes=VMEM_LIMIT),
        name="near_grads",
    )(at, k, d, gate, up, down)


def far_grads(came, w, partial):
    heads, width, hidden = partial.shape
    rows = came.shape[0]
    scratch = [pltpu.VMEM((rows, width), BF16)] * 2 + [pltpu.VMEM((rows, hidden), BF16)] * 3
    shape = out((SHARDS, 3, width // SHARDS, hidden), F32)
    return call(far_grads_kernel, "far_grads", shape, scratch, came, w, partial)


def split(x):
    high = x.astype(BF16)
    return high, (x - high.astype(F32)).astype(BF16)


def packed(high, low):
    return jnp.concatenate([high, high, low], axis=1)


def mirrored(left, corner):
    at = left.shape[1]
    return jnp.concatenate([left, jnp.concatenate([left[at:].T, corner], axis=0)], axis=1)


def gram_of(xh, xl):
    a, b = packed(xh, xl), jnp.concatenate([xh, xl, xh], axis=1)
    return mirrored(mm_nt(a, b[:TILE]), mm_nt(a[TILE:], b[TILE:]))


def square_of(ah, al):
    a, b = packed(ah, al), jnp.concatenate([ah, al, ah], axis=0)
    return mirrored(mm(a, b[:, :TILE]), mm(a[TILE:], b[:, TILE:]))


def newton_kernel(at_ref, g_ref, wg_ref, wu_ref, wd_ref, v_ref, x_s, f_s, sems):
    copies = [
        pltpu.make_async_copy(ref.at[at_ref[0]], f_s.at[m], sems.at[m])
        for m, ref in enumerate((wg_ref, wu_ref, wd_ref))
    ]
    for copy in copies:
        copy.start()
    matrices, width, hidden = x_s.shape
    every = range(matrices)
    for m in every:
        grad = g_ref[:, m].reshape(width, hidden)
        total = jnp.sum(jnp.sum(grad * grad, axis=1, keepdims=True), axis=0, keepdims=True)
        x_s[m] = grad * lax.rsqrt(total + eps_value)

    def sweep(_, carry):
        xs = [x_s[m] for m in every]
        parts = [split(x) for x in xs]
        grams = [gram_of(*p) for p in parts]
        squares = [square_of(*split(g)) for g in grams]
        mixers = [split(ns_b * g + ns_c * q) for g, q in zip(grams, squares)]
        for m, x, (xh, xl), mixer in zip(every, xs, parts, mixers):
            x_s[m] = ns_a * x + mm(packed(*mixer), jnp.concatenate([xh, xl, xh], axis=0))
        return carry

    lax.fori_loop(0, NS_STEPS, sweep, 0)
    for m, copy in enumerate(copies):
        copy.wait()
        v_ref[m] = (f_s[m] - x_s[m]).astype(BF16)


def newton(at, grads, gate, up, down):
    shape = (grads.shape[1], grads.shape[0] * grads.shape[2], grads.shape[3])
    vmem, hbm = pl.BlockSpec(memory_space=pltpu.VMEM), pl.BlockSpec(memory_space=pltpu.HBM)
    return pl.pallas_call(
        newton_kernel,
        out_shape=out(shape, BF16),
        in_specs=[pl.BlockSpec(memory_space=pltpu.SMEM), vmem, hbm, hbm, hbm],
        out_specs=vmem,
        scratch_shapes=[pltpu.VMEM(shape, F32)] * 2 + [pltpu.SemaphoreType.DMA((3,))],
        compiler_params=pltpu.CompilerParams(vmem_limit_bytes=VMEM_LIMIT),
        name="newton",
    )(at, grads, gate, up, down)


def query_rows(q, v_ref):
    gate = mm(q, v_ref[0])
    hidden = (gate * jax.nn.sigmoid(gate) * mm(q, v_ref[1])).astype(BF16)
    return mm_nt(hidden, v_ref[2]).astype(BF16)


def far_query_kernel(came, v_ref, o_ref):
    width = came.shape[1] // 2
    for left in (0, width):
        columns = slice(left, left + width)
        o_ref[:, columns] = query_rows(came[:, columns].astype(BF16), v_ref).astype(F32)


def near_query_kernel(q_ref, v_ref, o_ref):
    half = q_ref.shape[0] // 2
    for top in (0, half):
        rows = slice(top, top + half)
        o_ref[rows, :] = query_rows(q_ref[rows, :], v_ref)


def join_kernel(at_ref, o_ref, came, y_ref, z_ref):
    rows, width = o_ref.shape
    block = rows // 8
    for h in range(2):

        @pl.when(at_ref[0] == h)
        def _():
            near, far = slice(h * width, (h + 1) * width), slice((1 - h) * width, (2 - h) * width)
            for dy in range(2):
                for dz in range(4):
                    r = dy * 4 + dz
                    to_y, to_z = pl.ds(dz * block, block), pl.ds(dy * block, block)
                    mine = o_ref[r * block : (r + 1) * block, :]
                    other = came[side_by_side(rows, r, block, width)].astype(BF16)
                    for columns, piece in ((near, mine), (far, other)):
                        y_ref[dy, to_y, columns] = piece
                        z_ref[dz, to_z, columns] = piece


def join(at, mine, came):
    rows, width = mine.shape
    shapes = [out((n, rows // n, 2 * width), BF16) for n in (2, 4)]
    return call(join_kernel, "join", shapes, [], at, mine, came)


def swap(a, axis):
    return lax.ppermute(a, axis, [(0, 1), (1, 0)])


def ring(a, shift):
    return lax.ppermute(a, "z", [(i, (i + shift) % 4) for i in range(4)])


def plane_scatter(a):
    return jnp.sum(lax.all_to_all(a, PLANE, 0, 0, tiled=True), axis=0)


def plane_gather(a):
    same = jnp.broadcast_to(a[None], (SHARDS,) + a.shape)
    return lax.all_to_all(same, PLANE, 0, 0, tiled=True)


def together(*arrays):
    return lax.optimization_barrier(arrays)


def halves(a):
    half = a.shape[0] // 2
    return a[:half], a[half:]


def pass_two(a):
    up, down = halves(a)
    return ring(up, 1), ring(down, -1)


def pass_one(one, three, came):
    up, down = came
    one = jnp.concatenate([one[: up.shape[0]] + up, one[up.shape[0] :]], axis=0)
    three = jnp.concatenate([three[: up.shape[0]], three[up.shape[0] :] + down], axis=0)
    return (ring(one, 1), ring(three, -1)), (one, three)


def project_scatter(by_y, by_z, weight):
    wa, wb = weight[:, :CUT], weight[:, CUT:]
    b_far, by_z = together(mm(by_y[1], wb), by_z)
    b_came = swap(b_far, "yl")
    a_came = pass_two(mm(by_z[2], wa))
    a_came, a_sent = pass_one(mm(by_z[1], wa), mm(by_z[3], wa), a_came)
    b = mm(by_y[0], wb) + b_came
    b = b.reshape(4, -1, b.shape[1])
    b_came = pass_two(b[2])
    a = mm(by_z[0], wa) + sum(a_came)
    a, a_far = halves(a)
    a_came = swap(a_far, "yl")
    b_came, _ = pass_one(b[1], b[3], b_came)
    return jnp.concatenate([a + a_came, b[0] + sum(b_came)], axis=1)


def body(keys, queries, values, rates, gate, up, down, out_weight):
    at = jnp.stack([lax.axis_index(name).astype(jnp.int32) for name in ("core", "yl", "z")])
    weights = tuple(pltpu.with_memory_space_constraint(w, pltpu.HBM) for w in (gate, up, down))
    k, d, sent = sort_tokens(at, keys, values, rates.T)
    came = swap(sent, "core")
    partial, rounded = near_grads(at, k, d, *weights)
    total = plane_scatter(far_grads(came, rounded, partial))
    total, queries = together(total, queries)
    q, q_sent = sort_queries(at, queries)
    whole, q_sent = together(plane_gather(total), q_sent)
    q_came = swap(q_sent, "core")
    v = newton(at, whole, *weights)
    o_came = swap(call(far_query_kernel, "far_query", out(q_sent.shape, F32), [], q_came, v), "core")
    o = call(near_query_kernel, "near_query", out(q.shape, BF16), [], q, v)
    by_y, by_z = join(at, o, o_came)
    return project_scatter(by_y, by_z, out_weight).astype(BF16)


def solution(mesh):
    fine = Mesh(mesh.devices.reshape(2, 4, 4, 2, 2), AXES)
    ctx, head = ("x", "yh", "core"), ("yl", "z")
    in_specs = (
        P(ctx, head),
        P(ctx, head),
        P(ctx, head),
        P(ctx, head),
        P(head, None, None),
        P(head, None, None),
        P(head, None, None),
        P(head, None),
    )
    out_specs = P(ctx + head, None)
    return jax.shard_map(body, mesh=fine, in_specs=in_specs, out_specs=out_specs, check_vma=False)
```

```python
import jax
import jax.numpy as jnp
from jax import lax
from jax.experimental import pallas as pl
from jax.experimental.pallas import tpu as pltpu
from jax.sharding import Mesh, PartitionSpec as P

NS_STEPS = 5
ns_a = 3.4445
ns_b = -4.775
ns_c = 2.0315
eps_value = 1e-06

AXES = ("yl", "z", "x", "yh", "core")
PLANE = ("x", "yh")
SHARDS = 8
TILE = 256
VMEM_LIMIT = 24 << 20
CUT = 2816
Y_ORDER = (2, 0, 1, 3)
F32 = jnp.float32
BF16 = jnp.bfloat16


def mm(a, b):
    return jnp.dot(a, b, preferred_element_type=F32)


def mm_nt(a, b):
    return lax.dot_general(a, b, (((1,), (1,)), ((), ())), preferred_element_type=F32)


def call(kernel, name, outs, scratch, *operands):
    specs = [pl.BlockSpec(memory_space=pltpu.SMEM if a.dtype == jnp.int32 else pltpu.VMEM) for a in operands]
    return pl.pallas_call(
        kernel,
        out_shape=outs,
        in_specs=specs,
        out_specs=jax.tree.map(lambda _: pl.BlockSpec(memory_space=pltpu.VMEM), outs),
        scratch_shapes=scratch,
        compiler_params=pltpu.CompilerParams(vmem_limit_bytes=VMEM_LIMIT),
        name=name,
    )(*operands)


def out(shape, dtype):
    return jax.ShapeDtypeStruct(shape, dtype)


def sort_tokens_kernel(at_ref, k_ref, v_ref, r_ref, k_o, d_o, sent):
    width = k_o.shape[1]
    for h in range(2):

        @pl.when(at_ref[0] == h)
        def _():
            near, far = slice(h * width, (h + 1) * width), slice((1 - h) * width, (2 - h) * width)
            k_o[...] = k_ref[:, near]
            sent[:, :width] = k_ref[:, far].astype(F32)
            for head, columns in ((h, near), (1 - h, far)):
                rate = r_ref[head : head + 1, :].T
                d = (-rate * v_ref[:, columns].astype(F32)).astype(BF16)
                if head == h:
                    d_o[...] = d
                else:
                    sent[:, width:] = d.astype(F32)


def sort_tokens(at, keys, values, rates):
    shape = (keys.shape[0], keys.shape[1] // 2)
    shapes = [out(shape, BF16), out(shape, BF16), out(keys.shape, F32)]
    return call(sort_tokens_kernel, "sort_tokens", shapes, [], at, keys, values, rates)


def side_by_side(rows, r, block, width):
    top = (r * block) % (rows // 2)
    left = width * ((r * block) // (rows // 2))
    return slice(top, top + block), slice(left, left + width)


def sort_queries_kernel(at_ref, q_ref, q_o, sent):
    rows, width = q_o.shape
    block = rows // 8
    for h in range(2):

        @pl.when(at_ref[0] == h)
        def _():
            near, far = slice(h * width, (h + 1) * width), slice((1 - h) * width, (2 - h) * width)
            for r in range(8):
                row = ((at_ref[1] + r // 4) % 2) * 4 + (at_ref[2] + r % 4) % 4
                source = pl.ds(pl.multiple_of(row * block, block), block)
                q_o[r * block : (r + 1) * block, :] = q_ref[source, near]
                to_rows, to_columns = side_by_side(rows, r, block, width)
                sent[to_rows, to_columns] = q_ref[source, far].astype(F32)


def sort_queries(at, queries):
    rows, columns = queries.shape
    shapes = [out((rows, columns // 2), BF16), out((rows // 2, columns), F32)]
    return call(sort_queries_kernel, "sort_queries", shapes, [], at, queries)


def grads_of(k_ref, d_ref, w_ref, hk_s, dg_s, du_s):
    rows = k_ref.shape[0]
    wg, wu, wd = w_ref[0], w_ref[1], w_ref[2]
    step = 256
    for t in range(0, rows, step):
        at = slice(t, t + step)
        k = k_ref[at, :]
        gate = mm(k, wg)
        upper = mm(k, wu)
        dhid = mm(d_ref[at, :], wd)
        sig = jax.nn.sigmoid(gate)
        act = gate * sig
        hk_s[at, :] = (act * upper).astype(BF16)
        dg_s[at, :] = (dhid * upper * sig * (1.0 + gate * (1.0 - sig))).astype(BF16)
        du_s[at, :] = (dhid * act).astype(BF16)
    kt = k_ref[...].T
    dt = d_ref[...].T
    for m, (left, right) in enumerate(((kt, dg_s), (kt, du_s), (dt, hk_s))):
        yield m, mm(left, right[...])


def near_grads_kernel(at_ref, k_ref, d_ref, g_ref, u_ref, w_ref, o_ref, b_ref, f_s, hk_s, dg_s, du_s, sems):
    copies = [
        pltpu.make_async_copy(ref.at[at_ref[0]], f_s.at[m], sems.at[m]) for m, ref in enumerate((g_ref, u_ref, w_ref))
    ]
    for copy in copies:
        copy.start()
    for m, copy in enumerate(copies):
        copy.wait()
        b_ref[m] = f_s[m].astype(BF16)
    for m, grad in grads_of(k_ref, d_ref, b_ref, hk_s, dg_s, du_s):
        o_ref[m] = grad


def far_grads_kernel(came, b_ref, p_ref, o_ref, k_s, d_s, hk_s, dg_s, du_s):
    part = o_ref.shape[2]
    width = k_s.shape[1]
    k_s[...] = came[:, :width].astype(BF16)
    d_s[...] = came[:, width:].astype(BF16)
    for m, grad in grads_of(k_s, d_s, b_ref, hk_s, dg_s, du_s):
        for j in range(SHARDS):
            rows = slice(j * part, (j + 1) * part)
            o_ref[j, m] = grad[rows, :] + p_ref[m, rows, :]


def near_grads(at, k, d, gate, up, down):
    heads, width, hidden = gate.shape
    vmem, hbm = pl.BlockSpec(memory_space=pltpu.VMEM), pl.BlockSpec(memory_space=pltpu.HBM)
    shape = (3, width, hidden)
    return pl.pallas_call(
        near_grads_kernel,
        out_shape=[out(shape, F32), out(shape, BF16)],
        in_specs=[pl.BlockSpec(memory_space=pltpu.SMEM), vmem, vmem, hbm, hbm, hbm],
        out_specs=[vmem, vmem],
        scratch_shapes=[pltpu.VMEM(shape, F32)]
        + [pltpu.VMEM((k.shape[0], hidden), BF16)] * 3
        + [pltpu.SemaphoreType.DMA((3,))],
        compiler_params=pltpu.CompilerParams(vmem_limit_bytes=VMEM_LIMIT),
        name="near_grads",
    )(at, k, d, gate, up, down)


def far_grads(came, w, partial):
    heads, width, hidden = partial.shape
    rows = came.shape[0]
    scratch = [pltpu.VMEM((rows, width), BF16)] * 2 + [pltpu.VMEM((rows, hidden), BF16)] * 3
    shape = out((SHARDS, 3, width // SHARDS, hidden), F32)
    return call(far_grads_kernel, "far_grads", shape, scratch, came, w, partial)


def split(x):
    high = x.astype(BF16)
    return high, (x - high.astype(F32)).astype(BF16)


def packed(high, low):
    return jnp.concatenate([high, high, low], axis=1)


def mirrored(left, corner):
    at = left.shape[1]
    return jnp.concatenate([left, jnp.concatenate([left[at:].T, corner], axis=0)], axis=1)


def gram_of(xh, xl):
    a, b = packed(xh, xl), jnp.concatenate([xh, xl, xh], axis=1)
    return mirrored(mm_nt(a, b[:TILE]), mm_nt(a[TILE:], b[TILE:]))


def square_of(ah, al):
    a, b = packed(ah, al), jnp.concatenate([ah, al, ah], axis=0)
    return mirrored(mm(a, b[:, :TILE]), mm(a[TILE:], b[:, TILE:]))


def newton_kernel(at_ref, g_ref, wg_ref, wu_ref, wd_ref, v_ref, x_s, f_s, sems):
    copies = [
        pltpu.make_async_copy(ref.at[at_ref[0]], f_s.at[m], sems.at[m])
        for m, ref in enumerate((wg_ref, wu_ref, wd_ref))
    ]
    for copy in copies:
        copy.start()
    matrices, width, hidden = x_s.shape
    every = range(matrices)
    for m in every:
        grad = g_ref[:, m].reshape(width, hidden)
        total = jnp.sum(jnp.sum(grad * grad, axis=1, keepdims=True), axis=0, keepdims=True)
        x_s[m] = grad * lax.rsqrt(total + eps_value)

    def sweep(_, carry):
        xs = [x_s[m] for m in every]
        parts = [split(x) for x in xs]
        grams = [gram_of(*p) for p in parts]
        squares = [square_of(*split(g)) for g in grams]
        mixers = [split(ns_b * g + ns_c * q) for g, q in zip(grams, squares)]
        for m, x, (xh, xl), mixer in zip(every, xs, parts, mixers):
            x_s[m] = ns_a * x + mm(packed(*mixer), jnp.concatenate([xh, xl, xh], axis=0))
        return carry

    lax.fori_loop(0, NS_STEPS, sweep, 0)
    for m, copy in enumerate(copies):
        copy.wait()
        v_ref[m] = (f_s[m] - x_s[m]).astype(BF16)


def newton(at, grads, gate, up, down):
    shape = (grads.shape[1], grads.shape[0] * grads.shape[2], grads.shape[3])
    vmem, hbm = pl.BlockSpec(memory_space=pltpu.VMEM), pl.BlockSpec(memory_space=pltpu.HBM)
    return pl.pallas_call(
        newton_kernel,
        out_shape=out(shape, BF16),
        in_specs=[pl.BlockSpec(memory_space=pltpu.SMEM), vmem, hbm, hbm, hbm],
        out_specs=vmem,
        scratch_shapes=[pltpu.VMEM(shape, F32)] * 2 + [pltpu.SemaphoreType.DMA((3,))],
        compiler_params=pltpu.CompilerParams(vmem_limit_bytes=VMEM_LIMIT),
        name="newton",
    )(at, grads, gate, up, down)


def query_rows(q, v_ref):
    gate = mm(q, v_ref[0])
    hidden = (gate * jax.nn.sigmoid(gate) * mm(q, v_ref[1])).astype(BF16)
    return mm_nt(hidden, v_ref[2]).astype(BF16)


def far_query_kernel(came, v_ref, o_ref):
    width = came.shape[1] // 2
    for left in (0, width):
        columns = slice(left, left + width)
        o_ref[:, columns] = query_rows(came[:, columns].astype(BF16), v_ref).astype(F32)


def near_query_kernel(q_ref, v_ref, o_ref):
    half = q_ref.shape[0] // 2
    for top in (0, half):
        rows = slice(top, top + half)
        o_ref[rows, :] = query_rows(q_ref[rows, :], v_ref)


def join_kernel(at_ref, o_ref, came, y_ref, z_ref):
    rows, width = o_ref.shape
    block = rows // 8
    for h in range(2):

        @pl.when(at_ref[0] == h)
        def _():
            near, far = slice(h * width, (h + 1) * width), slice((1 - h) * width, (2 - h) * width)
            for dy in range(2):
                for dz in range(4):
                    r = dy * 4 + dz
                    to_y, to_z = pl.ds(Y_ORDER.index(dz) * block, block), pl.ds(dy * block, block)
                    mine = o_ref[r * block : (r + 1) * block, :]
                    other = came[side_by_side(rows, r, block, width)].astype(BF16)
                    for columns, piece in ((near, mine), (far, other)):
                        y_ref[dy, to_y, columns] = piece
                        z_ref[dz, to_z, columns] = piece


def join(at, mine, came):
    rows, width = mine.shape
    shapes = [out((n, rows // n, 2 * width), BF16) for n in (2, 4)]
    return call(join_kernel, "join", shapes, [], at, mine, came)


def swap(a, axis):
    return lax.ppermute(a, axis, [(0, 1), (1, 0)])


def ring(a, shift):
    return lax.ppermute(a, "z", [(i, (i + shift) % 4) for i in range(4)])


def plane_scatter(a):
    return jnp.sum(lax.all_to_all(a, PLANE, 0, 0, tiled=True), axis=0)


def plane_gather(a):
    same = jnp.broadcast_to(a[None], (SHARDS,) + a.shape)
    return lax.all_to_all(same, PLANE, 0, 0, tiled=True)


def together(*arrays):
    return lax.optimization_barrier(arrays)


def halves(a):
    half = a.shape[0] // 2
    return a[:half], a[half:]


def both_ways(up, down):
    return ring(up, 1), ring(down, -1)


def project_scatter(by_y, by_z, weight):
    wa, wb = weight[:, :CUT], weight[:, CUT:]
    block = by_z.shape[1] // 2
    far_two, far_rest = mm(by_y[1, :block], wb), mm(by_y[1, block:], wb)
    far_two, far_rest, by_z = together(far_two, far_rest, by_z)
    b_two, b_rest = swap(far_two, "yl"), swap(far_rest, "yl")
    up, down = both_ways(*halves(mm(by_z[2], wa)))
    one, three = mm(by_z[1], wa), mm(by_z[3], wa)
    one = jnp.concatenate([one[:block] + up, one[block:]], axis=0)
    three = jnp.concatenate([three[:block], three[block:] + down], axis=0)
    one, three, b_two = together(one, three, b_two)
    a_came = both_ways(one, three)
    b_two = b_two + mm(by_y[0, :block], wb)
    b_up, b_down = both_ways(*halves(b_two))
    b_rest = b_rest + mm(by_y[0, block:], wb)
    half = block // 2
    b_one, b_three = b_rest[block : 2 * block], b_rest[2 * block :]
    b_one = jnp.concatenate([b_one[:half] + b_up, b_one[half:]], axis=0)
    b_three = jnp.concatenate([b_three[:half], b_three[half:] + b_down], axis=0)
    a = mm(by_z[0], wa) + sum(a_came)
    a, b_one, b_three = together(a, b_one, b_three)
    b_came = both_ways(b_one, b_three)
    a_came = swap(a[block:], "yl")
    return jnp.concatenate([a[:block] + a_came, b_rest[:block] + sum(b_came)], axis=1)


def body(keys, queries, values, rates, gate, up, down, out_weight):
    at = jnp.stack([lax.axis_index(name).astype(jnp.int32) for name in ("core", "yl", "z")])
    weights = tuple(pltpu.with_memory_space_constraint(w, pltpu.HBM) for w in (gate, up, down))
    k, d, sent = sort_tokens(at, keys, values, rates.T)
    came = swap(sent, "core")
    partial, rounded = near_grads(at, k, d, *weights)
    queries, partial = together(queries, partial)
    q, q_sent = sort_queries(at, queries)
    summed = far_grads(came, rounded, partial)
    q_sent, summed = together(q_sent, summed)
    total = plane_scatter(summed)
    whole, q_sent = together(plane_gather(total), q_sent)
    q_came = swap(q_sent, "core")
    v = newton(at, whole, *weights)
    o_came = swap(call(far_query_kernel, "far_query", out(q_sent.shape, F32), [], q_came, v), "core")
    o = call(near_query_kernel, "near_query", out(q.shape, BF16), [], q, v)
    by_y, by_z = join(at, o, o_came)
    return project_scatter(by_y, by_z, out_weight).astype(BF16)


def solution(mesh):
    fine = Mesh(mesh.devices.reshape(2, 4, 4, 2, 2), AXES)
    ctx, head = ("x", "yh", "core"), ("yl", "z")
    in_specs = (
        P(ctx, head),
        P(ctx, head),
        P(ctx, head),
        P(ctx, head),
        P(head, None, None),
        P(head, None, None),
        P(head, None, None),
        P(head, None),
    )
    out_specs = P(ctx + head, None)
    return jax.shard_map(body, mesh=fine, in_specs=in_specs, out_specs=out_specs, check_vma=False)
```

```python
import jax
import jax.numpy as jnp
from jax import lax
from jax.experimental import pallas as pl
from jax.experimental.pallas import tpu as pltpu
from jax.sharding import Mesh, PartitionSpec as P

NS_STEPS = 5
ns_a = 3.4445
ns_b = -4.775
ns_c = 2.0315
eps_value = 1e-06

AXES = ("yl", "z", "x", "yh", "core")
PLANE = ("x", "yh")
SHARDS = 8
TILE = 256
VMEM_LIMIT = 24 << 20
CUT = 2944
Y_ORDER = (2, 0, 1, 3)
F32 = jnp.float32
BF16 = jnp.bfloat16


def mm(a, b):
    return jnp.dot(a, b, preferred_element_type=F32)


def mm_nt(a, b):
    return lax.dot_general(a, b, (((1,), (1,)), ((), ())), preferred_element_type=F32)


def call(kernel, name, outs, scratch, *operands):
    specs = [pl.BlockSpec(memory_space=pltpu.SMEM if a.dtype == jnp.int32 else pltpu.VMEM) for a in operands]
    return pl.pallas_call(
        kernel,
        out_shape=outs,
        in_specs=specs,
        out_specs=jax.tree.map(lambda _: pl.BlockSpec(memory_space=pltpu.VMEM), outs),
        scratch_shapes=scratch,
        compiler_params=pltpu.CompilerParams(vmem_limit_bytes=VMEM_LIMIT),
        name=name,
    )(*operands)


def out(shape, dtype):
    return jax.ShapeDtypeStruct(shape, dtype)


def sort_tokens_kernel(at_ref, k_ref, v_ref, r_ref, k_o, d_o, sent):
    width = k_o.shape[1]
    for h in range(2):

        @pl.when(at_ref[0] == h)
        def _():
            near, far = slice(h * width, (h + 1) * width), slice((1 - h) * width, (2 - h) * width)
            k_o[...] = k_ref[:, near]
            sent[:, :width] = k_ref[:, far].astype(F32)
            for head, columns in ((h, near), (1 - h, far)):
                rate = r_ref[head : head + 1, :].T
                d = (-rate * v_ref[:, columns].astype(F32)).astype(BF16)
                if head == h:
                    d_o[...] = d
                else:
                    sent[:, width:] = d.astype(F32)


def sort_tokens(at, keys, values, rates):
    shape = (keys.shape[0], keys.shape[1] // 2)
    shapes = [out(shape, BF16), out(shape, BF16), out(keys.shape, F32)]
    return call(sort_tokens_kernel, "sort_tokens", shapes, [], at, keys, values, rates)


def side_by_side(rows, r, block, width):
    top = (r * block) % (rows // 2)
    left = width * ((r * block) // (rows // 2))
    return slice(top, top + block), slice(left, left + width)


def sort_queries_kernel(at_ref, q_ref, q_o, sent):
    rows, width = q_o.shape
    block = rows // 8
    for h in range(2):

        @pl.when(at_ref[0] == h)
        def _():
            near, far = slice(h * width, (h + 1) * width), slice((1 - h) * width, (2 - h) * width)
            for r in range(8):
                row = ((at_ref[1] + r // 4) % 2) * 4 + (at_ref[2] + r % 4) % 4
                source = pl.ds(pl.multiple_of(row * block, block), block)
                q_o[r * block : (r + 1) * block, :] = q_ref[source, near]
                to_rows, to_columns = side_by_side(rows, r, block, width)
                sent[to_rows, to_columns] = q_ref[source, far].astype(F32)


def sort_queries(at, queries):
    rows, columns = queries.shape
    shapes = [out((rows, columns // 2), BF16), out((rows // 2, columns), F32)]
    return call(sort_queries_kernel, "sort_queries", shapes, [], at, queries)


def grads_of(k_ref, d_ref, w_ref, hk_s, dg_s, du_s):
    rows = k_ref.shape[0]
    wg, wu, wd = w_ref[0], w_ref[1], w_ref[2]
    step = 256
    for t in range(0, rows, step):
        at = slice(t, t + step)
        k = k_ref[at, :]
        gate = mm(k, wg)
        upper = mm(k, wu)
        dhid = mm(d_ref[at, :], wd)
        sig = jax.nn.sigmoid(gate)
        act = gate * sig
        hk_s[at, :] = (act * upper).astype(BF16)
        dg_s[at, :] = (dhid * upper * sig * (1.0 + gate * (1.0 - sig))).astype(BF16)
        du_s[at, :] = (dhid * act).astype(BF16)
    kt = k_ref[...].T
    dt = d_ref[...].T
    for m, (left, right) in enumerate(((kt, dg_s), (kt, du_s), (dt, hk_s))):
        yield m, mm(left, right[...])


def near_grads_kernel(at_ref, k_ref, d_ref, g_ref, u_ref, w_ref, o_ref, b_ref, f_s, hk_s, dg_s, du_s, sems):
    copies = [
        pltpu.make_async_copy(ref.at[at_ref[0]], f_s.at[m], sems.at[m]) for m, ref in enumerate((g_ref, u_ref, w_ref))
    ]
    for copy in copies:
        copy.start()
    for m, copy in enumerate(copies):
        copy.wait()
        b_ref[m] = f_s[m].astype(BF16)
    for m, grad in grads_of(k_ref, d_ref, b_ref, hk_s, dg_s, du_s):
        o_ref[m] = grad


def far_grads_kernel(came, b_ref, p_ref, o_ref, k_s, d_s, hk_s, dg_s, du_s):
    part = o_ref.shape[2]
    width = k_s.shape[1]
    k_s[...] = came[:, :width].astype(BF16)
    d_s[...] = came[:, width:].astype(BF16)
    for m, grad in grads_of(k_s, d_s, b_ref, hk_s, dg_s, du_s):
        for j in range(SHARDS):
            rows = slice(j * part, (j + 1) * part)
            o_ref[j, m] = grad[rows, :] + p_ref[m, rows, :]


def near_grads(at, k, d, gate, up, down):
    heads, width, hidden = gate.shape
    vmem, hbm = pl.BlockSpec(memory_space=pltpu.VMEM), pl.BlockSpec(memory_space=pltpu.HBM)
    shape = (3, width, hidden)
    return pl.pallas_call(
        near_grads_kernel,
        out_shape=[out(shape, F32), out(shape, BF16)],
        in_specs=[pl.BlockSpec(memory_space=pltpu.SMEM), vmem, vmem, hbm, hbm, hbm],
        out_specs=[vmem, vmem],
        scratch_shapes=[pltpu.VMEM(shape, F32)]
        + [pltpu.VMEM((k.shape[0], hidden), BF16)] * 3
        + [pltpu.SemaphoreType.DMA((3,))],
        compiler_params=pltpu.CompilerParams(vmem_limit_bytes=VMEM_LIMIT),
        name="near_grads",
    )(at, k, d, gate, up, down)


def far_grads(came, w, partial):
    heads, width, hidden = partial.shape
    rows = came.shape[0]
    scratch = [pltpu.VMEM((rows, width), BF16)] * 2 + [pltpu.VMEM((rows, hidden), BF16)] * 3
    shape = out((SHARDS, 3, width // SHARDS, hidden), F32)
    return call(far_grads_kernel, "far_grads", shape, scratch, came, w, partial)


def split(x):
    high = x.astype(BF16)
    return high, (x - high.astype(F32)).astype(BF16)


def packed(high, low):
    return jnp.concatenate([high, high, low], axis=1)


def mirrored(left, corner):
    at = left.shape[1]
    return jnp.concatenate([left, jnp.concatenate([left[at:].T, corner], axis=0)], axis=1)


def gram_of(xh, xl):
    a, b = packed(xh, xl), jnp.concatenate([xh, xl, xh], axis=1)
    return mirrored(mm_nt(a, b[:TILE]), mm_nt(a[TILE:], b[TILE:]))


def square_of(ah, al):
    a, b = packed(ah, al), jnp.concatenate([ah, al, ah], axis=0)
    return mirrored(mm(a, b[:, :TILE]), mm(a[TILE:], b[:, TILE:]))


def newton_kernel(at_ref, g_ref, wg_ref, wu_ref, wd_ref, v_ref, x_s, f_s, sems):
    copies = [
        pltpu.make_async_copy(ref.at[at_ref[0]], f_s.at[m], sems.at[m])
        for m, ref in enumerate((wg_ref, wu_ref, wd_ref))
    ]
    for copy in copies:
        copy.start()
    matrices, width, hidden = x_s.shape
    every = range(matrices)
    for m in every:
        grad = g_ref[:, m].reshape(width, hidden)
        total = jnp.sum(jnp.sum(grad * grad, axis=1, keepdims=True), axis=0, keepdims=True)
        x_s[m] = grad * lax.rsqrt(total + eps_value)

    def sweep(_, carry):
        xs = [x_s[m] for m in every]
        parts = [split(x) for x in xs]
        grams = [gram_of(*p) for p in parts]
        squares = [square_of(*split(g)) for g in grams]
        mixers = [split(ns_b * g + ns_c * q) for g, q in zip(grams, squares)]
        for m, x, (xh, xl), mixer in zip(every, xs, parts, mixers):
            x_s[m] = ns_a * x + mm(packed(*mixer), jnp.concatenate([xh, xl, xh], axis=0))
        return carry

    lax.fori_loop(0, NS_STEPS, sweep, 0)
    for m, copy in enumerate(copies):
        copy.wait()
        v_ref[m] = (f_s[m] - x_s[m]).astype(BF16)


def newton(at, grads, gate, up, down):
    shape = (grads.shape[1], grads.shape[0] * grads.shape[2], grads.shape[3])
    vmem, hbm = pl.BlockSpec(memory_space=pltpu.VMEM), pl.BlockSpec(memory_space=pltpu.HBM)
    return pl.pallas_call(
        newton_kernel,
        out_shape=out(shape, BF16),
        in_specs=[pl.BlockSpec(memory_space=pltpu.SMEM), vmem, hbm, hbm, hbm],
        out_specs=vmem,
        scratch_shapes=[pltpu.VMEM(shape, F32)] * 2 + [pltpu.SemaphoreType.DMA((3,))],
        compiler_params=pltpu.CompilerParams(vmem_limit_bytes=VMEM_LIMIT),
        name="newton",
    )(at, grads, gate, up, down)


def query_rows(q, v_ref):
    gate = mm(q, v_ref[0])
    hidden = (gate * jax.nn.sigmoid(gate) * mm(q, v_ref[1])).astype(BF16)
    return mm_nt(hidden, v_ref[2]).astype(BF16)


def far_query_kernel(came, v_ref, o_ref):
    width = came.shape[1] // 2
    for left in (0, width):
        columns = slice(left, left + width)
        o_ref[:, columns] = query_rows(came[:, columns].astype(BF16), v_ref).astype(F32)


def near_query_kernel(q_ref, v_ref, o_ref):
    half = q_ref.shape[0] // 2
    for top in (0, half):
        rows = slice(top, top + half)
        o_ref[rows, :] = query_rows(q_ref[rows, :], v_ref)


def join_kernel(at_ref, o_ref, came, y_ref, z_ref):
    rows, width = o_ref.shape
    block = rows // 8
    for h in range(2):

        @pl.when(at_ref[0] == h)
        def _():
            near, far = slice(h * width, (h + 1) * width), slice((1 - h) * width, (2 - h) * width)
            for dy in range(2):
                for dz in range(4):
                    r = dy * 4 + dz
                    to_y, to_z = pl.ds(Y_ORDER.index(dz) * block, block), pl.ds(dy * block, block)
                    mine = o_ref[r * block : (r + 1) * block, :]
                    other = came[side_by_side(rows, r, block, width)].astype(BF16)
                    for columns, piece in ((near, mine), (far, other)):
                        y_ref[dy, to_y, columns] = piece
                        z_ref[dz, to_z, columns] = piece


def join(at, mine, came):
    rows, width = mine.shape
    shapes = [out((n, rows // n, 2 * width), BF16) for n in (2, 4)]
    return call(join_kernel, "join", shapes, [], at, mine, came)


def swap(a, axis):
    return lax.ppermute(a, axis, [(0, 1), (1, 0)])


def ring(a, shift):
    return lax.ppermute(a, "z", [(i, (i + shift) % 4) for i in range(4)])


def plane_scatter(a):
    return jnp.sum(lax.all_to_all(a, PLANE, 0, 0, tiled=True), axis=0)


def plane_gather(a):
    same = jnp.broadcast_to(a[None], (SHARDS,) + a.shape)
    return lax.all_to_all(same, PLANE, 0, 0, tiled=True)


def together(*arrays):
    return lax.optimization_barrier(arrays)


def halves(a):
    half = a.shape[0] // 2
    return a[:half], a[half:]


def both_ways(up, down):
    return ring(up, 1), ring(down, -1)


def project_scatter(by_y, by_z, weight):
    wa, wb = weight[:, :CUT], weight[:, CUT:]
    block = by_z.shape[1] // 2
    far_two, by_y, by_z = together(mm(by_y[1, :block], wb), by_y, by_z)
    b_two = swap(far_two, "yl")
    up, down = both_ways(*halves(mm(by_z[2], wa)))
    far_rest, b_two, by_y, by_z = together(mm(by_y[1, block:], wb), b_two, by_y, by_z)
    b_rest = swap(far_rest, "yl")
    b_two = b_two + mm(by_y[0, :block], wb)
    b_up, b_down = both_ways(*halves(b_two))
    one, three = mm(by_z[1], wa), mm(by_z[3], wa)
    one = jnp.concatenate([one[:block] + up, one[block:]], axis=0)
    three = jnp.concatenate([three[:block], three[block:] + down], axis=0)
    a_came = both_ways(one, three)
    b_rest = b_rest + mm(by_y[0, block:], wb)
    half = block // 2
    b_one, b_three = b_rest[block : 2 * block], b_rest[2 * block :]
    b_one = jnp.concatenate([b_one[:half] + b_up, b_one[half:]], axis=0)
    b_three = jnp.concatenate([b_three[:half], b_three[half:] + b_down], axis=0)
    a = mm(by_z[0], wa) + sum(a_came)
    b_came = both_ways(b_one, b_three)
    a_came = swap(a[block:], "yl")
    return jnp.concatenate([a[:block] + a_came, b_rest[:block] + sum(b_came)], axis=1)


def body(keys, queries, values, rates, gate, up, down, out_weight):
    at = jnp.stack([lax.axis_index(name).astype(jnp.int32) for name in ("core", "yl", "z")])
    weights = tuple(pltpu.with_memory_space_constraint(w, pltpu.HBM) for w in (gate, up, down))
    k, d, sent = sort_tokens(at, keys, values, rates.T)
    came = swap(sent, "core")
    partial, rounded = near_grads(at, k, d, *weights)
    queries, partial = together(queries, partial)
    q, q_sent = sort_queries(at, queries)
    summed = far_grads(came, rounded, partial)
    q_sent, summed = together(q_sent, summed)
    total = plane_scatter(summed)
    whole, q_sent = together(plane_gather(total), q_sent)
    q_came = swap(q_sent, "core")
    v = newton(at, whole, *weights)
    o_came = swap(call(far_query_kernel, "far_query", out(q_sent.shape, F32), [], q_came, v), "core")
    o = call(near_query_kernel, "near_query", out(q.shape, BF16), [], q, v)
    by_y, by_z = join(at, o, o_came)
    return project_scatter(by_y, by_z, out_weight).astype(BF16)


def solution(mesh):
    fine = Mesh(mesh.devices.reshape(2, 4, 4, 2, 2), AXES)
    ctx, head = ("x", "yh", "core"), ("yl", "z")
    in_specs = (
        P(ctx, head),
        P(ctx, head),
        P(ctx, head),
        P(ctx, head),
        P(head, None, None),
        P(head, None, None),
        P(head, None, None),
        P(head, None),
    )
    out_specs = P(ctx + head, None)
    return jax.shard_map(body, mesh=fine, in_specs=in_specs, out_specs=out_specs, check_vma=False)
```

```python
import jax
import jax.numpy as jnp
from jax import lax
from jax.experimental import pallas as pl
from jax.experimental.pallas import tpu as pltpu
from jax.sharding import Mesh, PartitionSpec as P

NS_STEPS = 5
ns_a = 3.4445
ns_b = -4.775
ns_c = 2.0315
eps_value = 1e-06

AXES = ("yl", "z", "x", "yh", "core")
PLANE = ("x", "yh")
SHARDS = 8
TILE = 256
VMEM_LIMIT = 24 << 20
CUT = 2304
MIDDLE = 1408
Y_ORDER = (2, 0, 1, 3)
F32 = jnp.float32
BF16 = jnp.bfloat16


def mm(a, b):
    return jnp.dot(a, b, preferred_element_type=F32)


def mm_nt(a, b):
    return lax.dot_general(a, b, (((1,), (1,)), ((), ())), preferred_element_type=F32)


def call(kernel, name, outs, scratch, *operands):
    specs = [pl.BlockSpec(memory_space=pltpu.SMEM if a.dtype == jnp.int32 else pltpu.VMEM) for a in operands]
    return pl.pallas_call(
        kernel,
        out_shape=outs,
        in_specs=specs,
        out_specs=jax.tree.map(lambda _: pl.BlockSpec(memory_space=pltpu.VMEM), outs),
        scratch_shapes=scratch,
        compiler_params=pltpu.CompilerParams(vmem_limit_bytes=VMEM_LIMIT),
        name=name,
    )(*operands)


def out(shape, dtype):
    return jax.ShapeDtypeStruct(shape, dtype)


def sort_tokens_kernel(at_ref, k_ref, v_ref, r_ref, k_o, d_o, sent):
    width = k_o.shape[1]
    for h in range(2):

        @pl.when(at_ref[0] == h)
        def _():
            near, far = slice(h * width, (h + 1) * width), slice((1 - h) * width, (2 - h) * width)
            k_o[...] = k_ref[:, near]
            sent[:, :width] = k_ref[:, far].astype(F32)
            for head, columns in ((h, near), (1 - h, far)):
                rate = r_ref[head : head + 1, :].T
                d = (-rate * v_ref[:, columns].astype(F32)).astype(BF16)
                if head == h:
                    d_o[...] = d
                else:
                    sent[:, width:] = d.astype(F32)


def sort_tokens(at, keys, values, rates):
    shape = (keys.shape[0], keys.shape[1] // 2)
    shapes = [out(shape, BF16), out(shape, BF16), out(keys.shape, F32)]
    return call(sort_tokens_kernel, "sort_tokens", shapes, [], at, keys, values, rates)


def side_by_side(rows, r, block, width):
    top = (r * block) % (rows // 2)
    left = width * ((r * block) // (rows // 2))
    return slice(top, top + block), slice(left, left + width)


def sort_queries_kernel(at_ref, q_ref, q_o, sent):
    rows, width = q_o.shape
    block = rows // 8
    for h in range(2):

        @pl.when(at_ref[0] == h)
        def _():
            near, far = slice(h * width, (h + 1) * width), slice((1 - h) * width, (2 - h) * width)
            for r in range(8):
                row = ((at_ref[1] + r // 4) % 2) * 4 + (at_ref[2] + r % 4) % 4
                source = pl.ds(pl.multiple_of(row * block, block), block)
                q_o[r * block : (r + 1) * block, :] = q_ref[source, near]
                to_rows, to_columns = side_by_side(rows, r, block, width)
                sent[to_rows, to_columns] = q_ref[source, far].astype(F32)


def sort_queries(at, queries):
    rows, columns = queries.shape
    shapes = [out((rows, columns // 2), BF16), out((rows // 2, columns), F32)]
    return call(sort_queries_kernel, "sort_queries", shapes, [], at, queries)


def grads_of(k_ref, d_ref, w_ref, hk_s, dg_s, du_s):
    rows = k_ref.shape[0]
    wg, wu, wd = w_ref[0], w_ref[1], w_ref[2]
    step = 256
    for t in range(0, rows, step):
        at = slice(t, t + step)
        k = k_ref[at, :]
        gate = mm(k, wg)
        upper = mm(k, wu)
        dhid = mm(d_ref[at, :], wd)
        sig = jax.nn.sigmoid(gate)
        act = gate * sig
        hk_s[at, :] = (act * upper).astype(BF16)
        dg_s[at, :] = (dhid * upper * sig * (1.0 + gate * (1.0 - sig))).astype(BF16)
        du_s[at, :] = (dhid * act).astype(BF16)
    kt = k_ref[...].T
    dt = d_ref[...].T
    for m, (left, right) in enumerate(((kt, dg_s), (kt, du_s), (dt, hk_s))):
        yield m, mm(left, right[...])


def near_grads_kernel(at_ref, k_ref, d_ref, g_ref, u_ref, w_ref, o_ref, b_ref, f_s, hk_s, dg_s, du_s, sems):
    copies = [
        pltpu.make_async_copy(ref.at[at_ref[0]], f_s.at[m], sems.at[m]) for m, ref in enumerate((g_ref, u_ref, w_ref))
    ]
    for copy in copies:
        copy.start()
    for m, copy in enumerate(copies):
        copy.wait()
        b_ref[m] = f_s[m].astype(BF16)
    for m, grad in grads_of(k_ref, d_ref, b_ref, hk_s, dg_s, du_s):
        o_ref[m] = grad


def far_grads_kernel(came, b_ref, p_ref, o_ref, k_s, d_s, hk_s, dg_s, du_s):
    part = o_ref.shape[2]
    width = k_s.shape[1]
    k_s[...] = came[:, :width].astype(BF16)
    d_s[...] = came[:, width:].astype(BF16)
    for m, grad in grads_of(k_s, d_s, b_ref, hk_s, dg_s, du_s):
        for j in range(SHARDS):
            rows = slice(j * part, (j + 1) * part)
            o_ref[j, m] = grad[rows, :] + p_ref[m, rows, :]


def near_grads(at, k, d, gate, up, down):
    heads, width, hidden = gate.shape
    vmem, hbm = pl.BlockSpec(memory_space=pltpu.VMEM), pl.BlockSpec(memory_space=pltpu.HBM)
    shape = (3, width, hidden)
    return pl.pallas_call(
        near_grads_kernel,
        out_shape=[out(shape, F32), out(shape, BF16)],
        in_specs=[pl.BlockSpec(memory_space=pltpu.SMEM), vmem, vmem, hbm, hbm, hbm],
        out_specs=[vmem, vmem],
        scratch_shapes=[pltpu.VMEM(shape, F32)]
        + [pltpu.VMEM((k.shape[0], hidden), BF16)] * 3
        + [pltpu.SemaphoreType.DMA((3,))],
        compiler_params=pltpu.CompilerParams(vmem_limit_bytes=VMEM_LIMIT),
        name="near_grads",
    )(at, k, d, gate, up, down)


def far_grads(came, w, partial):
    heads, width, hidden = partial.shape
    rows = came.shape[0]
    scratch = [pltpu.VMEM((rows, width), BF16)] * 2 + [pltpu.VMEM((rows, hidden), BF16)] * 3
    shape = out((SHARDS, 3, width // SHARDS, hidden), F32)
    return call(far_grads_kernel, "far_grads", shape, scratch, came, w, partial)


def split(x):
    high = x.astype(BF16)
    return high, (x - high.astype(F32)).astype(BF16)


def packed(high, low):
    return jnp.concatenate([high, high, low], axis=1)


def mirrored(left, corner):
    at = left.shape[1]
    return jnp.concatenate([left, jnp.concatenate([left[at:].T, corner], axis=0)], axis=1)


def gram_of(xh, xl):
    a, b = packed(xh, xl), jnp.concatenate([xh, xl, xh], axis=1)
    return mirrored(mm_nt(a, b[:TILE]), mm_nt(a[TILE:], b[TILE:]))


def square_of(ah, al):
    a, b = packed(ah, al), jnp.concatenate([ah, al, ah], axis=0)
    return mirrored(mm(a, b[:, :TILE]), mm(a[TILE:], b[:, TILE:]))


def newton_kernel(at_ref, g_ref, wg_ref, wu_ref, wd_ref, v_ref, x_s, f_s, sems):
    copies = [
        pltpu.make_async_copy(ref.at[at_ref[0]], f_s.at[m], sems.at[m])
        for m, ref in enumerate((wg_ref, wu_ref, wd_ref))
    ]
    for copy in copies:
        copy.start()
    matrices, width, hidden = x_s.shape
    every = range(matrices)
    for m in every:
        grad = g_ref[:, m].reshape(width, hidden)
        total = jnp.sum(jnp.sum(grad * grad, axis=1, keepdims=True), axis=0, keepdims=True)
        x_s[m] = grad * lax.rsqrt(total + eps_value)

    def sweep(_, carry):
        xs = [x_s[m] for m in every]
        parts = [split(x) for x in xs]
        grams = [gram_of(*p) for p in parts]
        squares = [square_of(*split(g)) for g in grams]
        mixers = [split(ns_b * g + ns_c * q) for g, q in zip(grams, squares)]
        for m, x, (xh, xl), mixer in zip(every, xs, parts, mixers):
            x_s[m] = ns_a * x + mm(packed(*mixer), jnp.concatenate([xh, xl, xh], axis=0))
        return carry

    lax.fori_loop(0, NS_STEPS, sweep, 0)
    for m, copy in enumerate(copies):
        copy.wait()
        v_ref[m] = (f_s[m] - x_s[m]).astype(BF16)


def newton(at, grads, gate, up, down):
    shape = (grads.shape[1], grads.shape[0] * grads.shape[2], grads.shape[3])
    vmem, hbm = pl.BlockSpec(memory_space=pltpu.VMEM), pl.BlockSpec(memory_space=pltpu.HBM)
    return pl.pallas_call(
        newton_kernel,
        out_shape=out(shape, BF16),
        in_specs=[pl.BlockSpec(memory_space=pltpu.SMEM), vmem, hbm, hbm, hbm],
        out_specs=vmem,
        scratch_shapes=[pltpu.VMEM(shape, F32)] * 2 + [pltpu.SemaphoreType.DMA((3,))],
        compiler_params=pltpu.CompilerParams(vmem_limit_bytes=VMEM_LIMIT),
        name="newton",
    )(at, grads, gate, up, down)


def query_rows(q, v_ref):
    gate = mm(q, v_ref[0])
    hidden = (gate * jax.nn.sigmoid(gate) * mm(q, v_ref[1])).astype(BF16)
    return mm_nt(hidden, v_ref[2]).astype(BF16)


def far_query_kernel(came, v_ref, o_ref):
    width = came.shape[1] // 2
    for left in (0, width):
        columns = slice(left, left + width)
        o_ref[:, columns] = query_rows(came[:, columns].astype(BF16), v_ref).astype(F32)


def near_query_kernel(q_ref, v_ref, o_ref):
    half = q_ref.shape[0] // 2
    for top in (0, half):
        rows = slice(top, top + half)
        o_ref[rows, :] = query_rows(q_ref[rows, :], v_ref)


def join_kernel(at_ref, o_ref, came, y_ref, z_ref):
    rows, width = o_ref.shape
    block = rows // 8
    for h in range(2):

        @pl.when(at_ref[0] == h)
        def _():
            near, far = slice(h * width, (h + 1) * width), slice((1 - h) * width, (2 - h) * width)
            for dy in range(2):
                for dz in range(4):
                    r = dy * 4 + dz
                    to_y, to_z = pl.ds(Y_ORDER.index(dz) * block, block), pl.ds(dy * block, block)
                    mine = o_ref[r * block : (r + 1) * block, :]
                    other = came[side_by_side(rows, r, block, width)].astype(BF16)
                    for columns, piece in ((near, mine), (far, other)):
                        y_ref[dy, to_y, columns] = piece
                        z_ref[dz, to_z, columns] = piece


def join(at, mine, came):
    rows, width = mine.shape
    shapes = [out((n, rows // n, 2 * width), BF16) for n in (2, 4)]
    return call(join_kernel, "join", shapes, [], at, mine, came)


def swap(a, axis):
    return lax.ppermute(a, axis, [(0, 1), (1, 0)])


def ring(a, shift):
    return lax.ppermute(a, "z", [(i, (i + shift) % 4) for i in range(4)])


def plane_scatter(a):
    return jnp.sum(lax.all_to_all(a, PLANE, 0, 0, tiled=True), axis=0)


def plane_gather(a):
    same = jnp.broadcast_to(a[None], (SHARDS,) + a.shape)
    return lax.all_to_all(same, PLANE, 0, 0, tiled=True)


def together(*arrays):
    return lax.optimization_barrier(arrays)


def halves(a):
    half = a.shape[0] // 2
    return a[:half], a[half:]


def both_ways(up, down):
    return ring(up, 1), ring(down, -1)


def project_scatter(by_y, by_z, weight):
    wb, wa = weight[:, :CUT], weight[:, CUT:]
    block = by_z.shape[1] // 2
    far_two, by_y, by_z = together(mm(by_y[1, :block], wb), by_y, by_z)
    b_two = swap(far_two, "yl")
    up, down = both_ways(*halves(mm(by_z[2], wa)))
    far_rest, b_two, by_y, by_z = together(mm(by_y[1, block:], wb), b_two, by_y, by_z)
    b_rest = swap(far_rest, "yl")
    b_two = b_two + mm(by_y[0, :block], wb)
    b_up, b_down = both_ways(*halves(b_two))
    one, three = mm(by_z[1], wa), mm(by_z[3], wa)
    one = jnp.concatenate([one[:block] + up, one[block:]], axis=0)
    three = jnp.concatenate([three[:block], three[block:] + down], axis=0)
    a_came = both_ways(one[:, :MIDDLE], three[:, :MIDDLE])
    later, b_up, b_down = together((one[:, MIDDLE:], three[:, MIDDLE:]), b_up, b_down)
    a_more = both_ways(*later)
    a = mm(by_z[0], wa[:, :MIDDLE]) + sum(a_came)
    b_rest = b_rest + mm(by_y[0, block:], wb)
    half = block // 2
    b_one, b_three = b_rest[block : 2 * block], b_rest[2 * block :]
    b_one = jnp.concatenate([b_one[:half] + b_up, b_one[half:]], axis=0)
    b_three = jnp.concatenate([b_three[:half], b_three[half:] + b_down], axis=0)
    a, b_one, b_three, by_z = together(a, b_one, b_three, by_z)
    a_came = swap(a[block:], "yl")
    b_came = both_ways(b_one, b_three)
    more = mm(by_z[0], wa[:, MIDDLE:]) + sum(a_more)
    more_came = swap(more[block:], "yl")
    return jnp.concatenate(
        [b_rest[:block] + sum(b_came), a[:block] + a_came, more[:block] + more_came], axis=1
    )


def body(keys, queries, values, rates, gate, up, down, out_weight):
    at = jnp.stack([lax.axis_index(name).astype(jnp.int32) for name in ("core", "yl", "z")])
    weights = tuple(pltpu.with_memory_space_constraint(w, pltpu.HBM) for w in (gate, up, down))
    k, d, sent = sort_tokens(at, keys, values, rates.T)
    came = swap(sent, "core")
    partial, rounded = near_grads(at, k, d, *weights)
    queries, partial = together(queries, partial)
    q, q_sent = sort_queries(at, queries)
    summed = far_grads(came, rounded, partial)
    q_sent, summed = together(q_sent, summed)
    total = plane_scatter(summed)
    whole, q_sent = together(plane_gather(total), q_sent)
    q_came = swap(q_sent, "core")
    v = newton(at, whole, *weights)
    o_came = swap(call(far_query_kernel, "far_query", out(q_sent.shape, F32), [], q_came, v), "core")
    o = call(near_query_kernel, "near_query", out(q.shape, BF16), [], q, v)
    by_y, by_z = join(at, o, o_came)
    return project_scatter(by_y, by_z, out_weight).astype(BF16)


def solution(mesh):
    fine = Mesh(mesh.devices.reshape(2, 4, 4, 2, 2), AXES)
    ctx, head = ("x", "yh", "core"), ("yl", "z")
    in_specs = (
        P(ctx, head),
        P(ctx, head),
        P(ctx, head),
        P(ctx, head),
        P(head, None, None),
        P(head, None, None),
        P(head, None, None),
        P(head, None),
    )
    out_specs = P(ctx + head, None)
    return jax.shard_map(body, mesh=fine, in_specs=in_specs, out_specs=out_specs, check_vma=False)
```

```python
import jax
import jax.numpy as jnp
from jax import lax
from jax.experimental import pallas as pl
from jax.experimental.pallas import tpu as pltpu
from jax.sharding import Mesh, PartitionSpec as P

NS_STEPS = 5
ns_a = 3.4445
ns_b = -4.775
ns_c = 2.0315
eps_value = 1e-06

AXES = ("yl", "z", "x", "yh", "core")
PLANE = ("x", "yh")
SHARDS = 8
TILE = 256
VMEM_LIMIT = 24 << 20
CUT = 2304
MIDDLE = 1920
Y_ORDER = (2, 0, 1, 3)
F32 = jnp.float32
BF16 = jnp.bfloat16


def mm(a, b):
    return jnp.dot(a, b, preferred_element_type=F32)


def mm_nt(a, b):
    return lax.dot_general(a, b, (((1,), (1,)), ((), ())), preferred_element_type=F32)


def call(kernel, name, outs, scratch, *operands):
    specs = [pl.BlockSpec(memory_space=pltpu.SMEM if a.dtype == jnp.int32 else pltpu.VMEM) for a in operands]
    return pl.pallas_call(
        kernel,
        out_shape=outs,
        in_specs=specs,
        out_specs=jax.tree.map(lambda _: pl.BlockSpec(memory_space=pltpu.VMEM), outs),
        scratch_shapes=scratch,
        compiler_params=pltpu.CompilerParams(vmem_limit_bytes=VMEM_LIMIT),
        name=name,
    )(*operands)


def in_hbm(a):
    return pltpu.with_memory_space_constraint(a, pltpu.HBM)


def out(shape, dtype):
    return jax.ShapeDtypeStruct(shape, dtype)


def sort_tokens_kernel(at_ref, r_ref, k_ref, v_ref, k_o, d_o, sent, k_s, v_s, sems):
    rows, width = k_o.shape
    half = rows // 2
    copies = [
        pltpu.make_async_copy(ref.at[pl.ds(i * half, half)], to.at[pl.ds(i * half, half)], sems.at[2 * n + i])
        for n, (ref, to) in enumerate(((k_ref, k_s), (v_ref, v_s)))
        for i in range(2)
    ]
    for copy in copies:
        copy.start()
    for copy in copies:
        copy.wait()
    for h in range(2):

        @pl.when(at_ref[0] == h)
        def _():
            near, far = slice(h * width, (h + 1) * width), slice((1 - h) * width, (2 - h) * width)
            k_o[...] = k_s[:, near]
            sent[:, :width] = k_s[:, far].astype(F32)
            for head, columns in ((h, near), (1 - h, far)):
                rate = r_ref[head : head + 1, :].T
                d = (-rate * v_s[:, columns].astype(F32)).astype(BF16)
                if head == h:
                    d_o[...] = d
                else:
                    sent[:, width:] = d.astype(F32)


def sort_tokens(at, keys, values, rates):
    shape = (keys.shape[0], keys.shape[1] // 2)
    vmem, hbm = pl.BlockSpec(memory_space=pltpu.VMEM), pl.BlockSpec(memory_space=pltpu.HBM)
    return pl.pallas_call(
        sort_tokens_kernel,
        out_shape=[out(shape, BF16), out(shape, BF16), out(keys.shape, F32)],
        in_specs=[pl.BlockSpec(memory_space=pltpu.SMEM), vmem, hbm, hbm],
        out_specs=[vmem] * 3,
        scratch_shapes=[pltpu.VMEM(keys.shape, BF16)] * 2 + [pltpu.SemaphoreType.DMA((4,))],
        compiler_params=pltpu.CompilerParams(vmem_limit_bytes=VMEM_LIMIT),
        name="sort_tokens",
    )(at, rates, in_hbm(keys), in_hbm(values))


def side_by_side(rows, r, block, width):
    top = (r * block) % (rows // 2)
    left = width * ((r * block) // (rows // 2))
    return slice(top, top + block), slice(left, left + width)


def sort_queries_kernel(at_ref, q_ref, q_o, sent):
    rows, width = q_o.shape
    block = rows // 8
    for h in range(2):

        @pl.when(at_ref[0] == h)
        def _():
            near, far = slice(h * width, (h + 1) * width), slice((1 - h) * width, (2 - h) * width)
            for r in range(8):
                row = ((at_ref[1] + r // 4) % 2) * 4 + (at_ref[2] + r % 4) % 4
                source = pl.ds(pl.multiple_of(row * block, block), block)
                q_o[r * block : (r + 1) * block, :] = q_ref[source, near]
                to_rows, to_columns = side_by_side(rows, r, block, width)
                sent[to_rows, to_columns] = q_ref[source, far].astype(F32)


def sort_queries(at, queries):
    rows, columns = queries.shape
    shapes = [out((rows, columns // 2), BF16), out((rows // 2, columns), F32)]
    return call(sort_queries_kernel, "sort_queries", shapes, [], at, queries)


def grads_of(k_ref, d_ref, w_ref, hk_s, dg_s, du_s):
    rows = k_ref.shape[0]
    wg, wu, wd = w_ref[0], w_ref[1], w_ref[2]
    step = 256
    for t in range(0, rows, step):
        at = slice(t, t + step)
        k = k_ref[at, :]
        gate = mm(k, wg)
        upper = mm(k, wu)
        dhid = mm(d_ref[at, :], wd)
        sig = jax.nn.sigmoid(gate)
        act = gate * sig
        hk_s[at, :] = (act * upper).astype(BF16)
        dg_s[at, :] = (dhid * upper * sig * (1.0 + gate * (1.0 - sig))).astype(BF16)
        du_s[at, :] = (dhid * act).astype(BF16)
    kt = k_ref[...].T
    dt = d_ref[...].T
    for m, (left, right) in enumerate(((kt, dg_s), (kt, du_s), (dt, hk_s))):
        yield m, mm(left, right[...])


def near_grads_kernel(at_ref, k_ref, d_ref, g_ref, u_ref, w_ref, o_ref, b_ref, f_s, hk_s, dg_s, du_s, sems):
    copies = [
        pltpu.make_async_copy(ref.at[at_ref[0]], f_s.at[m], sems.at[m]) for m, ref in enumerate((g_ref, u_ref, w_ref))
    ]
    for copy in copies:
        copy.start()
    for m, copy in enumerate(copies):
        copy.wait()
        b_ref[m] = f_s[m].astype(BF16)
    for m, grad in grads_of(k_ref, d_ref, b_ref, hk_s, dg_s, du_s):
        o_ref[m] = grad


def far_grads_kernel(came, b_ref, p_ref, o_ref, k_s, d_s, hk_s, dg_s, du_s):
    part = o_ref.shape[2]
    width = k_s.shape[1]
    k_s[...] = came[:, :width].astype(BF16)
    d_s[...] = came[:, width:].astype(BF16)
    for m, grad in grads_of(k_s, d_s, b_ref, hk_s, dg_s, du_s):
        for j in range(SHARDS):
            rows = slice(j * part, (j + 1) * part)
            o_ref[j, m] = grad[rows, :] + p_ref[m, rows, :]


def near_grads(at, k, d, gate, up, down):
    heads, width, hidden = gate.shape
    vmem, hbm = pl.BlockSpec(memory_space=pltpu.VMEM), pl.BlockSpec(memory_space=pltpu.HBM)
    shape = (3, width, hidden)
    return pl.pallas_call(
        near_grads_kernel,
        out_shape=[out(shape, F32), out(shape, BF16)],
        in_specs=[pl.BlockSpec(memory_space=pltpu.SMEM), vmem, vmem, hbm, hbm, hbm],
        out_specs=[vmem, vmem],
        scratch_shapes=[pltpu.VMEM(shape, F32)]
        + [pltpu.VMEM((k.shape[0], hidden), BF16)] * 3
        + [pltpu.SemaphoreType.DMA((3,))],
        compiler_params=pltpu.CompilerParams(vmem_limit_bytes=VMEM_LIMIT),
        name="near_grads",
    )(at, k, d, gate, up, down)


def far_grads(came, w, partial):
    heads, width, hidden = partial.shape
    rows = came.shape[0]
    scratch = [pltpu.VMEM((rows, width), BF16)] * 2 + [pltpu.VMEM((rows, hidden), BF16)] * 3
    shape = out((SHARDS, 3, width // SHARDS, hidden), F32)
    return call(far_grads_kernel, "far_grads", shape, scratch, came, w, partial)


def split(x):
    high = x.astype(BF16)
    return high, (x - high.astype(F32)).astype(BF16)


def packed(high, low):
    return jnp.concatenate([high, high, low], axis=1)


def mirrored(left, corner):
    at = left.shape[1]
    return jnp.concatenate([left, jnp.concatenate([left[at:].T, corner], axis=0)], axis=1)


def gram_of(xh, xl):
    a, b = packed(xh, xl), jnp.concatenate([xh, xl, xh], axis=1)
    return mirrored(mm_nt(a, b[:TILE]), mm_nt(a[TILE:], b[TILE:]))


def square_of(ah, al):
    a, b = packed(ah, al), jnp.concatenate([ah, al, ah], axis=0)
    return mirrored(mm(a, b[:, :TILE]), mm(a[TILE:], b[:, TILE:]))


def newton_kernel(at_ref, g_ref, wg_ref, wu_ref, wd_ref, v_ref, x_s, f_s, sems):
    copies = [
        pltpu.make_async_copy(ref.at[at_ref[0]], f_s.at[m], sems.at[m])
        for m, ref in enumerate((wg_ref, wu_ref, wd_ref))
    ]
    for copy in copies:
        copy.start()
    matrices, width, hidden = x_s.shape
    every = range(matrices)
    for m in every:
        grad = g_ref[:, m].reshape(width, hidden)
        total = jnp.sum(jnp.sum(grad * grad, axis=1, keepdims=True), axis=0, keepdims=True)
        x_s[m] = grad * lax.rsqrt(total + eps_value)

    def sweep(_, carry):
        xs = [x_s[m] for m in every]
        parts = [split(x) for x in xs]
        grams = [gram_of(*p) for p in parts]
        squares = [square_of(*split(g)) for g in grams]
        mixers = [split(ns_b * g + ns_c * q) for g, q in zip(grams, squares)]
        for m, x, (xh, xl), mixer in zip(every, xs, parts, mixers):
            x_s[m] = ns_a * x + mm(packed(*mixer), jnp.concatenate([xh, xl, xh], axis=0))
        return carry

    lax.fori_loop(0, NS_STEPS, sweep, 0)
    for m, copy in enumerate(copies):
        copy.wait()
        v_ref[m] = (f_s[m] - x_s[m]).astype(BF16)


def newton(at, grads, gate, up, down):
    shape = (grads.shape[1], grads.shape[0] * grads.shape[2], grads.shape[3])
    vmem, hbm = pl.BlockSpec(memory_space=pltpu.VMEM), pl.BlockSpec(memory_space=pltpu.HBM)
    return pl.pallas_call(
        newton_kernel,
        out_shape=out(shape, BF16),
        in_specs=[pl.BlockSpec(memory_space=pltpu.SMEM), vmem, hbm, hbm, hbm],
        out_specs=vmem,
        scratch_shapes=[pltpu.VMEM(shape, F32)] * 2 + [pltpu.SemaphoreType.DMA((3,))],
        compiler_params=pltpu.CompilerParams(vmem_limit_bytes=VMEM_LIMIT),
        name="newton",
    )(at, grads, gate, up, down)


def query_rows(q, v_ref):
    gate = mm(q, v_ref[0])
    hidden = (gate * jax.nn.sigmoid(gate) * mm(q, v_ref[1])).astype(BF16)
    return mm_nt(hidden, v_ref[2]).astype(BF16)


def far_query_kernel(came, v_ref, o_ref):
    width = came.shape[1] // 2
    for left in (0, width):
        columns = slice(left, left + width)
        o_ref[:, columns] = query_rows(came[:, columns].astype(BF16), v_ref).astype(F32)


def near_query_kernel(q_ref, v_ref, o_ref):
    half = q_ref.shape[0] // 2
    for top in (0, half):
        rows = slice(top, top + half)
        o_ref[rows, :] = query_rows(q_ref[rows, :], v_ref)


def join_kernel(at_ref, o_ref, came, y_ref, z_ref):
    rows, width = o_ref.shape
    block = rows // 8
    for h in range(2):

        @pl.when(at_ref[0] == h)
        def _():
            near, far = slice(h * width, (h + 1) * width), slice((1 - h) * width, (2 - h) * width)
            for dy in range(2):
                for dz in range(4):
                    r = dy * 4 + dz
                    to_y, to_z = pl.ds(Y_ORDER.index(dz) * block, block), pl.ds(dy * block, block)
                    mine = o_ref[r * block : (r + 1) * block, :]
                    other = came[side_by_side(rows, r, block, width)].astype(BF16)
                    for columns, piece in ((near, mine), (far, other)):
                        y_ref[dy, to_y, columns] = piece
                        z_ref[dz, to_z, columns] = piece


def join(at, mine, came):
    rows, width = mine.shape
    shapes = [out((n, rows // n, 2 * width), BF16) for n in (2, 4)]
    return call(join_kernel, "join", shapes, [], at, mine, came)


def swap(a, axis):
    return lax.ppermute(a, axis, [(0, 1), (1, 0)])


def ring(a, shift):
    return lax.ppermute(a, "z", [(i, (i + shift) % 4) for i in range(4)])


def plane_scatter(a):
    return jnp.sum(lax.all_to_all(a, PLANE, 0, 0, tiled=True), axis=0)


def plane_gather(a):
    same = jnp.broadcast_to(a[None], (SHARDS,) + a.shape)
    return lax.all_to_all(same, PLANE, 0, 0, tiled=True)


def together(*arrays):
    return lax.optimization_barrier(arrays)


def halves(a):
    half = a.shape[0] // 2
    return a[:half], a[half:]


def both_ways(up, down):
    return ring(up, 1), ring(down, -1)


def project_scatter(by_y, by_z, weight):
    wb, wa = weight[:, :CUT], weight[:, CUT:]
    block = by_z.shape[1] // 2
    far_two, by_y, by_z = together(mm(by_y[1, :block], wb), by_y, by_z)
    b_two = swap(far_two, "yl")
    up, down = both_ways(*halves(mm(by_z[2], wa)))
    far_rest, b_two, by_y, by_z = together(mm(by_y[1, block:], wb), b_two, by_y, by_z)
    b_rest = swap(far_rest, "yl")
    b_two = b_two + mm(by_y[0, :block], wb)
    b_up, b_down = both_ways(*halves(b_two))
    one, three = mm(by_z[1], wa), mm(by_z[3], wa)
    one = jnp.concatenate([one[:block] + up, one[block:]], axis=0)
    three = jnp.concatenate([three[:block], three[block:] + down], axis=0)
    a_came = both_ways(one[:, :MIDDLE], three[:, :MIDDLE])
    later, b_up, b_down = together((one[:, MIDDLE:], three[:, MIDDLE:]), b_up, b_down)
    a_more = both_ways(*later)
    a = mm(by_z[0], wa[:, :MIDDLE]) + sum(a_came)
    b_rest = b_rest + mm(by_y[0, block:], wb)
    half = block // 2
    b_one, b_three = b_rest[block : 2 * block], b_rest[2 * block :]
    b_one = jnp.concatenate([b_one[:half] + b_up, b_one[half:]], axis=0)
    b_three = jnp.concatenate([b_three[:half], b_three[half:] + b_down], axis=0)
    a, b_one, b_three, by_z = together(a, b_one, b_three, by_z)
    a_came = swap(a[block:], "yl")
    b_came = both_ways(b_one, b_three)
    more = mm(by_z[0], wa[:, MIDDLE:]) + sum(a_more)
    more_came = swap(more[block:], "yl")
    return jnp.concatenate(
        [b_rest[:block] + sum(b_came), a[:block] + a_came, more[:block] + more_came], axis=1
    )


def body(keys, queries, values, rates, gate, up, down, out_weight):
    at = jnp.stack([lax.axis_index(name).astype(jnp.int32) for name in ("core", "yl", "z")])
    weights = tuple(in_hbm(w) for w in (gate, up, down))
    k, d, sent = sort_tokens(at, keys, values, rates.T)
    came = swap(sent, "core")
    partial, rounded = near_grads(at, k, d, *weights)
    queries, partial = together(queries, partial)
    q, q_sent = sort_queries(at, queries)
    summed = far_grads(came, rounded, partial)
    q_sent, summed = together(q_sent, summed)
    total = plane_scatter(summed)
    whole, q_sent = together(plane_gather(total), q_sent)
    q_came = swap(q_sent, "core")
    v = newton(at, whole, *weights)
    o_came = swap(call(far_query_kernel, "far_query", out(q_sent.shape, F32), [], q_came, v), "core")
    o = call(near_query_kernel, "near_query", out(q.shape, BF16), [], q, v)
    by_y, by_z = join(at, o, o_came)
    return project_scatter(by_y, by_z, out_weight).astype(BF16)


def solution(mesh):
    fine = Mesh(mesh.devices.reshape(2, 4, 4, 2, 2), AXES)
    ctx, head = ("x", "yh", "core"), ("yl", "z")
    in_specs = (
        P(ctx, head),
        P(ctx, head),
        P(ctx, head),
        P(ctx, head),
        P(head, None, None),
        P(head, None, None),
        P(head, None, None),
        P(head, None),
    )
    out_specs = P(ctx + head, None)
    return jax.shard_map(body, mesh=fine, in_specs=in_specs, out_specs=out_specs, check_vma=False)
```

```python
import jax
import jax.numpy as jnp
from jax import lax
from jax.experimental import pallas as pl
from jax.experimental.pallas import tpu as pltpu
from jax.sharding import Mesh, PartitionSpec as P

NS_STEPS = 5
ns_a = 3.4445
ns_b = -4.775
ns_c = 2.0315
eps_value = 1e-06

AXES = ("yl", "z", "x", "yh", "core")
PLANE = ("x", "yh")
SHARDS = 8
TILE = 256
VMEM_LIMIT = 24 << 20
CUT = 2304
MIDDLE = 1408
Y_ORDER = (2, 0, 1, 3)
F32 = jnp.float32
BF16 = jnp.bfloat16


def mm(a, b):
    return jnp.dot(a, b, preferred_element_type=F32)


def mm_nt(a, b):
    return lax.dot_general(a, b, (((1,), (1,)), ((), ())), preferred_element_type=F32)


def call(kernel, name, outs, scratch, *operands):
    specs = [pl.BlockSpec(memory_space=pltpu.SMEM if a.dtype == jnp.int32 else pltpu.VMEM) for a in operands]
    return pl.pallas_call(
        kernel,
        out_shape=outs,
        in_specs=specs,
        out_specs=jax.tree.map(lambda _: pl.BlockSpec(memory_space=pltpu.VMEM), outs),
        scratch_shapes=scratch,
        compiler_params=pltpu.CompilerParams(vmem_limit_bytes=VMEM_LIMIT),
        name=name,
    )(*operands)


def in_hbm(a):
    return pltpu.with_memory_space_constraint(a, pltpu.HBM)


def out(shape, dtype):
    return jax.ShapeDtypeStruct(shape, dtype)


def sort_tokens_kernel(at_ref, r_ref, k_ref, v_ref, k_o, d_o, sent, k_s, v_s, sems):
    rows, width = k_o.shape
    half = rows // 2
    copies = [
        pltpu.make_async_copy(ref.at[pl.ds(i * half, half)], to.at[pl.ds(i * half, half)], sems.at[2 * n + i])
        for n, (ref, to) in enumerate(((k_ref, k_s), (v_ref, v_s)))
        for i in range(2)
    ]
    for copy in copies:
        copy.start()
    for copy in copies:
        copy.wait()
    for h in range(2):

        @pl.when(at_ref[0] == h)
        def _():
            near, far = slice(h * width, (h + 1) * width), slice((1 - h) * width, (2 - h) * width)
            k_o[...] = k_s[:, near]
            sent[:, :width] = k_s[:, far].astype(F32)
            for head, columns in ((h, near), (1 - h, far)):
                rate = r_ref[head : head + 1, :].T
                d = (-rate * v_s[:, columns].astype(F32)).astype(BF16)
                if head == h:
                    d_o[...] = d
                else:
                    sent[:, width:] = d.astype(F32)


def sort_tokens(at, keys, values, rates):
    shape = (keys.shape[0], keys.shape[1] // 2)
    vmem, hbm = pl.BlockSpec(memory_space=pltpu.VMEM), pl.BlockSpec(memory_space=pltpu.HBM)
    return pl.pallas_call(
        sort_tokens_kernel,
        out_shape=[out(shape, BF16), out(shape, BF16), out(keys.shape, F32)],
        in_specs=[pl.BlockSpec(memory_space=pltpu.SMEM), vmem, hbm, hbm],
        out_specs=[vmem] * 3,
        scratch_shapes=[pltpu.VMEM(keys.shape, BF16)] * 2 + [pltpu.SemaphoreType.DMA((4,))],
        compiler_params=pltpu.CompilerParams(vmem_limit_bytes=VMEM_LIMIT),
        name="sort_tokens",
    )(at, rates, in_hbm(keys), in_hbm(values))


def side_by_side(rows, r, block, width):
    top = (r * block) % (rows // 2)
    left = width * ((r * block) // (rows // 2))
    return slice(top, top + block), slice(left, left + width)


def sort_queries_kernel(at_ref, q_ref, q_o, sent):
    rows, width = q_o.shape
    block = rows // 8
    for h in range(2):

        @pl.when(at_ref[0] == h)
        def _():
            near, far = slice(h * width, (h + 1) * width), slice((1 - h) * width, (2 - h) * width)
            for r in range(8):
                row = ((at_ref[1] + r // 4) % 2) * 4 + (at_ref[2] + r % 4) % 4
                source = pl.ds(pl.multiple_of(row * block, block), block)
                q_o[r * block : (r + 1) * block, :] = q_ref[source, near]
                to_rows, to_columns = side_by_side(rows, r, block, width)
                sent[to_rows, to_columns] = q_ref[source, far].astype(F32)


def sort_queries(at, queries):
    rows, columns = queries.shape
    shapes = [out((rows, columns // 2), BF16), out((rows // 2, columns), F32)]
    return call(sort_queries_kernel, "sort_queries", shapes, [], at, queries)


def grads_of(k_ref, d_ref, w_ref, hk_s, dg_s, du_s):
    rows = k_ref.shape[0]
    wg, wu, wd = w_ref[0], w_ref[1], w_ref[2]
    step = 256
    for t in range(0, rows, step):
        at = slice(t, t + step)
        k = k_ref[at, :]
        gate = mm(k, wg)
        upper = mm(k, wu)
        dhid = mm(d_ref[at, :], wd)
        sig = jax.nn.sigmoid(gate)
        act = gate * sig
        hk_s[at, :] = (act * upper).astype(BF16)
        dg_s[at, :] = (dhid * upper * sig * (1.0 + gate * (1.0 - sig))).astype(BF16)
        du_s[at, :] = (dhid * act).astype(BF16)
    kt = k_ref[...].T
    dt = d_ref[...].T
    for m, (left, right) in enumerate(((kt, dg_s), (kt, du_s), (dt, hk_s))):
        yield m, mm(left, right[...])


def near_grads_kernel(at_ref, k_ref, d_ref, g_ref, u_ref, w_ref, o_ref, b_ref, f_s, hk_s, dg_s, du_s, sems):
    copies = [
        pltpu.make_async_copy(ref.at[at_ref[0]], f_s.at[m], sems.at[m]) for m, ref in enumerate((g_ref, u_ref, w_ref))
    ]
    for copy in copies:
        copy.start()
    for m, copy in enumerate(copies):
        copy.wait()
        b_ref[m] = f_s[m].astype(BF16)
    for m, grad in grads_of(k_ref, d_ref, b_ref, hk_s, dg_s, du_s):
        o_ref[m] = grad


def far_grads_kernel(came, b_ref, p_ref, o_ref, k_s, d_s, hk_s, dg_s, du_s):
    part = o_ref.shape[2]
    width = k_s.shape[1]
    k_s[...] = came[:, :width].astype(BF16)
    d_s[...] = came[:, width:].astype(BF16)
    for m, grad in grads_of(k_s, d_s, b_ref, hk_s, dg_s, du_s):
        for j in range(SHARDS):
            rows = slice(j * part, (j + 1) * part)
            o_ref[j, m] = grad[rows, :] + p_ref[m, rows, :]


def near_grads(at, k, d, gate, up, down):
    heads, width, hidden = gate.shape
    vmem, hbm = pl.BlockSpec(memory_space=pltpu.VMEM), pl.BlockSpec(memory_space=pltpu.HBM)
    shape = (3, width, hidden)
    return pl.pallas_call(
        near_grads_kernel,
        out_shape=[out(shape, F32), out(shape, BF16)],
        in_specs=[pl.BlockSpec(memory_space=pltpu.SMEM), vmem, vmem, hbm, hbm, hbm],
        out_specs=[vmem, vmem],
        scratch_shapes=[pltpu.VMEM(shape, F32)]
        + [pltpu.VMEM((k.shape[0], hidden), BF16)] * 3
        + [pltpu.SemaphoreType.DMA((3,))],
        compiler_params=pltpu.CompilerParams(vmem_limit_bytes=VMEM_LIMIT),
        name="near_grads",
    )(at, k, d, gate, up, down)


def far_grads(came, w, partial):
    heads, width, hidden = partial.shape
    rows = came.shape[0]
    scratch = [pltpu.VMEM((rows, width), BF16)] * 2 + [pltpu.VMEM((rows, hidden), BF16)] * 3
    shape = out((SHARDS, 3, width // SHARDS, hidden), F32)
    return call(far_grads_kernel, "far_grads", shape, scratch, came, w, partial)


def split(x):
    high = x.astype(BF16)
    return high, (x - high.astype(F32)).astype(BF16)


def packed(high, low):
    return jnp.concatenate([high, high, low], axis=1)


def mirrored(left, corner):
    at = left.shape[1]
    return jnp.concatenate([left, jnp.concatenate([left[at:].T, corner], axis=0)], axis=1)


def gram_of(xh, xl):
    a, b = packed(xh, xl), jnp.concatenate([xh, xl, xh], axis=1)
    return mirrored(mm_nt(a, b[:TILE]), mm_nt(a[TILE:], b[TILE:]))


def square_of(ah, al):
    a, b = packed(ah, al), jnp.concatenate([ah, al, ah], axis=0)
    return mirrored(mm(a, b[:, :TILE]), mm(a[TILE:], b[:, TILE:]))


def newton_kernel(at_ref, g_ref, wg_ref, wu_ref, wd_ref, v_ref, x_s, f_s, sems):
    copies = [
        pltpu.make_async_copy(ref.at[at_ref[0]], f_s.at[m], sems.at[m])
        for m, ref in enumerate((wg_ref, wu_ref, wd_ref))
    ]
    for copy in copies:
        copy.start()
    matrices, width, hidden = x_s.shape
    every = range(matrices)
    for m in every:
        grad = g_ref[:, m].reshape(width, hidden)
        total = jnp.sum(jnp.sum(grad * grad, axis=1, keepdims=True), axis=0, keepdims=True)
        x_s[m] = grad * lax.rsqrt(total + eps_value)

    def sweep(_, carry):
        xs = [x_s[m] for m in every]
        parts = [split(x) for x in xs]
        grams = [gram_of(*p) for p in parts]
        squares = [square_of(*split(g)) for g in grams]
        mixers = [split(ns_b * g + ns_c * q) for g, q in zip(grams, squares)]
        for m, x, (xh, xl), mixer in zip(every, xs, parts, mixers):
            x_s[m] = ns_a * x + mm(packed(*mixer), jnp.concatenate([xh, xl, xh], axis=0))
        return carry

    lax.fori_loop(0, NS_STEPS, sweep, 0)
    for m, copy in enumerate(copies):
        copy.wait()
        v_ref[m] = (f_s[m] - x_s[m]).astype(BF16)


def newton(at, grads, gate, up, down):
    shape = (grads.shape[1], grads.shape[0] * grads.shape[2], grads.shape[3])
    vmem, hbm = pl.BlockSpec(memory_space=pltpu.VMEM), pl.BlockSpec(memory_space=pltpu.HBM)
    return pl.pallas_call(
        newton_kernel,
        out_shape=out(shape, BF16),
        in_specs=[pl.BlockSpec(memory_space=pltpu.SMEM), vmem, hbm, hbm, hbm],
        out_specs=vmem,
        scratch_shapes=[pltpu.VMEM(shape, F32)] * 2 + [pltpu.SemaphoreType.DMA((3,))],
        compiler_params=pltpu.CompilerParams(vmem_limit_bytes=VMEM_LIMIT),
        name="newton",
    )(at, grads, gate, up, down)


def query_rows(q, v_ref):
    gate = mm(q, v_ref[0])
    hidden = (gate * jax.nn.sigmoid(gate) * mm(q, v_ref[1])).astype(BF16)
    return mm_nt(hidden, v_ref[2]).astype(BF16)


def far_query_kernel(came, v_ref, o_ref):
    width = came.shape[1] // 2
    for left in (0, width):
        columns = slice(left, left + width)
        o_ref[:, columns] = query_rows(came[:, columns].astype(BF16), v_ref).astype(F32)


def near_query_kernel(q_ref, v_ref, o_ref):
    half = q_ref.shape[0] // 2
    for top in (0, half):
        rows = slice(top, top + half)
        o_ref[rows, :] = query_rows(q_ref[rows, :], v_ref)


def join_kernel(at_ref, o_ref, came, y_ref, z_ref):
    rows, width = o_ref.shape
    block = rows // 8
    for h in range(2):

        @pl.when(at_ref[0] == h)
        def _():
            near, far = slice(h * width, (h + 1) * width), slice((1 - h) * width, (2 - h) * width)
            for dy in range(2):
                for dz in range(4):
                    r = dy * 4 + dz
                    to_y, to_z = pl.ds(Y_ORDER.index(dz) * block, block), pl.ds(dy * block, block)
                    mine = o_ref[r * block : (r + 1) * block, :]
                    other = came[side_by_side(rows, r, block, width)].astype(BF16)
                    for columns, piece in ((near, mine), (far, other)):
                        y_ref[dy, to_y, columns] = piece
                        z_ref[dz, to_z, columns] = piece


def join(at, mine, came):
    rows, width = mine.shape
    shapes = [out((n, rows // n, 2 * width), BF16) for n in (2, 4)]
    return call(join_kernel, "join", shapes, [], at, mine, came)


def swap(a, axis):
    return lax.ppermute(a, axis, [(0, 1), (1, 0)])


def ring(a, shift):
    return lax.ppermute(a, "z", [(i, (i + shift) % 4) for i in range(4)])


def sum_kernel(a_ref, o_ref):
    total = a_ref[0]
    for j in range(1, SHARDS):
        total = total + a_ref[j]
    for j in range(SHARDS):
        o_ref[j] = total


def plane_sum(a):
    came = lax.all_to_all(a, PLANE, 0, 0, tiled=True)
    same = call(sum_kernel, "sum_parts", out(a.shape, a.dtype), [], came)
    return lax.all_to_all(same, PLANE, 0, 0, tiled=True)


def together(*arrays):
    return lax.optimization_barrier(arrays)


def halves(a):
    half = a.shape[0] // 2
    return a[:half], a[half:]


def both_ways(up, down):
    return ring(up, 1), ring(down, -1)


def project_scatter(by_y, by_z, weight):
    wb, wa = weight[:, :CUT], weight[:, CUT:]
    block = by_z.shape[1] // 2
    far_two, by_y, by_z = together(mm(by_y[1, :block], wb), by_y, by_z)
    b_two = swap(far_two, "yl")
    up, down = both_ways(*halves(mm(by_z[2], wa)))
    far_rest, b_two, by_y, by_z = together(mm(by_y[1, block:], wb), b_two, by_y, by_z)
    b_rest = swap(far_rest, "yl")
    b_two = b_two + mm(by_y[0, :block], wb)
    b_up, b_down = both_ways(*halves(b_two))
    one, three = mm(by_z[1], wa), mm(by_z[3], wa)
    one = jnp.concatenate([one[:block] + up, one[block:]], axis=0)
    three = jnp.concatenate([three[:block], three[block:] + down], axis=0)
    a_came = both_ways(one[:, :MIDDLE], three[:, :MIDDLE])
    later, b_up, b_down = together((one[:, MIDDLE:], three[:, MIDDLE:]), b_up, b_down)
    a_more = both_ways(*later)
    a = mm(by_z[0], wa[:, :MIDDLE]) + sum(a_came)
    b_rest = b_rest + mm(by_y[0, block:], wb)
    half = block // 2
    b_one, b_three = b_rest[block : 2 * block], b_rest[2 * block :]
    b_one = jnp.concatenate([b_one[:half] + b_up, b_one[half:]], axis=0)
    b_three = jnp.concatenate([b_three[:half], b_three[half:] + b_down], axis=0)
    a, b_one, b_three, by_z = together(a, b_one, b_three, by_z)
    a_came = swap(a[block:], "yl")
    b_came = both_ways(b_one, b_three)
    more = mm(by_z[0], wa[:, MIDDLE:]) + sum(a_more)
    more_came = swap(more[block:], "yl")
    return jnp.concatenate(
        [b_rest[:block] + sum(b_came), a[:block] + a_came, more[:block] + more_came], axis=1
    )


def body(keys, queries, values, rates, gate, up, down, out_weight):
    at = jnp.stack([lax.axis_index(name).astype(jnp.int32) for name in ("core", "yl", "z")])
    weights = tuple(in_hbm(w) for w in (gate, up, down))
    k, d, sent = sort_tokens(at, keys, values, rates.T)
    came = swap(sent, "core")
    partial, rounded = near_grads(at, k, d, *weights)
    queries, partial = together(queries, partial)
    q, q_sent = sort_queries(at, queries)
    summed = far_grads(came, rounded, partial)
    q_sent, summed = together(q_sent, summed)
    whole, q_sent = together(plane_sum(summed), q_sent)
    q_came = swap(q_sent, "core")
    v = newton(at, whole, *weights)
    o_came = swap(call(far_query_kernel, "far_query", out(q_sent.shape, F32), [], q_came, v), "core")
    o = call(near_query_kernel, "near_query", out(q.shape, BF16), [], q, v)
    by_y, by_z = join(at, o, o_came)
    return project_scatter(by_y, by_z, out_weight).astype(BF16)


def solution(mesh):
    fine = Mesh(mesh.devices.reshape(2, 4, 4, 2, 2), AXES)
    ctx, head = ("x", "yh", "core"), ("yl", "z")
    in_specs = (
        P(ctx, head),
        P(ctx, head),
        P(ctx, head),
        P(ctx, head),
        P(head, None, None),
        P(head, None, None),
        P(head, None, None),
        P(head, None),
    )
    out_specs = P(ctx + head, None)
    return jax.shard_map(body, mesh=fine, in_specs=in_specs, out_specs=out_specs, check_vma=False)
```

```python
import jax
import jax.numpy as jnp
from jax import lax
from jax.experimental import pallas as pl
from jax.experimental.pallas import tpu as pltpu
from jax.sharding import Mesh, PartitionSpec as P

NS_STEPS = 5
ns_a = 3.4445
ns_b = -4.775
ns_c = 2.0315
eps_value = 1e-06

AXES = ("yl", "z", "x", "yh", "core")
PLANE = ("x", "yh")
SHARDS = 8
TILE = 256
VMEM_LIMIT = 24 << 20
CUT = 2304
MIDDLE = 1408
Y_ORDER = (2, 0, 1, 3)
F32 = jnp.float32
BF16 = jnp.bfloat16


def mm(a, b):
    return jnp.dot(a, b, preferred_element_type=F32)


def mm_nt(a, b):
    return lax.dot_general(a, b, (((1,), (1,)), ((), ())), preferred_element_type=F32)


def call(kernel, name, outs, scratch, *operands):
    specs = [pl.BlockSpec(memory_space=pltpu.SMEM if a.dtype == jnp.int32 else pltpu.VMEM) for a in operands]
    return pl.pallas_call(
        kernel,
        out_shape=outs,
        in_specs=specs,
        out_specs=jax.tree.map(lambda _: pl.BlockSpec(memory_space=pltpu.VMEM), outs),
        scratch_shapes=scratch,
        compiler_params=pltpu.CompilerParams(vmem_limit_bytes=VMEM_LIMIT),
        name=name,
    )(*operands)


def in_hbm(a):
    return pltpu.with_memory_space_constraint(a, pltpu.HBM)


def out(shape, dtype):
    return jax.ShapeDtypeStruct(shape, dtype)


def sort_tokens_kernel(at_ref, r_ref, k_ref, v_ref, k_o, d_o, sent, k_s, v_s, sems):
    rows, width = k_o.shape
    half = rows // 2
    copies = [
        pltpu.make_async_copy(ref.at[pl.ds(i * half, half)], to.at[pl.ds(i * half, half)], sems.at[2 * n + i])
        for n, (ref, to) in enumerate(((k_ref, k_s), (v_ref, v_s)))
        for i in range(2)
    ]
    for copy in copies:
        copy.start()
    for copy in copies:
        copy.wait()
    for h in range(2):

        @pl.when(at_ref[0] == h)
        def _():
            near, far = slice(h * width, (h + 1) * width), slice((1 - h) * width, (2 - h) * width)
            k_o[...] = k_s[:, near]
            sent[:, :width] = k_s[:, far].astype(F32)
            for head, columns in ((h, near), (1 - h, far)):
                rate = r_ref[head : head + 1, :].T
                d = (-rate * v_s[:, columns].astype(F32)).astype(BF16)
                if head == h:
                    d_o[...] = d
                else:
                    sent[:, width:] = d.astype(F32)


def sort_tokens(at, keys, values, rates):
    shape = (keys.shape[0], keys.shape[1] // 2)
    vmem, hbm = pl.BlockSpec(memory_space=pltpu.VMEM), pl.BlockSpec(memory_space=pltpu.HBM)
    return pl.pallas_call(
        sort_tokens_kernel,
        out_shape=[out(shape, BF16), out(shape, BF16), out(keys.shape, F32)],
        in_specs=[pl.BlockSpec(memory_space=pltpu.SMEM), vmem, hbm, hbm],
        out_specs=[vmem] * 3,
        scratch_shapes=[pltpu.VMEM(keys.shape, BF16)] * 2 + [pltpu.SemaphoreType.DMA((4,))],
        compiler_params=pltpu.CompilerParams(vmem_limit_bytes=VMEM_LIMIT),
        name="sort_tokens",
    )(at, rates, in_hbm(keys), in_hbm(values))


def side_by_side(rows, r, block, width):
    top = (r * block) % (rows // 2)
    left = width * ((r * block) // (rows // 2))
    return slice(top, top + block), slice(left, left + width)


def sort_queries_kernel(at_ref, q_ref, q_o, sent):
    rows, width = q_o.shape
    block = rows // 8
    for h in range(2):

        @pl.when(at_ref[0] == h)
        def _():
            near, far = slice(h * width, (h + 1) * width), slice((1 - h) * width, (2 - h) * width)
            for r in range(8):
                row = ((at_ref[1] + r // 4) % 2) * 4 + (at_ref[2] + r % 4) % 4
                source = pl.ds(pl.multiple_of(row * block, block), block)
                q_o[r * block : (r + 1) * block, :] = q_ref[source, near]
                to_rows, to_columns = side_by_side(rows, r, block, width)
                sent[to_rows, to_columns] = q_ref[source, far].astype(F32)


def sort_queries(at, queries):
    rows, columns = queries.shape
    shapes = [out((rows, columns // 2), BF16), out((rows // 2, columns), F32)]
    return call(sort_queries_kernel, "sort_queries", shapes, [], at, queries)


def grads_of(k_ref, d_ref, w_ref, hk_s, dg_s, du_s):
    rows = k_ref.shape[0]
    wg, wu, wd = w_ref[0], w_ref[1], w_ref[2]
    step = 256
    for t in range(0, rows, step):
        at = slice(t, t + step)
        k = k_ref[at, :]
        gate = mm(k, wg)
        upper = mm(k, wu)
        dhid = mm(d_ref[at, :], wd)
        sig = jax.nn.sigmoid(gate)
        act = gate * sig
        hk_s[at, :] = (act * upper).astype(BF16)
        dg_s[at, :] = (dhid * upper * sig * (1.0 + gate * (1.0 - sig))).astype(BF16)
        du_s[at, :] = (dhid * act).astype(BF16)
    kt = k_ref[...].T
    dt = d_ref[...].T
    for m, (left, right) in enumerate(((kt, dg_s), (kt, du_s), (dt, hk_s))):
        yield m, mm(left, right[...])


def near_grads_kernel(at_ref, k_ref, d_ref, g_ref, u_ref, w_ref, o_ref, b_ref, f_s, hk_s, dg_s, du_s, sems):
    copies = [
        pltpu.make_async_copy(ref.at[at_ref[0]], f_s.at[m], sems.at[m]) for m, ref in enumerate((g_ref, u_ref, w_ref))
    ]
    for copy in copies:
        copy.start()
    for m, copy in enumerate(copies):
        copy.wait()
        b_ref[m] = f_s[m].astype(BF16)
    for m, grad in grads_of(k_ref, d_ref, b_ref, hk_s, dg_s, du_s):
        o_ref[m] = grad


def far_grads_kernel(came, b_ref, p_ref, o_ref, k_s, d_s, hk_s, dg_s, du_s):
    part = o_ref.shape[2]
    width = k_s.shape[1]
    k_s[...] = came[:, :width].astype(BF16)
    d_s[...] = came[:, width:].astype(BF16)
    for m, grad in grads_of(k_s, d_s, b_ref, hk_s, dg_s, du_s):
        for j in range(SHARDS):
            rows = slice(j * part, (j + 1) * part)
            o_ref[j, m] = grad[rows, :] + p_ref[m, rows, :]


def near_grads(at, k, d, gate, up, down):
    heads, width, hidden = gate.shape
    vmem, hbm = pl.BlockSpec(memory_space=pltpu.VMEM), pl.BlockSpec(memory_space=pltpu.HBM)
    shape = (3, width, hidden)
    return pl.pallas_call(
        near_grads_kernel,
        out_shape=[out(shape, F32), out(shape, BF16)],
        in_specs=[pl.BlockSpec(memory_space=pltpu.SMEM), vmem, vmem, hbm, hbm, hbm],
        out_specs=[vmem, vmem],
        scratch_shapes=[pltpu.VMEM(shape, F32)]
        + [pltpu.VMEM((k.shape[0], hidden), BF16)] * 3
        + [pltpu.SemaphoreType.DMA((3,))],
        compiler_params=pltpu.CompilerParams(vmem_limit_bytes=VMEM_LIMIT),
        name="near_grads",
    )(at, k, d, gate, up, down)


def far_grads(came, w, partial):
    heads, width, hidden = partial.shape
    rows = came.shape[0]
    scratch = [pltpu.VMEM((rows, width), BF16)] * 2 + [pltpu.VMEM((rows, hidden), BF16)] * 3
    shape = out((SHARDS, 3, width // SHARDS, hidden), F32)
    return call(far_grads_kernel, "far_grads", shape, scratch, came, w, partial)


def split(x):
    high = x.astype(BF16)
    return high, (x - high.astype(F32)).astype(BF16)


def packed(high, low):
    return jnp.concatenate([high, high, low], axis=1)


def mirrored(left, corner):
    at = left.shape[1]
    return jnp.concatenate([left, jnp.concatenate([left[at:].T, corner], axis=0)], axis=1)


def gram_of(xh, xl):
    a, b = packed(xh, xl), jnp.concatenate([xh, xl, xh], axis=1)
    return mirrored(mm_nt(a, b[:TILE]), mm_nt(a[TILE:], b[TILE:]))


def square_of(ah, al):
    a, b = packed(ah, al), jnp.concatenate([ah, al, ah], axis=0)
    return mirrored(mm(a, b[:, :TILE]), mm(a[TILE:], b[:, TILE:]))


def newton_kernel(at_ref, g_ref, wg_ref, wu_ref, wd_ref, v_ref, x_s, f_s, sems):
    copies = [
        pltpu.make_async_copy(ref.at[at_ref[0]], f_s.at[m], sems.at[m])
        for m, ref in enumerate((wg_ref, wu_ref, wd_ref))
    ]
    for copy in copies:
        copy.start()
    matrices, width, hidden = x_s.shape
    every = range(matrices)
    for m in every:
        grad = g_ref[:, m].reshape(width, hidden)
        total = jnp.sum(jnp.sum(grad * grad, axis=1, keepdims=True), axis=0, keepdims=True)
        x_s[m] = grad * lax.rsqrt(total + eps_value)

    def sweep():
        xs = [x_s[m] for m in every]
        parts = [split(x) for x in xs]
        grams = [gram_of(*p) for p in parts]
        squares = [square_of(*split(g)) for g in grams]
        mixers = [split(ns_b * g + ns_c * q) for g, q in zip(grams, squares)]
        for m, x, (xh, xl), mixer in zip(every, xs, parts, mixers):
            x_s[m] = ns_a * x + mm(packed(*mixer), jnp.concatenate([xh, xl, xh], axis=0))

    def sweeps(_, carry):
        sweep()
        sweep()
        return carry

    lax.fori_loop(0, NS_STEPS // 2, sweeps, 0)
    for _ in range(NS_STEPS % 2):
        sweep()
    for m, copy in enumerate(copies):
        copy.wait()
        v_ref[m] = (f_s[m] - x_s[m]).astype(BF16)


def newton(at, grads, gate, up, down):
    shape = (grads.shape[1], grads.shape[0] * grads.shape[2], grads.shape[3])
    vmem, hbm = pl.BlockSpec(memory_space=pltpu.VMEM), pl.BlockSpec(memory_space=pltpu.HBM)
    return pl.pallas_call(
        newton_kernel,
        out_shape=out(shape, BF16),
        in_specs=[pl.BlockSpec(memory_space=pltpu.SMEM), vmem, hbm, hbm, hbm],
        out_specs=vmem,
        scratch_shapes=[pltpu.VMEM(shape, F32)] * 2 + [pltpu.SemaphoreType.DMA((3,))],
        compiler_params=pltpu.CompilerParams(vmem_limit_bytes=VMEM_LIMIT),
        name="newton",
    )(at, grads, gate, up, down)


def query_rows(q, v_ref):
    gate = mm(q, v_ref[0])
    hidden = (gate * jax.nn.sigmoid(gate) * mm(q, v_ref[1])).astype(BF16)
    return mm_nt(hidden, v_ref[2]).astype(BF16)


def far_query_kernel(came, v_ref, o_ref):
    width = came.shape[1] // 2
    for left in (0, width):
        columns = slice(left, left + width)
        o_ref[:, columns] = query_rows(came[:, columns].astype(BF16), v_ref).astype(F32)


def near_query_kernel(q_ref, v_ref, o_ref):
    half = q_ref.shape[0] // 2
    for top in (0, half):
        rows = slice(top, top + half)
        o_ref[rows, :] = query_rows(q_ref[rows, :], v_ref)


def join_kernel(at_ref, o_ref, came, y_ref, z_ref):
    rows, width = o_ref.shape
    block = rows // 8
    for h in range(2):

        @pl.when(at_ref[0] == h)
        def _():
            near, far = slice(h * width, (h + 1) * width), slice((1 - h) * width, (2 - h) * width)
            for dy in range(2):
                for dz in range(4):
                    r = dy * 4 + dz
                    to_y, to_z = pl.ds(Y_ORDER.index(dz) * block, block), pl.ds(dy * block, block)
                    mine = o_ref[r * block : (r + 1) * block, :]
                    other = came[side_by_side(rows, r, block, width)].astype(BF16)
                    for columns, piece in ((near, mine), (far, other)):
                        y_ref[dy, to_y, columns] = piece
                        z_ref[dz, to_z, columns] = piece


def join(at, mine, came):
    rows, width = mine.shape
    shapes = [out((n, rows // n, 2 * width), BF16) for n in (2, 4)]
    return call(join_kernel, "join", shapes, [], at, mine, came)


def swap(a, axis):
    return lax.ppermute(a, axis, [(0, 1), (1, 0)])


def ring(a, shift):
    return lax.ppermute(a, "z", [(i, (i + shift) % 4) for i in range(4)])


def sum_kernel(a_ref, o_ref):
    total = a_ref[0]
    for j in range(1, SHARDS):
        total = total + a_ref[j]
    for j in range(SHARDS):
        o_ref[j] = total


def plane_sum(a):
    came = lax.all_to_all(a, PLANE, 0, 0, tiled=True)
    same = call(sum_kernel, "sum_parts", out(a.shape, a.dtype), [], came)
    return lax.all_to_all(same, PLANE, 0, 0, tiled=True)


def together(*arrays):
    return lax.optimization_barrier(arrays)


def halves(a):
    half = a.shape[0] // 2
    return a[:half], a[half:]


def both_ways(up, down):
    return ring(up, 1), ring(down, -1)


def project_scatter(by_y, by_z, weight):
    wb, wa = weight[:, :CUT], weight[:, CUT:]
    block = by_z.shape[1] // 2
    far_two, by_y, by_z = together(mm(by_y[1, :block], wb), by_y, by_z)
    b_two = swap(far_two, "yl")
    up, down = both_ways(*halves(mm(by_z[2], wa)))
    far_rest, b_two, by_y, by_z = together(mm(by_y[1, block:], wb), b_two, by_y, by_z)
    b_rest = swap(far_rest, "yl")
    b_two = b_two + mm(by_y[0, :block], wb)
    b_up, b_down = both_ways(*halves(b_two))
    one, three = mm(by_z[1], wa), mm(by_z[3], wa)
    one = jnp.concatenate([one[:block] + up, one[block:]], axis=0)
    three = jnp.concatenate([three[:block], three[block:] + down], axis=0)
    a_came = both_ways(one[:, :MIDDLE], three[:, :MIDDLE])
    later, b_up, b_down = together((one[:, MIDDLE:], three[:, MIDDLE:]), b_up, b_down)
    a_more = both_ways(*later)
    a = mm(by_z[0], wa[:, :MIDDLE]) + sum(a_came)
    b_rest = b_rest + mm(by_y[0, block:], wb)
    half = block // 2
    b_one, b_three = b_rest[block : 2 * block], b_rest[2 * block :]
    b_one = jnp.concatenate([b_one[:half] + b_up, b_one[half:]], axis=0)
    b_three = jnp.concatenate([b_three[:half], b_three[half:] + b_down], axis=0)
    a, b_one, b_three, by_z = together(a, b_one, b_three, by_z)
    a_came = swap(a[block:], "yl")
    b_came = both_ways(b_one, b_three)
    more = mm(by_z[0], wa[:, MIDDLE:]) + sum(a_more)
    more_came = swap(more[block:], "yl")
    return jnp.concatenate(
        [b_rest[:block] + sum(b_came), a[:block] + a_came, more[:block] + more_came], axis=1
    )


def body(keys, queries, values, rates, gate, up, down, out_weight):
    at = jnp.stack([lax.axis_index(name).astype(jnp.int32) for name in ("core", "yl", "z")])
    weights = tuple(in_hbm(w) for w in (gate, up, down))
    k, d, sent = sort_tokens(at, keys, values, rates.T)
    came = swap(sent, "core")
    partial, rounded = near_grads(at, k, d, *weights)
    queries, partial = together(queries, partial)
    q, q_sent = sort_queries(at, queries)
    summed = far_grads(came, rounded, partial)
    q_sent, summed = together(q_sent, summed)
    whole, q_sent = together(plane_sum(summed), q_sent)
    q_came = swap(q_sent, "core")
    v = newton(at, whole, *weights)
    o_came = swap(call(far_query_kernel, "far_query", out(q_sent.shape, F32), [], q_came, v), "core")
    o = call(near_query_kernel, "near_query", out(q.shape, BF16), [], q, v)
    by_y, by_z = join(at, o, o_came)
    return project_scatter(by_y, by_z, out_weight).astype(BF16)


def solution(mesh):
    fine = Mesh(mesh.devices.reshape(2, 4, 4, 2, 2), AXES)
    ctx, head = ("x", "yh", "core"), ("yl", "z")
    in_specs = (
        P(ctx, head),
        P(ctx, head),
        P(ctx, head),
        P(ctx, head),
        P(head, None, None),
        P(head, None, None),
        P(head, None, None),
        P(head, None),
    )
    out_specs = P(ctx + head, None)
    return jax.shard_map(body, mesh=fine, in_specs=in_specs, out_specs=out_specs, check_vma=False)
```

```python
import jax
import jax.numpy as jnp
from jax import lax
from jax.experimental import pallas as pl
from jax.experimental.pallas import tpu as pltpu
from jax.sharding import Mesh, PartitionSpec as P

NS_STEPS = 5
ns_a = 3.4445
ns_b = -4.775
ns_c = 2.0315
eps_value = 1e-06

AXES = ("yl", "z", "x", "yh", "core")
PLANE = ("x", "yh")
SHARDS = 8
TILE = 256
VMEM_LIMIT = 24 << 20
CUT = 2304
MIDDLE = 1408
Y_ORDER = (2, 0, 1, 3)
F32 = jnp.float32
BF16 = jnp.bfloat16


def mm(a, b):
    return jnp.dot(a, b, preferred_element_type=F32)


def mm_nt(a, b):
    return lax.dot_general(a, b, (((1,), (1,)), ((), ())), preferred_element_type=F32)


def call(kernel, name, outs, scratch, *operands):
    specs = [pl.BlockSpec(memory_space=pltpu.SMEM if a.dtype == jnp.int32 else pltpu.VMEM) for a in operands]
    return pl.pallas_call(
        kernel,
        out_shape=outs,
        in_specs=specs,
        out_specs=jax.tree.map(lambda _: pl.BlockSpec(memory_space=pltpu.VMEM), outs),
        scratch_shapes=scratch,
        compiler_params=pltpu.CompilerParams(vmem_limit_bytes=VMEM_LIMIT),
        name=name,
    )(*operands)


def in_hbm(a):
    return pltpu.with_memory_space_constraint(a, pltpu.HBM)


def out(shape, dtype):
    return jax.ShapeDtypeStruct(shape, dtype)


def sort_tokens_kernel(at_ref, r_ref, k_ref, v_ref, k_o, d_o, sent, k_s, v_s, sems):
    rows, width = k_o.shape
    half = rows // 2
    copies = [
        pltpu.make_async_copy(ref.at[pl.ds(i * half, half)], to.at[pl.ds(i * half, half)], sems.at[2 * n + i])
        for n, (ref, to) in enumerate(((k_ref, k_s), (v_ref, v_s)))
        for i in range(2)
    ]
    for copy in copies:
        copy.start()
    for copy in copies:
        copy.wait()
    for h in range(2):

        @pl.when(at_ref[0] == h)
        def _():
            near, far = slice(h * width, (h + 1) * width), slice((1 - h) * width, (2 - h) * width)
            k_o[...] = k_s[:, near]
            sent[:, :width] = k_s[:, far].astype(F32)
            for head, columns in ((h, near), (1 - h, far)):
                rate = r_ref[head : head + 1, :].T
                d = (-rate * v_s[:, columns].astype(F32)).astype(BF16)
                if head == h:
                    d_o[...] = d
                else:
                    sent[:, width:] = d.astype(F32)


def sort_tokens(at, keys, values, rates):
    shape = (keys.shape[0], keys.shape[1] // 2)
    vmem, hbm = pl.BlockSpec(memory_space=pltpu.VMEM), pl.BlockSpec(memory_space=pltpu.HBM)
    return pl.pallas_call(
        sort_tokens_kernel,
        out_shape=[out(shape, BF16), out(shape, BF16), out(keys.shape, F32)],
        in_specs=[pl.BlockSpec(memory_space=pltpu.SMEM), vmem, hbm, hbm],
        out_specs=[vmem] * 3,
        scratch_shapes=[pltpu.VMEM(keys.shape, BF16)] * 2 + [pltpu.SemaphoreType.DMA((4,))],
        compiler_params=pltpu.CompilerParams(vmem_limit_bytes=VMEM_LIMIT),
        name="sort_tokens",
    )(at, rates, in_hbm(keys), in_hbm(values))


def side_by_side(rows, r, block, width):
    top = (r * block) % (rows // 2)
    left = width * ((r * block) // (rows // 2))
    return slice(top, top + block), slice(left, left + width)


def sort_queries_kernel(at_ref, q_ref, q_o, sent):
    rows, width = q_o.shape
    block = rows // 8
    for h in range(2):

        @pl.when(at_ref[0] == h)
        def _():
            near, far = slice(h * width, (h + 1) * width), slice((1 - h) * width, (2 - h) * width)
            for r in range(8):
                row = ((at_ref[1] + r // 4) % 2) * 4 + (at_ref[2] + r % 4) % 4
                source = pl.ds(pl.multiple_of(row * block, block), block)
                q_o[r * block : (r + 1) * block, :] = q_ref[source, near]
                to_rows, to_columns = side_by_side(rows, r, block, width)
                sent[to_rows, to_columns] = q_ref[source, far].astype(F32)


def sort_queries(at, queries):
    rows, columns = queries.shape
    shapes = [out((rows, columns // 2), BF16), out((rows // 2, columns), F32)]
    return call(sort_queries_kernel, "sort_queries", shapes, [], at, queries)


def grads_of(k_ref, d_ref, w_ref, hk_s, dg_s, du_s):
    rows = k_ref.shape[0]
    wg, wu, wd = w_ref[0], w_ref[1], w_ref[2]
    step = 256
    for t in range(0, rows, step):
        at = slice(t, t + step)
        k = k_ref[at, :]
        gate = mm(k, wg)
        upper = mm(k, wu)
        dhid = mm(d_ref[at, :], wd)
        sig = jax.nn.sigmoid(gate)
        act = gate * sig
        hk_s[at, :] = (act * upper).astype(BF16)
        dg_s[at, :] = (dhid * upper * sig * (1.0 + gate * (1.0 - sig))).astype(BF16)
        du_s[at, :] = (dhid * act).astype(BF16)
    kt = k_ref[...].T
    dt = d_ref[...].T
    for m, (left, right) in enumerate(((kt, dg_s), (kt, du_s), (dt, hk_s))):
        yield m, mm(left, right[...])


def near_grads_kernel(at_ref, k_ref, d_ref, g_ref, u_ref, w_ref, o_ref, b_ref, f_s, hk_s, dg_s, du_s, sems):
    copies = [
        pltpu.make_async_copy(ref.at[at_ref[0]], f_s.at[m], sems.at[m]) for m, ref in enumerate((g_ref, u_ref, w_ref))
    ]
    for copy in copies:
        copy.start()
    for m, copy in enumerate(copies):
        copy.wait()
        b_ref[m] = f_s[m].astype(BF16)
    for m, grad in grads_of(k_ref, d_ref, b_ref, hk_s, dg_s, du_s):
        o_ref[m] = grad


def far_grads_kernel(came, b_ref, p_ref, o_ref, k_s, d_s, hk_s, dg_s, du_s):
    part = o_ref.shape[2]
    width = k_s.shape[1]
    k_s[...] = came[:, :width].astype(BF16)
    d_s[...] = came[:, width:].astype(BF16)
    for m, grad in grads_of(k_s, d_s, b_ref, hk_s, dg_s, du_s):
        for j in range(SHARDS):
            rows = slice(j * part, (j + 1) * part)
            o_ref[j, m] = grad[rows, :] + p_ref[m, rows, :]


def near_grads(at, k, d, gate, up, down):
    heads, width, hidden = gate.shape
    vmem, hbm = pl.BlockSpec(memory_space=pltpu.VMEM), pl.BlockSpec(memory_space=pltpu.HBM)
    shape = (3, width, hidden)
    return pl.pallas_call(
        near_grads_kernel,
        out_shape=[out(shape, F32), out(shape, BF16)],
        in_specs=[pl.BlockSpec(memory_space=pltpu.SMEM), vmem, vmem, hbm, hbm, hbm],
        out_specs=[vmem, vmem],
        scratch_shapes=[pltpu.VMEM(shape, F32)]
        + [pltpu.VMEM((k.shape[0], hidden), BF16)] * 3
        + [pltpu.SemaphoreType.DMA((3,))],
        compiler_params=pltpu.CompilerParams(vmem_limit_bytes=VMEM_LIMIT),
        name="near_grads",
    )(at, k, d, gate, up, down)


def far_grads(came, w, partial):
    heads, width, hidden = partial.shape
    rows = came.shape[0]
    scratch = [pltpu.VMEM((rows, width), BF16)] * 2 + [pltpu.VMEM((rows, hidden), BF16)] * 3
    shape = out((SHARDS, 3, width // SHARDS, hidden), F32)
    return call(far_grads_kernel, "far_grads", shape, scratch, came, w, partial)


def split(x):
    high = x.astype(BF16)
    return high, (x - high.astype(F32)).astype(BF16)


def packed(high, low):
    return jnp.concatenate([high, high, low], axis=1)


def mirrored(left, corner):
    at = left.shape[1]
    return jnp.concatenate([left, jnp.concatenate([left[at:].T, corner], axis=0)], axis=1)


def gram_of(xh, xl):
    a, b = packed(xh, xl), jnp.concatenate([xh, xl, xh], axis=1)
    return mirrored(mm_nt(a, b[:TILE]), mm_nt(a[TILE:], b[TILE:]))


def square_of(ah, al):
    a, b = packed(ah, al), jnp.concatenate([ah, al, ah], axis=0)
    return mirrored(mm(a, b[:, :TILE]), mm(a[TILE:], b[:, TILE:]))


def newton_kernel(at_ref, g_ref, wg_ref, wu_ref, wd_ref, v_ref, x_s, f_s, sems):
    copies = [
        pltpu.make_async_copy(ref.at[at_ref[0]], f_s.at[m], sems.at[m])
        for m, ref in enumerate((wg_ref, wu_ref, wd_ref))
    ]
    for copy in copies:
        copy.start()
    matrices, width, hidden = x_s.shape
    every = range(matrices)
    for m in every:
        grad = g_ref[:, m].reshape(width, hidden)
        total = jnp.sum(jnp.sum(grad * grad, axis=1, keepdims=True), axis=0, keepdims=True)
        x_s[m] = grad * lax.rsqrt(total + eps_value)

    def sweep(_, carry):
        xs = [x_s[m] for m in every]
        parts = [split(x) for x in xs]
        grams = [gram_of(*p) for p in parts]
        squares = [square_of(*split(g)) for g in grams]
        mixers = [split(ns_b * g + ns_c * q) for g, q in zip(grams, squares)]
        for m, x, (xh, xl), mixer in zip(every, xs, parts, mixers):
            x_s[m] = ns_a * x + mm(packed(*mixer), jnp.concatenate([xh, xl, xh], axis=0))
        return carry

    lax.fori_loop(0, NS_STEPS, sweep, 0)
    for m, copy in enumerate(copies):
        copy.wait()
        v_ref[m] = (f_s[m] - x_s[m]).astype(BF16)


def newton(at, grads, gate, up, down):
    shape = (grads.shape[1], grads.shape[0] * grads.shape[2], grads.shape[3])
    vmem, hbm = pl.BlockSpec(memory_space=pltpu.VMEM), pl.BlockSpec(memory_space=pltpu.HBM)
    return pl.pallas_call(
        newton_kernel,
        out_shape=out(shape, BF16),
        in_specs=[pl.BlockSpec(memory_space=pltpu.SMEM), vmem, hbm, hbm, hbm],
        out_specs=vmem,
        scratch_shapes=[pltpu.VMEM(shape, F32)] * 2 + [pltpu.SemaphoreType.DMA((3,))],
        compiler_params=pltpu.CompilerParams(vmem_limit_bytes=VMEM_LIMIT),
        name="newton",
    )(at, grads, gate, up, down)


def query_rows(q, v_ref):
    gate = mm(q, v_ref[0])
    hidden = (gate * jax.nn.sigmoid(gate) * mm(q, v_ref[1])).astype(BF16)
    return mm_nt(hidden, v_ref[2]).astype(BF16)


def far_query_kernel(came, v_ref, o_ref):
    width = came.shape[1] // 2
    for left in (0, width):
        columns = slice(left, left + width)
        o_ref[:, columns] = query_rows(came[:, columns].astype(BF16), v_ref).astype(F32)


def near_query_kernel(q_ref, v_ref, o_ref):
    half = q_ref.shape[0] // 2
    for top in (0, half):
        rows = slice(top, top + half)
        o_ref[rows, :] = query_rows(q_ref[rows, :], v_ref)


def join_kernel(at_ref, o_ref, came, y_ref, z_ref):
    rows, width = o_ref.shape
    block = rows // 8
    for h in range(2):

        @pl.when(at_ref[0] == h)
        def _():
            near, far = slice(h * width, (h + 1) * width), slice((1 - h) * width, (2 - h) * width)
            for dy in range(2):
                for dz in range(4):
                    r = dy * 4 + dz
                    to_y, to_z = pl.ds(Y_ORDER.index(dz) * block, block), pl.ds(dy * block, block)
                    mine = o_ref[r * block : (r + 1) * block, :]
                    other = came[side_by_side(rows, r, block, width)].astype(BF16)
                    for columns, piece in ((near, mine), (far, other)):
                        y_ref[dy, to_y, columns] = piece
                        z_ref[dz, to_z, columns] = piece


def join(at, mine, came):
    rows, width = mine.shape
    shapes = [out((n, rows // n, 2 * width), BF16) for n in (2, 4)]
    return call(join_kernel, "join", shapes, [], at, mine, came)


def swap(a, axis):
    return lax.ppermute(a, axis, [(0, 1), (1, 0)])


def ring(a, shift):
    return lax.ppermute(a, "z", [(i, (i + shift) % 4) for i in range(4)])


def sum_kernel(a_ref, o_ref):
    total = a_ref[0]
    for j in range(1, SHARDS):
        total = total + a_ref[j]
    for j in range(SHARDS):
        o_ref[j] = total


def plane_sum(a):
    came = lax.all_to_all(a, PLANE, 0, 0, tiled=True)
    same = call(sum_kernel, "sum_parts", out(a.shape, a.dtype), [], came)
    return lax.all_to_all(same, PLANE, 0, 0, tiled=True)


def together(*arrays):
    return lax.optimization_barrier(arrays)


def halves(a):
    half = a.shape[0] // 2
    return a[:half], a[half:]


def both_ways(up, down):
    return ring(up, 1), ring(down, -1)


def project_scatter(by_y, by_z, weight):
    wb, wa = weight[:, :CUT], weight[:, CUT:]
    block = by_z.shape[1] // 2
    far_two, by_y, by_z = together(mm(by_y[1, :block], wb), by_y, by_z)
    b_two = swap(far_two, "yl")
    up, down = both_ways(*halves(mm(by_z[2], wa)))
    far_rest, b_two, by_y, by_z = together(mm(by_y[1, block:], wb), b_two, by_y, by_z)
    b_rest = swap(far_rest, "yl")
    b_two = b_two + mm(by_y[0, :block], wb)
    b_up, b_down = both_ways(*halves(b_two))
    one, three = mm(by_z[1], wa), mm(by_z[3], wa)
    one = jnp.concatenate([one[:block] + up, one[block:]], axis=0)
    three = jnp.concatenate([three[:block], three[block:] + down], axis=0)
    a_came = both_ways(one[:, :MIDDLE], three[:, :MIDDLE])
    later, a_came = together((one[:, MIDDLE:], three[:, MIDDLE:]), a_came)
    a_more = both_ways(*later)
    a = mm(by_z[0], wa[:, :MIDDLE]) + sum(a_came)
    b_rest = b_rest + mm(by_y[0, block:], wb)
    half = block // 2
    b_one, b_three = b_rest[block : 2 * block], b_rest[2 * block :]
    b_one = jnp.concatenate([b_one[:half] + b_up, b_one[half:]], axis=0)
    b_three = jnp.concatenate([b_three[:half], b_three[half:] + b_down], axis=0)
    a, b_one, b_three, by_z = together(a, b_one, b_three, by_z)
    a_came = swap(a[block:], "yl")
    b_came = both_ways(b_one, b_three)
    more = mm(by_z[0], wa[:, MIDDLE:]) + sum(a_more)
    more_came = swap(more[block:], "yl")
    return jnp.concatenate(
        [b_rest[:block] + sum(b_came), a[:block] + a_came, more[:block] + more_came], axis=1
    )


def body(keys, queries, values, rates, gate, up, down, out_weight):
    at = jnp.stack([lax.axis_index(name).astype(jnp.int32) for name in ("core", "yl", "z")])
    weights = tuple(in_hbm(w) for w in (gate, up, down))
    k, d, sent = sort_tokens(at, keys, values, rates.T)
    came = swap(sent, "core")
    partial, rounded = near_grads(at, k, d, *weights)
    queries, partial = together(queries, partial)
    q, q_sent = sort_queries(at, queries)
    summed = far_grads(came, rounded, partial)
    q_sent, summed = together(q_sent, summed)
    whole, q_sent = together(plane_sum(summed), q_sent)
    q_came = swap(q_sent, "core")
    v = newton(at, whole, *weights)
    o_came = swap(call(far_query_kernel, "far_query", out(q_sent.shape, F32), [], q_came, v), "core")
    o = call(near_query_kernel, "near_query", out(q.shape, BF16), [], q, v)
    by_y, by_z = join(at, o, o_came)
    return project_scatter(by_y, by_z, out_weight).astype(BF16)


def solution(mesh):
    fine = Mesh(mesh.devices.reshape(2, 4, 4, 2, 2), AXES)
    ctx, head = ("x", "yh", "core"), ("yl", "z")
    in_specs = (
        P(ctx, head),
        P(ctx, head),
        P(ctx, head),
        P(ctx, head),
        P(head, None, None),
        P(head, None, None),
        P(head, None, None),
        P(head, None),
    )
    out_specs = P(ctx + head, None)
    return jax.shard_map(body, mesh=fine, in_specs=in_specs, out_specs=out_specs, check_vma=False)
```

```python
import jax
import jax.numpy as jnp
from jax import lax
from jax.experimental import pallas as pl
from jax.experimental.pallas import tpu as pltpu
from jax.sharding import Mesh, PartitionSpec as P

NS_STEPS = 5
ns_a = 3.4445
ns_b = -4.775
ns_c = 2.0315
eps_value = 1e-06

AXES = ("yl", "z", "x", "yh", "core")
PLANE = ("x", "yh")
SHARDS = 8
PARTS = 4
TILE = 256
VMEM_LIMIT = 24 << 20
CUT = 2304
MIDDLE = 1408
Y_ORDER = (2, 0, 1, 3)
F32 = jnp.float32
BF16 = jnp.bfloat16


def mm(a, b):
    return jnp.dot(a, b, preferred_element_type=F32)


def mm_nt(a, b):
    return lax.dot_general(a, b, (((1,), (1,)), ((), ())), preferred_element_type=F32)


def call(kernel, name, outs, scratch, *operands):
    specs = [pl.BlockSpec(memory_space=pltpu.SMEM if a.dtype == jnp.int32 else pltpu.VMEM) for a in operands]
    return pl.pallas_call(
        kernel,
        out_shape=outs,
        in_specs=specs,
        out_specs=jax.tree.map(lambda _: pl.BlockSpec(memory_space=pltpu.VMEM), outs),
        scratch_shapes=scratch,
        compiler_params=pltpu.CompilerParams(vmem_limit_bytes=VMEM_LIMIT),
        name=name,
    )(*operands)


def in_hbm(a):
    return pltpu.with_memory_space_constraint(a, pltpu.HBM)


def out(shape, dtype):
    return jax.ShapeDtypeStruct(shape, dtype)


def sort_tokens_kernel(at_ref, r_ref, k_ref, v_ref, k_o, d_o, sent, k_s, v_s, sems):
    rows, width = k_o.shape
    half = rows // 2
    copies = [
        pltpu.make_async_copy(ref.at[pl.ds(i * half, half)], to.at[pl.ds(i * half, half)], sems.at[2 * n + i])
        for n, (ref, to) in enumerate(((k_ref, k_s), (v_ref, v_s)))
        for i in range(2)
    ]
    for copy in copies:
        copy.start()
    for copy in copies:
        copy.wait()
    for h in range(2):

        @pl.when(at_ref[0] == h)
        def _():
            near, far = slice(h * width, (h + 1) * width), slice((1 - h) * width, (2 - h) * width)
            k_o[...] = k_s[:, near]
            sent[:, :width] = k_s[:, far].astype(F32)
            for head, columns in ((h, near), (1 - h, far)):
                rate = r_ref[head : head + 1, :].T
                d = (-rate * v_s[:, columns].astype(F32)).astype(BF16)
                if head == h:
                    d_o[...] = d
                else:
                    sent[:, width:] = d.astype(F32)


def sort_tokens(at, keys, values, rates):
    shape = (keys.shape[0], keys.shape[1] // 2)
    vmem, hbm = pl.BlockSpec(memory_space=pltpu.VMEM), pl.BlockSpec(memory_space=pltpu.HBM)
    return pl.pallas_call(
        sort_tokens_kernel,
        out_shape=[out(shape, BF16), out(shape, BF16), out(keys.shape, F32)],
        in_specs=[pl.BlockSpec(memory_space=pltpu.SMEM), vmem, hbm, hbm],
        out_specs=[vmem] * 3,
        scratch_shapes=[pltpu.VMEM(keys.shape, BF16)] * 2 + [pltpu.SemaphoreType.DMA((4,))],
        compiler_params=pltpu.CompilerParams(vmem_limit_bytes=VMEM_LIMIT),
        name="sort_tokens",
    )(at, rates, in_hbm(keys), in_hbm(values))


def side_by_side(rows, r, block, width):
    top = (r * block) % (rows // 2)
    left = width * ((r * block) // (rows // 2))
    return slice(top, top + block), slice(left, left + width)


def sort_queries_kernel(at_ref, q_ref, q_o, sent):
    rows, width = q_o.shape
    block = rows // 8
    for h in range(2):

        @pl.when(at_ref[0] == h)
        def _():
            near, far = slice(h * width, (h + 1) * width), slice((1 - h) * width, (2 - h) * width)
            for r in range(8):
                row = ((at_ref[1] + r // 4) % 2) * 4 + (at_ref[2] + r % 4) % 4
                source = pl.ds(pl.multiple_of(row * block, block), block)
                q_o[r * block : (r + 1) * block, :] = q_ref[source, near]
                to_rows, to_columns = side_by_side(rows, r, block, width)
                sent[to_rows, to_columns] = q_ref[source, far].astype(F32)


def sort_queries(at, queries):
    rows, columns = queries.shape
    shapes = [out((rows, columns // 2), BF16), out((rows // 2, columns), F32)]
    return call(sort_queries_kernel, "sort_queries", shapes, [], at, queries)


def grads_of(k_ref, d_ref, w_ref, hk_s, dg_s, du_s):
    rows = k_ref.shape[0]
    wg, wu, wd = w_ref[0], w_ref[1], w_ref[2]
    step = 256
    for t in range(0, rows, step):
        at = slice(t, t + step)
        k = k_ref[at, :]
        gate = mm(k, wg)
        upper = mm(k, wu)
        dhid = mm(d_ref[at, :], wd)
        sig = jax.nn.sigmoid(gate)
        act = gate * sig
        hk_s[at, :] = (act * upper).astype(BF16)
        dg_s[at, :] = (dhid * upper * sig * (1.0 + gate * (1.0 - sig))).astype(BF16)
        du_s[at, :] = (dhid * act).astype(BF16)
    kt = k_ref[...].T
    dt = d_ref[...].T
    for m, (left, right) in enumerate(((kt, dg_s), (kt, du_s), (dt, hk_s))):
        yield m, mm(left, right[...])


def near_grads_kernel(at_ref, k_ref, d_ref, g_ref, u_ref, w_ref, o_ref, b_ref, f_s, hk_s, dg_s, du_s, sems):
    step = f_s.shape[1] // PARTS
    copies = [
        pltpu.make_async_copy(
            ref.at[at_ref[0], pl.ds(i * step, step)], f_s.at[m, pl.ds(i * step, step)], sems.at[PARTS * m + i]
        )
        for m, ref in enumerate((g_ref, u_ref, w_ref))
        for i in range(PARTS)
    ]
    for copy in copies:
        copy.start()
    for n, copy in enumerate(copies):
        copy.wait()
        rows = slice(n % PARTS * step, n % PARTS * step + step)
        b_ref[n // PARTS, rows] = f_s[n // PARTS, rows].astype(BF16)
    for m, grad in grads_of(k_ref, d_ref, b_ref, hk_s, dg_s, du_s):
        o_ref[m] = grad


def far_grads_kernel(came, b_ref, p_ref, o_ref, k_s, d_s, hk_s, dg_s, du_s):
    part = o_ref.shape[2]
    width = k_s.shape[1]
    k_s[...] = came[:, :width].astype(BF16)
    d_s[...] = came[:, width:].astype(BF16)
    for m, grad in grads_of(k_s, d_s, b_ref, hk_s, dg_s, du_s):
        for j in range(SHARDS):
            rows = slice(j * part, (j + 1) * part)
            o_ref[j, m] = grad[rows, :] + p_ref[m, rows, :]


def near_grads(at, k, d, gate, up, down):
    heads, width, hidden = gate.shape
    vmem, hbm = pl.BlockSpec(memory_space=pltpu.VMEM), pl.BlockSpec(memory_space=pltpu.HBM)
    shape = (3, width, hidden)
    return pl.pallas_call(
        near_grads_kernel,
        out_shape=[out(shape, F32), out(shape, BF16)],
        in_specs=[pl.BlockSpec(memory_space=pltpu.SMEM), vmem, vmem, hbm, hbm, hbm],
        out_specs=[vmem, vmem],
        scratch_shapes=[pltpu.VMEM(shape, F32)]
        + [pltpu.VMEM((k.shape[0], hidden), BF16)] * 3
        + [pltpu.SemaphoreType.DMA((3 * PARTS,))],
        compiler_params=pltpu.CompilerParams(vmem_limit_bytes=VMEM_LIMIT),
        name="near_grads",
    )(at, k, d, gate, up, down)


def far_grads(came, w, partial):
    heads, width, hidden = partial.shape
    rows = came.shape[0]
    scratch = [pltpu.VMEM((rows, width), BF16)] * 2 + [pltpu.VMEM((rows, hidden), BF16)] * 3
    shape = out((SHARDS, 3, width // SHARDS, hidden), F32)
    return call(far_grads_kernel, "far_grads", shape, scratch, came, w, partial)


def split(x):
    high = x.astype(BF16)
    return high, (x - high.astype(F32)).astype(BF16)


def packed(high, low):
    return jnp.concatenate([high, high, low], axis=1)


def mirrored(left, corner):
    at = left.shape[1]
    return jnp.concatenate([left, jnp.concatenate([left[at:].T, corner], axis=0)], axis=1)


def gram_of(xh, xl):
    a, b = packed(xh, xl), jnp.concatenate([xh, xl, xh], axis=1)
    return mirrored(mm_nt(a, b[:TILE]), mm_nt(a[TILE:], b[TILE:]))


def square_of(ah, al):
    a, b = packed(ah, al), jnp.concatenate([ah, al, ah], axis=0)
    return mirrored(mm(a, b[:, :TILE]), mm(a[TILE:], b[:, TILE:]))


def newton_kernel(at_ref, g_ref, wg_ref, wu_ref, wd_ref, v_ref, x_s, f_s, sems):
    copies = [
        pltpu.make_async_copy(ref.at[at_ref[0]], f_s.at[m], sems.at[m])
        for m, ref in enumerate((wg_ref, wu_ref, wd_ref))
    ]
    for copy in copies:
        copy.start()
    matrices, width, hidden = x_s.shape
    every = range(matrices)
    for m in every:
        grad = g_ref[:, m].reshape(width, hidden)
        total = jnp.sum(jnp.sum(grad * grad, axis=1, keepdims=True), axis=0, keepdims=True)
        x_s[m] = grad * lax.rsqrt(total + eps_value)

    def sweep(_, carry):
        xs = [x_s[m] for m in every]
        parts = [split(x) for x in xs]
        grams = [gram_of(*p) for p in parts]
        squares = [square_of(*split(g)) for g in grams]
        mixers = [split(ns_b * g + ns_c * q) for g, q in zip(grams, squares)]
        for m, x, (xh, xl), mixer in zip(every, xs, parts, mixers):
            x_s[m] = ns_a * x + mm(packed(*mixer), jnp.concatenate([xh, xl, xh], axis=0))
        return carry

    lax.fori_loop(0, NS_STEPS, sweep, 0)
    for m, copy in enumerate(copies):
        copy.wait()
        v_ref[m] = (f_s[m] - x_s[m]).astype(BF16)


def newton(at, grads, gate, up, down):
    shape = (grads.shape[1], grads.shape[0] * grads.shape[2], grads.shape[3])
    vmem, hbm = pl.BlockSpec(memory_space=pltpu.VMEM), pl.BlockSpec(memory_space=pltpu.HBM)
    return pl.pallas_call(
        newton_kernel,
        out_shape=out(shape, BF16),
        in_specs=[pl.BlockSpec(memory_space=pltpu.SMEM), vmem, hbm, hbm, hbm],
        out_specs=vmem,
        scratch_shapes=[pltpu.VMEM(shape, F32)] * 2 + [pltpu.SemaphoreType.DMA((3,))],
        compiler_params=pltpu.CompilerParams(vmem_limit_bytes=VMEM_LIMIT),
        name="newton",
    )(at, grads, gate, up, down)


def query_rows(q, v_ref):
    gate = mm(q, v_ref[0])
    hidden = (gate * jax.nn.sigmoid(gate) * mm(q, v_ref[1])).astype(BF16)
    return mm_nt(hidden, v_ref[2]).astype(BF16)


def far_query_kernel(came, v_ref, o_ref):
    width = came.shape[1] // 2
    for left in (0, width):
        columns = slice(left, left + width)
        o_ref[:, columns] = query_rows(came[:, columns].astype(BF16), v_ref).astype(F32)


def near_query_kernel(q_ref, v_ref, o_ref):
    half = q_ref.shape[0] // 2
    for top in (0, half):
        rows = slice(top, top + half)
        o_ref[rows, :] = query_rows(q_ref[rows, :], v_ref)


def join_kernel(at_ref, o_ref, came, y_ref, z_ref):
    rows, width = o_ref.shape
    block = rows // 8
    for h in range(2):

        @pl.when(at_ref[0] == h)
        def _():
            near, far = slice(h * width, (h + 1) * width), slice((1 - h) * width, (2 - h) * width)
            for dy in range(2):
                for dz in range(4):
                    r = dy * 4 + dz
                    to_y, to_z = pl.ds(Y_ORDER.index(dz) * block, block), pl.ds(dy * block, block)
                    mine = o_ref[r * block : (r + 1) * block, :]
                    other = came[side_by_side(rows, r, block, width)].astype(BF16)
                    for columns, piece in ((near, mine), (far, other)):
                        y_ref[dy, to_y, columns] = piece
                        z_ref[dz, to_z, columns] = piece


def join(at, mine, came):
    rows, width = mine.shape
    shapes = [out((n, rows // n, 2 * width), BF16) for n in (2, 4)]
    return call(join_kernel, "join", shapes, [], at, mine, came)


def swap(a, axis):
    return lax.ppermute(a, axis, [(0, 1), (1, 0)])


def ring(a, shift):
    return lax.ppermute(a, "z", [(i, (i + shift) % 4) for i in range(4)])


def sum_kernel(a_ref, o_ref):
    total = a_ref[0]
    for j in range(1, SHARDS):
        total = total + a_ref[j]
    for j in range(SHARDS):
        o_ref[j] = total


def plane_sum(a):
    came = lax.all_to_all(a, PLANE, 0, 0, tiled=True)
    same = call(sum_kernel, "sum_parts", out(a.shape, a.dtype), [], came)
    return lax.all_to_all(same, PLANE, 0, 0, tiled=True)


def together(*arrays):
    return lax.optimization_barrier(arrays)


def halves(a):
    half = a.shape[0] // 2
    return a[:half], a[half:]


def both_ways(up, down):
    return ring(up, 1), ring(down, -1)


def project_scatter(by_y, by_z, weight):
    wb, wa = weight[:, :CUT], weight[:, CUT:]
    block = by_z.shape[1] // 2
    far_two, by_y, by_z = together(mm(by_y[1, :block], wb), by_y, by_z)
    b_two = swap(far_two, "yl")
    up, down = both_ways(*halves(mm(by_z[2], wa)))
    far_rest, b_two, by_y, by_z = together(mm(by_y[1, block:], wb), b_two, by_y, by_z)
    b_rest = swap(far_rest, "yl")
    b_two = b_two + mm(by_y[0, :block], wb)
    b_up, b_down = both_ways(*halves(b_two))
    one, three = mm(by_z[1], wa), mm(by_z[3], wa)
    one = jnp.concatenate([one[:block] + up, one[block:]], axis=0)
    three = jnp.concatenate([three[:block], three[block:] + down], axis=0)
    a_came = both_ways(one[:, :MIDDLE], three[:, :MIDDLE])
    later, b_up, b_down = together((one[:, MIDDLE:], three[:, MIDDLE:]), b_up, b_down)
    a_more = both_ways(*later)
    a = mm(by_z[0], wa[:, :MIDDLE]) + sum(a_came)
    b_rest = b_rest + mm(by_y[0, block:], wb)
    half = block // 2
    b_one, b_three = b_rest[block : 2 * block], b_rest[2 * block :]
    b_one = jnp.concatenate([b_one[:half] + b_up, b_one[half:]], axis=0)
    b_three = jnp.concatenate([b_three[:half], b_three[half:] + b_down], axis=0)
    a, b_one, b_three, by_z = together(a, b_one, b_three, by_z)
    a_came = swap(a[block:], "yl")
    b_came = both_ways(b_one, b_three)
    more = mm(by_z[0], wa[:, MIDDLE:]) + sum(a_more)
    more_came = swap(more[block:], "yl")
    return jnp.concatenate(
        [b_rest[:block] + sum(b_came), a[:block] + a_came, more[:block] + more_came], axis=1
    )


def body(keys, queries, values, rates, gate, up, down, out_weight):
    at = jnp.stack([lax.axis_index(name).astype(jnp.int32) for name in ("core", "yl", "z")])
    weights = tuple(in_hbm(w) for w in (gate, up, down))
    k, d, sent = sort_tokens(at, keys, values, rates.T)
    came = swap(sent, "core")
    partial, rounded = near_grads(at, k, d, *weights)
    queries, partial = together(queries, partial)
    q, q_sent = sort_queries(at, queries)
    summed = far_grads(came, rounded, partial)
    q_sent, summed = together(q_sent, summed)
    whole, q_sent = together(plane_sum(summed), q_sent)
    q_came = swap(q_sent, "core")
    v = newton(at, whole, *weights)
    o_came = swap(call(far_query_kernel, "far_query", out(q_sent.shape, F32), [], q_came, v), "core")
    o = call(near_query_kernel, "near_query", out(q.shape, BF16), [], q, v)
    by_y, by_z = join(at, o, o_came)
    return project_scatter(by_y, by_z, out_weight).astype(BF16)


def solution(mesh):
    fine = Mesh(mesh.devices.reshape(2, 4, 4, 2, 2), AXES)
    ctx, head = ("x", "yh", "core"), ("yl", "z")
    in_specs = (
        P(ctx, head),
        P(ctx, head),
        P(ctx, head),
        P(ctx, head),
        P(head, None, None),
        P(head, None, None),
        P(head, None, None),
        P(head, None),
    )
    out_specs = P(ctx + head, None)
    return jax.shard_map(body, mesh=fine, in_specs=in_specs, out_specs=out_specs, check_vma=False)
```

```python
import jax
import jax.numpy as jnp
from jax import lax
from jax.experimental import pallas as pl
from jax.experimental.pallas import tpu as pltpu
from jax.sharding import Mesh, PartitionSpec as P

NS_STEPS = 5
ns_a = 3.4445
ns_b = -4.775
ns_c = 2.0315
eps_value = 1e-06

AXES = ("yl", "z", "x", "yh", "core")
PLANE = ("x", "yh")
SHARDS = 8
TILE = 256
VMEM_LIMIT = 24 << 20
CUT = 2304
MIDDLE = 1408
Y_ORDER = (2, 0, 1, 3)
F32 = jnp.float32
BF16 = jnp.bfloat16


def mm(a, b):
    return jnp.dot(a, b, preferred_element_type=F32)


def mm_nt(a, b):
    return lax.dot_general(a, b, (((1,), (1,)), ((), ())), preferred_element_type=F32)


def call(kernel, name, outs, scratch, *operands):
    specs = [pl.BlockSpec(memory_space=pltpu.SMEM if a.dtype == jnp.int32 else pltpu.VMEM) for a in operands]
    return pl.pallas_call(
        kernel,
        out_shape=outs,
        in_specs=specs,
        out_specs=jax.tree.map(lambda _: pl.BlockSpec(memory_space=pltpu.VMEM), outs),
        scratch_shapes=scratch,
        compiler_params=pltpu.CompilerParams(vmem_limit_bytes=VMEM_LIMIT),
        name=name,
    )(*operands)


def in_hbm(a):
    return pltpu.with_memory_space_constraint(a, pltpu.HBM)


def out(shape, dtype):
    return jax.ShapeDtypeStruct(shape, dtype)


def sort_tokens_kernel(at_ref, r_ref, k_ref, v_ref, k_o, d_o, sent, k_s, v_s, sems):
    rows, width = k_o.shape
    half = rows // 2
    copies = [
        pltpu.make_async_copy(ref.at[pl.ds(i * half, half)], to.at[pl.ds(i * half, half)], sems.at[2 * n + i])
        for n, (ref, to) in enumerate(((k_ref, k_s), (v_ref, v_s)))
        for i in range(2)
    ]
    for copy in copies:
        copy.start()
    for copy in copies:
        copy.wait()
    for h in range(2):

        @pl.when(at_ref[0] == h)
        def _():
            near, far = slice(h * width, (h + 1) * width), slice((1 - h) * width, (2 - h) * width)
            k_o[...] = k_s[:, near]
            sent[:, :width] = k_s[:, far].astype(F32)
            for head, columns in ((h, near), (1 - h, far)):
                rate = r_ref[head : head + 1, :].T
                d = (-rate * v_s[:, columns].astype(F32)).astype(BF16)
                if head == h:
                    d_o[...] = d
                else:
                    sent[:, width:] = d.astype(F32)


def sort_tokens(at, keys, values, rates):
    shape = (keys.shape[0], keys.shape[1] // 2)
    vmem, hbm = pl.BlockSpec(memory_space=pltpu.VMEM), pl.BlockSpec(memory_space=pltpu.HBM)
    return pl.pallas_call(
        sort_tokens_kernel,
        out_shape=[out(shape, BF16), out(shape, BF16), out(keys.shape, F32)],
        in_specs=[pl.BlockSpec(memory_space=pltpu.SMEM), vmem, hbm, hbm],
        out_specs=[vmem] * 3,
        scratch_shapes=[pltpu.VMEM(keys.shape, BF16)] * 2 + [pltpu.SemaphoreType.DMA((4,))],
        compiler_params=pltpu.CompilerParams(vmem_limit_bytes=VMEM_LIMIT),
        name="sort_tokens",
    )(at, rates, in_hbm(keys), in_hbm(values))


def side_by_side(rows, r, block, width):
    top = (r * block) % (rows // 2)
    left = width * ((r * block) // (rows // 2))
    return slice(top, top + block), slice(left, left + width)


def sort_queries_kernel(at_ref, q_ref, q_o, sent):
    rows, width = q_o.shape
    block = rows // 8
    for h in range(2):

        @pl.when(at_ref[0] == h)
        def _():
            near, far = slice(h * width, (h + 1) * width), slice((1 - h) * width, (2 - h) * width)
            for r in range(8):
                row = ((at_ref[1] + r // 4) % 2) * 4 + (at_ref[2] + r % 4) % 4
                source = pl.ds(pl.multiple_of(row * block, block), block)
                q_o[r * block : (r + 1) * block, :] = q_ref[source, near]
                to_rows, to_columns = side_by_side(rows, r, block, width)
                sent[to_rows, to_columns] = q_ref[source, far].astype(F32)


def sort_queries(at, queries):
    rows, columns = queries.shape
    shapes = [out((rows, columns // 2), BF16), out((rows // 2, columns), F32)]
    return call(sort_queries_kernel, "sort_queries", shapes, [], at, queries)


def grads_of(k_ref, d_ref, w_ref, hk_s, dg_s, du_s, ready=lambda m: None):
    rows, step = k_ref.shape[0], 256
    chunks = [slice(t, t + step) for t in range(0, rows, step)]
    ready(0)
    gates = [mm(k_ref[at, :], w_ref[0]) for at in chunks]
    ready(1)
    uppers = [mm(k_ref[at, :], w_ref[1]) for at in chunks]
    ready(2)
    for at, gate, upper in zip(chunks, gates, uppers):
        dhid = mm(d_ref[at, :], w_ref[2])
        sig = jax.nn.sigmoid(gate)
        act = gate * sig
        hk_s[at, :] = (act * upper).astype(BF16)
        dg_s[at, :] = (dhid * upper * sig * (1.0 + gate * (1.0 - sig))).astype(BF16)
        du_s[at, :] = (dhid * act).astype(BF16)
    kt = k_ref[...].T
    dt = d_ref[...].T
    for m, (left, right) in enumerate(((kt, dg_s), (kt, du_s), (dt, hk_s))):
        yield m, mm(left, right[...])


def near_grads_kernel(at_ref, k_ref, d_ref, g_ref, u_ref, w_ref, o_ref, b_ref, f_s, hk_s, dg_s, du_s, sems):
    copies = [
        pltpu.make_async_copy(ref.at[at_ref[0]], f_s.at[m], sems.at[m]) for m, ref in enumerate((g_ref, u_ref, w_ref))
    ]
    for copy in copies:
        copy.start()

    def ready(m):
        copies[m].wait()
        b_ref[m] = f_s[m].astype(BF16)

    for m, grad in grads_of(k_ref, d_ref, b_ref, hk_s, dg_s, du_s, ready):
        o_ref[m] = grad


def far_grads_kernel(came, b_ref, p_ref, o_ref, k_s, d_s, hk_s, dg_s, du_s):
    part = o_ref.shape[2]
    width = k_s.shape[1]
    k_s[...] = came[:, :width].astype(BF16)
    d_s[...] = came[:, width:].astype(BF16)
    for m, grad in grads_of(k_s, d_s, b_ref, hk_s, dg_s, du_s):
        for j in range(SHARDS):
            rows = slice(j * part, (j + 1) * part)
            o_ref[j, m] = grad[rows, :] + p_ref[m, rows, :]


def near_grads(at, k, d, gate, up, down):
    heads, width, hidden = gate.shape
    vmem, hbm = pl.BlockSpec(memory_space=pltpu.VMEM), pl.BlockSpec(memory_space=pltpu.HBM)
    shape = (3, width, hidden)
    return pl.pallas_call(
        near_grads_kernel,
        out_shape=[out(shape, F32), out(shape, BF16)],
        in_specs=[pl.BlockSpec(memory_space=pltpu.SMEM), vmem, vmem, hbm, hbm, hbm],
        out_specs=[vmem, vmem],
        scratch_shapes=[pltpu.VMEM(shape, F32)]
        + [pltpu.VMEM((k.shape[0], hidden), BF16)] * 3
        + [pltpu.SemaphoreType.DMA((3,))],
        compiler_params=pltpu.CompilerParams(vmem_limit_bytes=VMEM_LIMIT),
        name="near_grads",
    )(at, k, d, gate, up, down)


def far_grads(came, w, partial):
    heads, width, hidden = partial.shape
    rows = came.shape[0]
    scratch = [pltpu.VMEM((rows, width), BF16)] * 2 + [pltpu.VMEM((rows, hidden), BF16)] * 3
    shape = out((SHARDS, 3, width // SHARDS, hidden), F32)
    return call(far_grads_kernel, "far_grads", shape, scratch, came, w, partial)


def split(x):
    high = x.astype(BF16)
    return high, (x - high.astype(F32)).astype(BF16)


def packed(high, low):
    return jnp.concatenate([high, high, low], axis=1)


def mirrored(left, corner):
    at = left.shape[1]
    return jnp.concatenate([left, jnp.concatenate([left[at:].T, corner], axis=0)], axis=1)


def gram_of(xh, xl):
    a, b = packed(xh, xl), jnp.concatenate([xh, xl, xh], axis=1)
    return mirrored(mm_nt(a, b[:TILE]), mm_nt(a[TILE:], b[TILE:]))


def square_of(ah, al):
    a, b = packed(ah, al), jnp.concatenate([ah, al, ah], axis=0)
    return mirrored(mm(a, b[:, :TILE]), mm(a[TILE:], b[:, TILE:]))


def newton_kernel(at_ref, g_ref, wg_ref, wu_ref, wd_ref, v_ref, x_s, f_s, sems):
    copies = [
        pltpu.make_async_copy(ref.at[at_ref[0]], f_s.at[m], sems.at[m])
        for m, ref in enumerate((wg_ref, wu_ref, wd_ref))
    ]
    for copy in copies:
        copy.start()
    matrices, width, hidden = x_s.shape
    every = range(matrices)
    for m in every:
        grad = g_ref[:, m].reshape(width, hidden)
        total = jnp.sum(jnp.sum(grad * grad, axis=1, keepdims=True), axis=0, keepdims=True)
        x_s[m] = grad * lax.rsqrt(total + eps_value)

    def sweep(_, carry):
        xs = [x_s[m] for m in every]
        parts = [split(x) for x in xs]
        grams = [gram_of(*p) for p in parts]
        squares = [square_of(*split(g)) for g in grams]
        mixers = [split(ns_b * g + ns_c * q) for g, q in zip(grams, squares)]
        for m, x, (xh, xl), mixer in zip(every, xs, parts, mixers):
            x_s[m] = ns_a * x + mm(packed(*mixer), jnp.concatenate([xh, xl, xh], axis=0))
        return carry

    lax.fori_loop(0, NS_STEPS, sweep, 0)
    for m, copy in enumerate(copies):
        copy.wait()
        v_ref[m] = (f_s[m] - x_s[m]).astype(BF16)


def newton(at, grads, gate, up, down):
    shape = (grads.shape[1], grads.shape[0] * grads.shape[2], grads.shape[3])
    vmem, hbm = pl.BlockSpec(memory_space=pltpu.VMEM), pl.BlockSpec(memory_space=pltpu.HBM)
    return pl.pallas_call(
        newton_kernel,
        out_shape=out(shape, BF16),
        in_specs=[pl.BlockSpec(memory_space=pltpu.SMEM), vmem, hbm, hbm, hbm],
        out_specs=vmem,
        scratch_shapes=[pltpu.VMEM(shape, F32)] * 2 + [pltpu.SemaphoreType.DMA((3,))],
        compiler_params=pltpu.CompilerParams(vmem_limit_bytes=VMEM_LIMIT),
        name="newton",
    )(at, grads, gate, up, down)


def query_rows(q, v_ref):
    gate = mm(q, v_ref[0])
    hidden = (gate * jax.nn.sigmoid(gate) * mm(q, v_ref[1])).astype(BF16)
    return mm_nt(hidden, v_ref[2]).astype(BF16)


def far_query_kernel(came, v_ref, o_ref):
    width = came.shape[1] // 2
    for left in (0, width):
        columns = slice(left, left + width)
        o_ref[:, columns] = query_rows(came[:, columns].astype(BF16), v_ref).astype(F32)


def near_query_kernel(q_ref, v_ref, o_ref):
    half = q_ref.shape[0] // 2
    for top in (0, half):
        rows = slice(top, top + half)
        o_ref[rows, :] = query_rows(q_ref[rows, :], v_ref)


def join_kernel(at_ref, o_ref, came, y_ref, z_ref):
    rows, width = o_ref.shape
    block = rows // 8
    for h in range(2):

        @pl.when(at_ref[0] == h)
        def _():
            near, far = slice(h * width, (h + 1) * width), slice((1 - h) * width, (2 - h) * width)
            for dy in range(2):
                for dz in range(4):
                    r = dy * 4 + dz
                    to_y, to_z = pl.ds(Y_ORDER.index(dz) * block, block), pl.ds(dy * block, block)
                    mine = o_ref[r * block : (r + 1) * block, :]
                    other = came[side_by_side(rows, r, block, width)].astype(BF16)
                    for columns, piece in ((near, mine), (far, other)):
                        y_ref[dy, to_y, columns] = piece
                        z_ref[dz, to_z, columns] = piece


def join(at, mine, came):
    rows, width = mine.shape
    shapes = [out((n, rows // n, 2 * width), BF16) for n in (2, 4)]
    return call(join_kernel, "join", shapes, [], at, mine, came)


def swap(a, axis):
    return lax.ppermute(a, axis, [(0, 1), (1, 0)])


def ring(a, shift):
    return lax.ppermute(a, "z", [(i, (i + shift) % 4) for i in range(4)])


def sum_kernel(a_ref, o_ref):
    total = a_ref[0]
    for j in range(1, SHARDS):
        total = total + a_ref[j]
    for j in range(SHARDS):
        o_ref[j] = total


def plane_sum(a):
    came = lax.all_to_all(a, PLANE, 0, 0, tiled=True)
    same = call(sum_kernel, "sum_parts", out(a.shape, a.dtype), [], came)
    return lax.all_to_all(same, PLANE, 0, 0, tiled=True)


def together(*arrays):
    return lax.optimization_barrier(arrays)


def halves(a):
    half = a.shape[0] // 2
    return a[:half], a[half:]


def both_ways(up, down):
    return ring(up, 1), ring(down, -1)


def project_scatter(by_y, by_z, weight):
    wb, wa = weight[:, :CUT], weight[:, CUT:]
    block = by_z.shape[1] // 2
    far_two, by_y, by_z = together(mm(by_y[1, :block], wb), by_y, by_z)
    b_two = swap(far_two, "yl")
    up, down = both_ways(*halves(mm(by_z[2], wa)))
    far_rest, b_two, by_y, by_z = together(mm(by_y[1, block:], wb), b_two, by_y, by_z)
    b_rest = swap(far_rest, "yl")
    b_two = b_two + mm(by_y[0, :block], wb)
    b_up, b_down = both_ways(*halves(b_two))
    one, three = mm(by_z[1], wa), mm(by_z[3], wa)
    one = jnp.concatenate([one[:block] + up, one[block:]], axis=0)
    three = jnp.concatenate([three[:block], three[block:] + down], axis=0)
    a_came = both_ways(one[:, :MIDDLE], three[:, :MIDDLE])
    later, b_up, b_down = together((one[:, MIDDLE:], three[:, MIDDLE:]), b_up, b_down)
    a_more = both_ways(*later)
    a = mm(by_z[0], wa[:, :MIDDLE]) + sum(a_came)
    b_rest = b_rest + mm(by_y[0, block:], wb)
    half = block // 2
    b_one, b_three = b_rest[block : 2 * block], b_rest[2 * block :]
    b_one = jnp.concatenate([b_one[:half] + b_up, b_one[half:]], axis=0)
    b_three = jnp.concatenate([b_three[:half], b_three[half:] + b_down], axis=0)
    a, b_one, b_three, by_z = together(a, b_one, b_three, by_z)
    a_came = swap(a[block:], "yl")
    b_came = both_ways(b_one, b_three)
    more = mm(by_z[0], wa[:, MIDDLE:]) + sum(a_more)
    more_came = swap(more[block:], "yl")
    return jnp.concatenate(
        [b_rest[:block] + sum(b_came), a[:block] + a_came, more[:block] + more_came], axis=1
    )


def body(keys, queries, values, rates, gate, up, down, out_weight):
    at = jnp.stack([lax.axis_index(name).astype(jnp.int32) for name in ("core", "yl", "z")])
    weights = tuple(in_hbm(w) for w in (gate, up, down))
    k, d, sent = sort_tokens(at, keys, values, rates.T)
    came = swap(sent, "core")
    partial, rounded = near_grads(at, k, d, *weights)
    queries, partial = together(queries, partial)
    q, q_sent = sort_queries(at, queries)
    summed = far_grads(came, rounded, partial)
    q_sent, summed = together(q_sent, summed)
    whole, q_sent = together(plane_sum(summed), q_sent)
    q_came = swap(q_sent, "core")
    v = newton(at, whole, *weights)
    o_came = swap(call(far_query_kernel, "far_query", out(q_sent.shape, F32), [], q_came, v), "core")
    o = call(near_query_kernel, "near_query", out(q.shape, BF16), [], q, v)
    by_y, by_z = join(at, o, o_came)
    return project_scatter(by_y, by_z, out_weight).astype(BF16)


def solution(mesh):
    fine = Mesh(mesh.devices.reshape(2, 4, 4, 2, 2), AXES)
    ctx, head = ("x", "yh", "core"), ("yl", "z")
    in_specs = (
        P(ctx, head),
        P(ctx, head),
        P(ctx, head),
        P(ctx, head),
        P(head, None, None),
        P(head, None, None),
        P(head, None, None),
        P(head, None),
    )
    out_specs = P(ctx + head, None)
    return jax.shard_map(body, mesh=fine, in_specs=in_specs, out_specs=out_specs, check_vma=False)
```
